32 devices in a mesh: seq: 8 (over y, x, core), head: 4 (over z).
Axes of the slice: x: 2, y: 2, z: 4, core: 2. Of those that a mesh axis runs over, the one named last changes fastest.
Arguments:
- inputs: bfloat16 [8, 1024, 512], P(None, ('seq', 'head')), may hold values from -8 to 8
- gain_first: float32 [512], replicated, may hold values from 0.25 to 1.75
- shift_first: float32 [512], replicated, may hold values from -3 to 3
- query_weight: bfloat16 [512, 512], replicated, may hold values from -0.25 to 0.25
- key_weight: bfloat16 [512, 512], replicated, may hold values from -0.25 to 0.25
- value_weight: bfloat16 [512, 512], replicated, may hold values from -0.25 to 0.25
- out_weight: bfloat16 [512, 512], replicated, may hold values from -1 to 1
- gain_second: float32 [512], replicated, may hold values from 0.25 to 1.75
- shift_second: float32 [512], replicated, may hold values from -3 to 3
- up_weight: bfloat16 [512, 2048], replicated, may hold values from -0.25 to 0.25
- up_bias: float32 [2048], replicated, may hold values from -3 to 3
- down_weight: bfloat16 [2048, 512], replicated, may hold values from -0.125 to 0.125
- down_bias: float32 [512], replicated, may hold values from -3 to 3
- cotangent: bfloat16 [8, 1024, 512], P(None, ('seq', 'head')), may hold values from -6 to 6
Outputs:
- layer_out: bfloat16 [8, 1024, 512], P(None, ('seq', 'head'))
- input_grad: bfloat16 [8, 1024, 512], P(None, ('seq', 'head'))
- gain_first_grad: float32 [512], P('seq')
- shift_first_grad: float32 [512], P('seq')
- query_grad: float32 [512, 512], P('seq', 'head')
- key_grad: float32 [512, 512], P('seq', 'head')
- value_grad: float32 [512, 512], P('seq', 'head')
- out_weight_grad: float32 [512, 512], P('seq', 'head')
- gain_second_grad: float32 [512], P('seq')
- shift_second_grad: float32 [512], P('seq')
- up_grad: float32 [512, 2048], P('seq', 'head')
- up_bias_grad: float32 [2048], P('seq')
- down_grad: float32 [2048, 512], P('seq', 'head')
- down_bias_grad: float32 [512], P('seq')
The draws below stay inside these ranges and needn't reach their ends.
All inputs are finite; a program needn't handle non-finite values.
Results may differ from the reference program's by a relative error of at most 0.009.
Values may be sent and summed in bfloat16 or wider, within the bound.
A program may use at most 192 MiB of HBM per device.

```python
from functools import reduce
import jax
import jax.numpy as jnp
from jax import lax

D = 512
H = 8
DH = 64
FF = 2048
BLOCK = 16
ROWS = 8
LEN = 1024


def draw_inputs(key, part):
    levels = (LEN // BLOCK).bit_length() - 1
    subkeys = jax.random.split(key, levels + 2)
    background = jax.random.normal(subkeys[0], (ROWS, LEN, D), jnp.float32)
    strength = 0.6
    combined = background
    for level_id in range(levels):
        span_rows = BLOCK * 2 ** level_id
        pieces = jax.random.normal(subkeys[level_id + 1], (ROWS, LEN // span_rows, D), jnp.float32)
        combined = combined + strength * jnp.repeat(pieces, span_rows, axis=1, total_repeat_length=LEN)
    return jnp.clip(combined, -8.0, 8.0).astype(jnp.bfloat16)


def level_of(own_key, shape, cuts, least, largest):
    def one(dim, shards_of):
        draws = jax.random.uniform(jax.random.fold_in(jax.random.fold_in(own_key, 6), dim), (shards_of,), jnp.float32, least / len(cuts), largest / len(cuts))
        return jnp.repeat(jnp.exp(draws), shape[dim] // shards_of).reshape((-1,) + (1,) * (len(shape) - dim - 1))

    loudness = one(*cuts[0])
    for cut in cuts[1:]:
        loudness = loudness * one(*cut)
    return loudness


def bell_draw(rng, shape, scale, most, cuts=(), kind=jnp.bfloat16):
    entries = jax.random.normal(rng, shape, jnp.float32) * scale
    if len(cuts) > 0:
        entries = level_of(rng, shape, cuts, -0.22, 0.18) * entries
    return jnp.clip(entries, min=-most, max=most).astype(kind)


def setup_inputs(seed: int = 0) -> dict:
    streams_of = jax.random.split(jax.random.key(seed), 15)
    return {
        "inputs": draw_inputs(jax.random.fold_in(streams_of[14], 71), 0),
        "gain_first": jnp.clip(1.0 + 0.15 * jax.random.normal(streams_of[1], (D,), jnp.float32), 0.25, 1.75),
        "shift_first": bell_draw(streams_of[2], (D,), 0.3, 3.0, (), jnp.float32),
        "query_weight": bell_draw(streams_of[3], (D, D), D ** -0.5, 0.25),
        "key_weight": bell_draw(streams_of[4], (D, D), D ** -0.5, 0.25),
        "value_weight": bell_draw(streams_of[5], (D, D), D ** -0.5, 0.25),
        "out_weight": bell_draw(streams_of[6], (D, D), (D // 16) ** -0.5, 1.0),
        "gain_second": jnp.clip(1.0 + 0.15 * jax.random.normal(streams_of[7], (D,), jnp.float32), 0.25, 1.75),
        "shift_second": bell_draw(streams_of[8], (D,), 0.3, 3.0, (), jnp.float32),
        "up_weight": bell_draw(streams_of[9], (D, FF), D ** -0.5, 0.25),
        "up_bias": bell_draw(streams_of[10], (FF,), 0.5, 3.0, (), jnp.float32),
        "down_weight": bell_draw(streams_of[11], (FF, D), FF ** -0.5, 0.125),
        "down_bias": bell_draw(streams_of[12], (D,), 0.3, 3.0, (), jnp.float32),
        "cotangent": bell_draw(streams_of[13], (ROWS, LEN, D), 1.0, 6.0, ((1, 32),)),
    }


EPSILON = 1e-05
HIGHEST = lax.Precision.HIGHEST

@jax.custom_vjp
def low(v):
    return lax.optimization_barrier(v.astype(jnp.bfloat16)).astype(jnp.float32)

@jax.custom_vjp
def low_back(v):
    return v

def low_keep(v):
    return (low(v), None)

def low_pass(kept, grad):
    return (grad,)

def back_keep(v):
    return (v, None)

def back_low(kept, grad):
    return (low(grad),)
low.defvjp(low_keep, low_pass)
low_back.defvjp(back_keep, back_low)

def norm_rows(values, gain, shift):
    center = values - lax.optimization_barrier(jnp.mean(values, axis=-1, keepdims=True))
    spread = lax.optimization_barrier(jnp.mean(center * center, axis=-1, keepdims=True))
    return center * lax.rsqrt(spread + EPSILON) * gain + shift

def exact_dot(left, right):
    return jnp.dot(left, right, precision=HIGHEST, preferred_element_type=jnp.float32)

def halve_rows(table):
    paired = table.reshape((table.shape[0] // 2, 2) + table.shape[1:])
    return lax.optimization_barrier(jnp.sum(paired, axis=1)) * 0.5

def flip_blocks(table):
    total_rows = table.shape[0]
    return table.reshape((total_rows // (2 * BLOCK), 2, BLOCK) + table.shape[1:])[:, ::-1].reshape(table.shape)

def block_scores(queries, keyset):
    groups = keyset.shape[0] // BLOCK
    total_rows = queries.shape[0]
    left_view = queries.reshape(groups, total_rows // groups, H, DH)
    right_view = keyset.reshape(groups, BLOCK, H, DH)
    return jnp.einsum('bmhd,bkhd->bmhk', left_view, right_view, precision=HIGHEST).reshape(total_rows, H, BLOCK)

def block_values(weights, valueset):
    groups = valueset.shape[0] // BLOCK
    total_rows = weights.shape[0]
    left_view = weights.reshape(groups, total_rows // groups, H, BLOCK)
    right_view = valueset.reshape(groups, BLOCK, H, DH)
    return jnp.einsum('bmhk,bkhd->bmhd', left_view, right_view, precision=HIGHEST).reshape(total_rows, H, DH)

def hier_attention(queries, keyrows, valrows):
    levels = (queries.shape[0] // BLOCK).bit_length() - 1
    key_sets = [keyrows]
    value_sets = [valrows]
    coarse_key, coarse_value = (keyrows, valrows)
    for level_id in range(levels):
        key_sets.append(flip_blocks(coarse_key))
        value_sets.append(flip_blocks(coarse_value))
        if level_id + 1 < levels:
            coarse_key = low(halve_rows(coarse_key))
            coarse_value = low(halve_rows(coarse_value))
    score_scale = DH ** (-0.5)
    scores = jnp.concatenate([block_scores(queries, keyset) for keyset in key_sets], axis=-1) * score_scale
    scores = low_back(scores)
    weights = low(jax.nn.softmax(scores, axis=-1))
    partials = [block_values(weights[:, :, BLOCK * position:BLOCK * (position + 1)], valueset) for position, valueset in enumerate(value_sets)]
    return reduce(jnp.add, partials)

def layer(sequence_rows, params):
    gain_first, shift_first, query_weight, key_weight, value_weight, out_weight, gain_second, shift_second, up_weight, up_bias, down_weight, down_bias = params
    normed = low(norm_rows(sequence_rows, gain_first, shift_first))
    queries = low(low_back(exact_dot(normed, query_weight))).reshape(-1, H, DH)
    keyrows = low(low_back(exact_dot(normed, key_weight))).reshape(-1, H, DH)
    valrows = low(low_back(exact_dot(normed, value_weight))).reshape(-1, H, DH)
    mixed = low(low_back(hier_attention(queries, keyrows, valrows))).reshape(-1, H * DH)
    residual = sequence_rows + low_back(exact_dot(mixed, out_weight))
    normed_two = low(norm_rows(residual, gain_second, shift_second))
    hidden = low_back(exact_dot(normed_two, up_weight) + up_bias)
    active = low(jax.nn.gelu(hidden, approximate=False))
    return residual + exact_dot(active, down_weight) + down_bias

def reference(inputs, gain_first, shift_first, query_weight, key_weight, value_weight, out_weight, gain_second, shift_second, up_weight, up_bias, down_weight, down_bias, cotangent):
    params = tuple((array_in.astype(jnp.float32) for array_in in (gain_first, shift_first, query_weight, key_weight, value_weight, out_weight, gain_second, shift_second, up_weight, up_bias, down_weight, down_bias)))

    def one_row(carry, pair_rows):
        sequence, grad_out = pair_rows
        result, backward = jax.vjp(layer, sequence, params)
        grad_in, grad_params = backward(grad_out)
        carry = jax.tree.map(jnp.add, carry, grad_params)
        return (carry, (result.astype(jnp.bfloat16), grad_in.astype(jnp.bfloat16)))
    zero_grads = jax.tree.map(jnp.zeros_like, params)
    totals, (layer_out, input_grad) = lax.scan(one_row, zero_grads, (inputs.astype(jnp.float32), cotangent.astype(jnp.float32)))
    return (layer_out, input_grad, totals[0], totals[1], totals[2], totals[3], totals[4], totals[5], totals[6], totals[7], totals[8], totals[9], totals[10], totals[11])
```

```python
import functools

import jax
import jax.numpy as jnp
from jax import lax
from jax.experimental import pallas as pl
from jax.experimental.pallas import tpu as pltpu
from jax.sharding import PartitionSpec as P

MESH = pl.DeviceIdType.MESH
BF = jnp.bfloat16
F32 = jnp.float32
DH = 64
BLOCK = 16
EPSILON = 1e-05
PAIR = 2 * DH
VEC_ROWS = 16


def idiv(value, k):
    return lax.div(value, jnp.int32(k))


def irem(value, k):
    return lax.rem(value, jnp.int32(k))


def bit_of(value, b):
    return irem(idiv(value, 1 << b), 2)


def flip(value, k):
    b = 0
    while k >> b:
        if (k >> b) & 1:
            value = value + (1 - 2 * bit_of(value, b)) * (1 << b)
        b += 1
    return value


def dot(a, b):
    return jnp.dot(a, b, preferred_element_type=F32)


def dot_t(a, b):
    return lax.dot_general(a, b, (((1,), (1,)), ((), ())), preferred_element_type=F32)


def t_dot(a, b):
    return lax.dot_general(a, b, (((0,), (0,)), ((), ())), preferred_element_type=F32)


def two_part_dot(a, b):
    high = b.astype(BF)
    low = (b - high.astype(F32)).astype(BF)
    return dot(a, high) + dot(a, low)


def pair_mean(rows):
    i = lax.broadcasted_iota(jnp.int32, (rows // 2, rows), 0)
    j = lax.broadcasted_iota(jnp.int32, (rows // 2, rows), 1)
    return jnp.where((j >> 1) == i, 0.5, 0.0).astype(BF)


class Plan:
    def __init__(self, seq, head, rows, pos, width, hidden):
        self.seq, self.head, self.rows, self.pos, self.width, self.hidden = seq, head, rows, pos, width, hidden
        self.minor = rows // head
        self.groups = seq // self.minor
        self.tokens = rows * pos
        self.pairs = width // PAIR
        self.local = (self.tokens // BLOCK).bit_length() - 1
        self.remote = self.groups.bit_length() - 1
        self.bits = seq.bit_length() - 1
        self.far = self.tokens * 2 - 2 * BLOCK
        keys = self.far + BLOCK * max(self.remote, 2)
        self.keys = -(-keys // 128) * 128
        self.blocks = {
            "down": (hidden // seq, width // head),
            "up": (width // seq, hidden // head),
            "out": (width // seq, width // head),
            "query": (width // seq, width // head),
            "key": (width // seq, width // head),
            "value": (width // seq, width // head),
        }
        straight = list(range(self.bits))
        turned = straight[:1] + straight[:0:-1]
        self.order = {
            "down": straight,
            "up": turned,
            "out": straight,
            "query": turned,
            "key": straight,
            "value": turned,
        }


class Summed:
    def __init__(self, plan, me, name, number, grad, got, got_head, send, recv, out):
        self.plan, self.name, self.number = plan, name, number
        self.s, self.h = me
        self.grad, self.got, self.got_head, self.out = grad, got, got_head, out
        self.send, self.recv = send, recv
        self.order = plan.order[name]
        self.started = []

    def index(self, fixed, other=None):
        at = []
        for b in reversed(range(self.plan.bits)):
            if b == other:
                at.append(1 - bit_of(self.s, b))
            elif b in fixed:
                at.append(bit_of(self.s, b))
            else:
                at.append(slice(None))
        return tuple(at)

    def put(self, s, h, value):
        at = tuple((s >> b) & 1 for b in reversed(range(self.plan.bits)))
        self.grad[at + (h,)] = value.astype(BF)

    def start(self, stage):
        b = self.order[stage]
        copy = pltpu.make_async_remote_copy(
            src_ref=self.grad.at[self.index(self.order[:stage], b)],
            dst_ref=self.got[stage],
            send_sem=self.send.at[self.number, stage],
            recv_sem=self.recv.at[self.number, stage],
            device_id=(flip(self.s, 1 << b), self.h),
            device_id_type=MESH,
        )
        copy.start()
        self.started.append(copy)

    def finish(self, stage):
        self.started[stage].wait_recv()
        at = self.index(self.order[: stage + 1])
        free = [n for n, a in zip(self.grad.shape, at) if isinstance(a, slice)] + [self.plan.head]
        combos = [()]
        for n in free:
            combos = [c + (i,) for c in combos for i in range(n)]
        for combo in combos:
            left = list(combo)
            full = tuple(left.pop(0) if isinstance(a, slice) else a for a in at) + (left.pop(0),)
            self.grad[full] = self.grad[full] + self.got[stage][combo]

    def start_head(self):
        at = self.index(self.order)
        for k in range(1, self.plan.head):
            peer = flip(self.h, k)
            copy = pltpu.make_async_remote_copy(
                src_ref=self.grad.at[at + (peer,)],
                dst_ref=self.got_head.at[k - 1],
                send_sem=self.send.at[self.number, self.plan.bits + k - 1],
                recv_sem=self.recv.at[self.number, self.plan.bits + k - 1],
                device_id=(self.s, peer),
                device_id_type=MESH,
            )
            copy.start()
            self.started.append(copy)

    def finish_head(self):
        total = self.grad[self.index(self.order) + (self.h,)].astype(F32)
        for k in range(1, self.plan.head):
            self.started[self.plan.bits + k - 1].wait_recv()
            total = total + self.got_head[k - 1].astype(F32)
        self.out[...] = total

    def drain(self):
        for copy in self.started:
            copy.wait_send()


def layer_kernel(plan, *refs):
    refs = list(refs)

    def take(n):
        taken = refs[:n]
        del refs[:n]
        return taken

    x_in, dy_in, gain_one, shift_one, gain_two, shift_two, up_bias, down_bias = take(8)
    weights_in = take(6)
    lo_out, ig_out = take(2)
    grads_out = take(6)
    (vec_out,) = take(1)
    xg, dyg, log, igg = take(4)
    wq, wk, wv, wo, wu, wd = weights = take(6)
    norm_b, n_one, rs_one, n_two, rs_two, norm_two_b, residual, d_residual = take(8)
    q_ref, k_ref, v_ref, prob_ref, mask_ref, mixed_ref = take(6)
    act_ref, slope_ref, dh_ref = take(3)
    dmixed_ref, dq_ref, dk_ref, dv_ref, far_ref = take(5)
    c_send, c_got, d_send, d_got = take(4)
    names = list(plan.blocks)
    grads = take(6)
    gots = [take(plan.bits) for _ in names]
    got_heads = take(6)
    vec_bufs, vec_got = take(2)
    send_a, recv_a, send_r, recv_r, send_s, recv_s, here = take(7)
    assert not refs

    seq, head, rows, width, tokens = plan.seq, plan.head, plan.rows, plan.width, plan.tokens
    s, h = lax.axis_index("seq"), lax.axis_index("head")
    c, g = irem(s, plan.minor), idiv(s, plan.minor)
    j = c * head + h

    def group_peer(k):
        other = flip(j, k)
        return other, (g * plan.minor + idiv(other, head), irem(other, head))

    def row_peer(k):
        other = flip(g, k)
        return other, (other * plan.minor + c, h)

    barrier = pltpu.get_barrier_semaphore()
    peers = {}
    for k in range(1, rows):
        peers[("group", k)] = group_peer(k)[1]
    for k in range(1, plan.groups):
        peers[("row", k)] = row_peer(k)[1]
    for device in peers.values():
        pl.semaphore_signal(barrier, inc=1, device_id=device, device_id_type=MESH)

    loads = [pltpu.make_async_copy(a, b, here.at[i]) for i, (a, b) in enumerate(zip(weights_in, weights))]
    for i in (1, 2, 0, 3, 4, 5):
        loads[i].start()
    own = [
        pltpu.make_async_copy(x_in.at[j], xg.at[j], here.at[6]),
        pltpu.make_async_copy(dy_in.at[j], dyg.at[j], here.at[7]),
    ]
    for copy in own:
        copy.start()

    i_q = lax.broadcasted_iota(jnp.int32, (tokens, plan.keys), 0)
    i_k = lax.broadcasted_iota(jnp.int32, (tokens, plan.keys), 1)
    valid = (i_k < tokens) & ((i_q >> 5) == (i_k >> 5))
    first = tokens
    for level in range(1, plan.local):
        count = tokens >> level
        block = (i_k - first) >> 4
        here_level = (i_k >= first) & (i_k < first + count)
        valid = valid | (here_level & (((i_q >> (4 + level)) ^ 1) == block))
        first += count
    valid = valid | ((i_k >= plan.far) & (i_k < plan.far + BLOCK * plan.remote))
    mask_ref[...] = jnp.where(valid, 0.0, -1e30).astype(F32)

    pl.semaphore_wait(barrier, len(peers))

    def exchange(number, source, target):
        copies = []
        for k in range(1, rows):
            other, device = group_peer(k)
            copy = pltpu.make_async_remote_copy(
                src_ref=source.at[other],
                dst_ref=target.at[j],
                send_sem=send_a.at[number, k],
                recv_sem=recv_a.at[number, k],
                device_id=device,
                device_id_type=MESH,
            )
            copy.start()
            copies.append(copy)
        return copies

    x_copies = exchange(0, x_in, xg)
    dy_copies = exchange(1, dy_in, dyg)

    def norm_stats(values):
        center = values - jnp.mean(values, axis=-1, keepdims=True)
        spread = jnp.mean(center * center, axis=-1, keepdims=True)
        scale = lax.rsqrt(spread + EPSILON)
        return center * scale, scale

    def norm_back(d_norm, n, scale, gain):
        weighted = d_norm * gain
        return scale * (
            weighted
            - jnp.mean(weighted, axis=-1, keepdims=True)
            - n * jnp.mean(weighted * n, axis=-1, keepdims=True)
        )

    def store_pairs(ref, first, value):
        for p in range(plan.pairs):
            ref[p, first : first + value.shape[0], :] = value[:, p * PAIR : (p + 1) * PAIR]

    own[0].wait()
    for copy in x_copies:
        copy.wait_recv()
    x = xg[...].reshape(tokens, width).astype(F32)
    n, scale = norm_stats(x)
    n_one[...] = n
    rs_one[...] = scale
    normed = (n * gain_one[...] + shift_one[...]).astype(BF)
    norm_b[...] = normed
    for index, (w, load, ref) in enumerate(((wk, loads[1], k_ref), (wv, loads[2], v_ref))):
        load.wait()
        level = dot(normed, w[...]).astype(BF)
        store_pairs(ref, 0, level)
        first = tokens
        for l in range(plan.local):
            level = dot(pair_mean(level.shape[0]), level).astype(BF)
            if l + 1 < plan.local:
                store_pairs(ref, first, level)
                first += level.shape[0]
        c_send[index] = level
    c_copies = []
    for k in range(1, plan.groups):
        other, device = row_peer(k)
        copy = pltpu.make_async_remote_copy(
            src_ref=c_send,
            dst_ref=c_got.at[g],
            send_sem=send_r.at[0, k],
            recv_sem=recv_r.at[0, k],
            device_id=device,
            device_id_type=MESH,
        )
        copy.start()
        c_copies.append(copy)
    loads[0].wait()
    store_pairs(q_ref, 0, (dot(normed, wq[...]) * (DH**-0.5)).astype(BF))

    for copy in c_copies:
        copy.wait_recv()
    for index, ref in enumerate((k_ref, v_ref)):
        for b in range(plan.remote):
            upper = idiv(g, 1 << b)
            base = (upper + 1 - 2 * irem(upper, 2)) * (1 << b)
            level = c_got[pl.ds(base, 1 << b), index].reshape(BLOCK << b, width)
            for _ in range(b):
                level = dot(pair_mean(level.shape[0]), level).astype(BF)
            store_pairs(ref, plan.far + BLOCK * b, level)
        end = plan.far + BLOCK * plan.remote
        if end < plan.keys:
            store_pairs(ref, end, jnp.zeros((plan.keys - end, width), BF))

    lane = lax.broadcasted_iota(jnp.int32, (1, PAIR), 1)
    low = lane < DH

    def only(e, value):
        return jnp.where(low if e == 0 else ~low, value, jnp.zeros_like(value))

    def attend(p, carry):
        q, k, v = q_ref[p], k_ref[p], v_ref[p]
        mixed = []
        for e in range(2):
            scores = dot_t(only(e, q), k) + mask_ref[...]
            top = jnp.max(scores, axis=-1, keepdims=True)
            raised = jnp.exp(scores - top)
            prob = raised / jnp.sum(raised, axis=-1, keepdims=True)
            prob_ref[2 * p + e] = prob
            mixed.append(dot(prob.astype(BF), v))
        mixed_ref[p] = jnp.where(low, mixed[0], mixed[1]).astype(BF)
        return carry

    lax.fori_loop(0, plan.pairs, attend, 0)

    def joined(ref):
        return jnp.concatenate([ref[p] for p in range(plan.pairs)], axis=1)

    loads[3].wait()
    mixed = joined(mixed_ref)
    res = xg[...].reshape(tokens, width).astype(F32) + dot(mixed, wo[...])
    residual[...] = res
    n, scale = norm_stats(res)
    n_two[...] = n
    rs_two[...] = scale
    norm_two_b[...] = (n * gain_two[...] + shift_two[...]).astype(BF)

    sums = [
        Summed(plan, (s, h), name, i, grads[i], gots[i], got_heads[i], send_s, recv_s, grads_out[i])
        for i, name in enumerate(names)
    ]
    down, up, out, query, key, value = sums
    row = lambda a: jnp.sum(a, axis=0, keepdims=True)

    def put_all(target, block, first_row, first_col):
        r, w = plan.blocks[target.name]
        for a in range(0, block.shape[0], r):
            for b in range(0, block.shape[1], w):
                target.put((first_row + a) // r, (first_col + b) // w, block[a : a + r, b : b + w])

    loads[4].wait()
    loads[5].wait()
    own[1].wait()
    for copy in dy_copies:
        copy.wait_recv()
    chunk = 512
    dy = dyg[...].reshape(tokens, width)
    for f in range(0, plan.hidden, chunk):
        hid = dot(norm_two_b[...], wu[:, f : f + chunk]) + up_bias[:, f : f + chunk]
        cdf = 0.5 * (1.0 + lax.erf(hid * (0.5**0.5)))
        act = (hid * cdf).astype(BF)
        act_ref[:, f : f + chunk] = act
        slope_ref[:, f : f + chunk] = cdf + hid * (jnp.exp(-0.5 * hid * hid) * 0.3989422804014327)
        put_all(down, t_dot(act, dy), f, 0)
    down.start(0)

    hidden_rows = []
    for f in range(0, plan.hidden, chunk):
        dh = (dot_t(dy, wd[f : f + chunk, :]) * slope_ref[:, f : f + chunk]).astype(BF)
        dh_ref[:, f : f + chunk] = dh
        hidden_rows.append(row(dh.astype(F32)))
        put_all(up, t_dot(norm_two_b[...], dh), 0, f)
    up.start(0)
    down.finish(0)
    down.start(1)

    d_norm_two = dot_t(dh_ref[...], wu[...])
    n = n_two[...]
    dy_f = dy.astype(F32)
    vec_bufs[0, 2:3, :] = row(d_norm_two * n)
    vec_bufs[0, 3:4, :] = row(d_norm_two)
    vec_bufs[0, 4:5, :] = row(dy_f)
    per = plan.hidden // width
    for i in range(per):
        flat = jnp.concatenate(hidden_rows, axis=1)
        vec_bufs[0, 5 + i : 6 + i, :] = flat[:, i * width : (i + 1) * width]
    d_res = dy_f + norm_back(d_norm_two, n, rs_two[...], gain_two[...])
    d_residual[...] = d_res
    d_mix = d_res.astype(BF)
    put_all(out, t_dot(joined(mixed_ref), d_mix), 0, 0)
    out.start(0)
    store_pairs(dmixed_ref, 0, dot_t(d_mix, wo[...]).astype(BF))
    up.finish(0)
    up.start(1)

    result = residual[...] + dot(act_ref[...], wd[...]) + down_bias[...]
    log[...] = result.astype(BF).reshape(rows, plan.pos, width)
    lo_copies = exchange(2, log, lo_out)
    lo_own = pltpu.make_async_copy(log.at[j], lo_out.at[j], here.at[8])
    lo_own.start()
    out.finish(0)
    out.start(1)

    i_t = lax.broadcasted_iota(jnp.int32, (tokens, tokens), 0)
    i_c = lax.broadcasted_iota(jnp.int32, (tokens, tokens), 1)
    spread = jnp.zeros((tokens, tokens), F32)
    first = 0
    for level in range(1, plan.local):
        count = tokens >> level
        spread = spread + jnp.where((i_t >> level) == (i_c - first), 0.5**level, 0.0)
        first += count
    spread = spread.astype(BF)

    def attend_back(p, carry):
        q, k, v, dm = q_ref[p], k_ref[p], v_ref[p], dmixed_ref[p]
        dq, dk, dv = [], 0.0, 0.0
        for e in range(2):
            dm_e = only(e, dm)
            prob = prob_ref[2 * p + e]
            d_prob = dot_t(dm_e, v)
            inner = jnp.sum(prob * d_prob, axis=-1, keepdims=True)
            d_scores = (prob * (d_prob - inner)).astype(BF)
            dq.append(dot(d_scores, k))
            dk = dk + t_dot(d_scores, only(e, q))
            dv = dv + t_dot(prob.astype(BF), dm_e)
        dq_ref[p] = (jnp.where(low, dq[0], dq[1]) * (DH**-0.5)).astype(BF)
        for index, (total, ref) in enumerate(((dk, dk_ref), (dv, dv_ref))):
            ref[p] = total[:tokens] + two_part_dot(spread, total[tokens : 2 * tokens])
            far_ref[index, p] = total[plan.far :]
        return carry

    half = plan.pairs // 2
    lax.fori_loop(0, half, attend_back, 0)
    down.finish(1)
    down.start(2)
    lax.fori_loop(half, plan.pairs, attend_back, 0)

    i_a = lax.broadcasted_iota(jnp.int32, (BLOCK, BLOCK), 0)
    i_b = lax.broadcasted_iota(jnp.int32, (BLOCK, BLOCK), 1)
    d_copies = []
    for k in range(1, plan.groups):
        other, device = row_peer(k)
        b = k.bit_length() - 1
        offset = irem(other, 1 << b)
        pick = jnp.where(((offset * BLOCK + i_a) >> b) == i_b, 0.5**b, 0.0).astype(BF)
        for index in range(2):
            for p in range(plan.pairs):
                level = far_ref[index, p, BLOCK * b : BLOCK * (b + 1), :].astype(BF)
                d_send[k, index, p] = dot(pick, level).astype(BF)
        copy = pltpu.make_async_remote_copy(
            src_ref=d_send.at[k],
            dst_ref=d_got.at[k],
            send_sem=send_r.at[1, k],
            recv_sem=recv_r.at[1, k],
            device_id=device,
            device_id_type=MESH,
        )
        copy.start()
        d_copies.append(copy)

    normed = norm_b[...]
    d_query = joined(dq_ref)
    put_all(query, t_dot(normed, d_query), 0, 0)
    query.start(0)
    up.finish(1)
    up.start(2)
    d_normed = dot_t(d_query, wq[...])
    out.finish(1)
    out.start(2)

    for copy in d_copies:
        copy.wait_recv()
    i_t = lax.broadcasted_iota(jnp.int32, (tokens, BLOCK), 0)
    i_c = lax.broadcasted_iota(jnp.int32, (tokens, BLOCK), 1)
    last = jnp.where((i_t >> plan.local) == i_c, 0.5**plan.local, 0.0).astype(BF)
    for index, (ref, w, target) in enumerate(((dk_ref, wk, key), (dv_ref, wv, value))):
        pieces = []
        for p in range(plan.pairs):
            total = ref[p]
            if plan.groups > 1:
                coarse = d_got[1, index, p].astype(F32)
                for k in range(2, plan.groups):
                    coarse = coarse + d_got[k, index, p].astype(F32)
                total = total + two_part_dot(last, coarse)
            pieces.append(total.astype(BF))
        d_part = jnp.concatenate(pieces, axis=1)
        put_all(target, t_dot(normed, d_part), 0, 0)
        target.start(0)
        d_normed = d_normed + dot_t(d_part, w[...])
    query.finish(0)
    query.start(1)

    n = n_one[...]
    vec_bufs[0, 0:1, :] = row(d_normed * n)
    vec_bufs[0, 1:2, :] = row(d_normed)
    for i in range(5 + per, VEC_ROWS):
        vec_bufs[0, i : i + 1, :] = jnp.zeros((1, width), F32)

    vec_copies = []

    def vec_start(stage):
        if stage < plan.bits:
            jobs = [(stage, (flip(s, 1 << stage), h))]
        else:
            jobs = [(plan.bits + k - 1, (s, flip(h, k))) for k in range(1, head)]
        for slot, device in jobs:
            copy = pltpu.make_async_remote_copy(
                src_ref=vec_bufs.at[min(slot, plan.bits)],
                dst_ref=vec_got.at[slot],
                send_sem=send_s.at[6, slot],
                recv_sem=recv_s.at[6, slot],
                device_id=device,
                device_id_type=MESH,
            )
            copy.start()
            vec_copies.append(copy)

    def vec_finish(stage):
        vec_copies[stage].wait_recv()
        vec_bufs[stage + 1] = vec_bufs[stage] + vec_got[stage]

    vec_start(0)
    d_first = norm_back(d_normed, n, rs_one[...], gain_one[...])
    igg[...] = (d_residual[...] + d_first).astype(BF).reshape(rows, plan.pos, width)
    ig_copies = exchange(3, igg, ig_out)
    ig_own = pltpu.make_async_copy(igg.at[j], ig_out.at[j], here.at[9])
    ig_own.start()

    key.finish(0)
    key.start(1)
    value.finish(0)
    value.start(1)
    vec_finish(0)
    done = {"down": 2, "up": 2, "out": 2, "query": 1, "key": 1, "value": 1}
    vec_done = 1
    while True:
        if vec_done <= plan.bits:
            vec_start(vec_done)
        for item in sums:
            stage = done[item.name]
            if stage < plan.bits:
                item.finish(stage)
                if stage + 1 < plan.bits:
                    item.start(stage + 1)
                else:
                    item.start_head()
            done[item.name] = stage + 1
        if vec_done < plan.bits:
            vec_finish(vec_done)
        vec_done += 1
        if vec_done > plan.bits and all(stage >= plan.bits for stage in done.values()):
            break
    for item in sums:
        item.finish_head()
    near = vec_bufs[plan.bits]
    parts = []
    for k in range(1, head):
        vec_copies[plan.bits + k - 1].wait_recv()
        parts.append(vec_got[plan.bits + k - 1])
    values = [near] + parts
    while len(values) > 1:
        values = [values[i] + values[i + 1] for i in range(0, len(values), 2)]
    vec_out[...] = values[0]

    for copy in lo_copies + ig_copies:
        copy.wait_recv()
    lo_own.wait()
    ig_own.wait()
    for copy in x_copies + dy_copies + lo_copies + ig_copies + c_copies + d_copies + vec_copies:
        copy.wait_send()
    for item in sums:
        item.drain()


def body(
    inputs,
    gain_first,
    shift_first,
    query_weight,
    key_weight,
    value_weight,
    out_weight,
    gain_second,
    shift_second,
    up_weight,
    up_bias,
    down_weight,
    down_bias,
    cotangent,
):
    rows, pos, width = inputs.shape
    hidden = up_weight.shape[1]
    plan = Plan(lax.axis_size("seq"), lax.axis_size("head"), rows, pos, width, hidden)
    tokens, keys, pairs, groups, bits = plan.tokens, plan.keys, plan.pairs, plan.groups, plan.bits
    vmem = pl.BlockSpec(memory_space=pltpu.VMEM)
    anywhere = pl.BlockSpec(memory_space=pl.ANY)
    names = list(plan.blocks)

    def buf(*shape, dtype=BF):
        return pltpu.VMEM(shape, dtype)

    scratch = [buf(rows, pos, width)] * 4
    scratch += [buf(width, width)] * 4 + [buf(width, hidden), buf(hidden, width)]
    scratch += [
        buf(tokens, width),
        buf(tokens, width, dtype=F32),
        buf(tokens, 1, dtype=F32),
        buf(tokens, width, dtype=F32),
        buf(tokens, 1, dtype=F32),
        buf(tokens, width),
        buf(tokens, width, dtype=F32),
        buf(tokens, width, dtype=F32),
    ]
    scratch += [
        buf(pairs, tokens, PAIR),
        buf(pairs, keys, PAIR),
        buf(pairs, keys, PAIR),
        buf(2 * pairs, tokens, keys, dtype=F32),
        buf(tokens, keys, dtype=F32),
        buf(pairs, tokens, PAIR),
    ]
    scratch += [buf(tokens, hidden), buf(tokens, hidden, dtype=F32), buf(tokens, hidden)]
    scratch += [
        buf(pairs, tokens, PAIR),
        buf(pairs, tokens, PAIR),
        buf(pairs, tokens, PAIR, dtype=F32),
        buf(pairs, tokens, PAIR, dtype=F32),
        buf(2, pairs, keys - plan.far, PAIR, dtype=F32),
    ]
    scratch += [
        buf(2, BLOCK, width),
        buf(groups, 2, BLOCK, width),
        buf(groups, 2, pairs, BLOCK, PAIR),
        buf(groups, 2, pairs, BLOCK, PAIR),
    ]
    head = plan.head
    scratch += [buf(*(2,) * bits, head, *plan.blocks[n]) for n in names]
    for n in names:
        scratch += [buf(*(2,) * (bits - 1 - i), head, *plan.blocks[n]) for i in range(bits)]
    scratch += [buf(head - 1, *plan.blocks[n]) for n in names]
    scratch += [buf(bits + 1, VEC_ROWS, width, dtype=F32), buf(bits + head - 1, VEC_ROWS, width, dtype=F32)]
    dma = pltpu.SemaphoreType.DMA
    scratch += [dma((4, rows)), dma((4, rows)), dma((2, groups)), dma((2, groups))]
    scratch += [dma((7, bits + head - 1)), dma((7, bits + head - 1)), dma((10,))]

    line = lambda a: a.reshape(1, -1)
    results = pl.pallas_call(
        functools.partial(layer_kernel, plan),
        out_shape=[
            jax.ShapeDtypeStruct(inputs.shape, BF),
            jax.ShapeDtypeStruct(inputs.shape, BF),
            *(jax.ShapeDtypeStruct(plan.blocks[n], F32) for n in names),
            jax.ShapeDtypeStruct((VEC_ROWS, width), F32),
        ],
        in_specs=[anywhere, anywhere] + [vmem] * 6 + [anywhere] * 6,
        out_specs=[anywhere, anywhere] + [vmem] * 7,
        scratch_shapes=scratch,
        compiler_params=pltpu.CompilerParams(
            collective_id=0, has_side_effects=True, vmem_limit_bytes=56 << 20
        ),
        name="layer",
    )(
        inputs,
        cotangent,
        line(gain_first),
        line(shift_first),
        line(gain_second),
        line(shift_second),
        line(up_bias),
        line(down_bias),
        query_weight,
        key_weight,
        value_weight,
        out_weight,
        up_weight,
        down_weight,
    )
    layer_out, input_grad, down_g, up_g, out_g, query_g, key_g, value_g, vec = results
    seq_index = lax.axis_index("seq")

    def mine(vector):
        share = vector.shape[0] // plan.seq
        return lax.dynamic_slice_in_dim(vector, seq_index * share, share, 0)

    per = hidden // width
    return (
        layer_out,
        input_grad,
        mine(vec[0]),
        mine(vec[1]),
        query_g,
        key_g,
        value_g,
        out_g,
        mine(vec[2]),
        mine(vec[3]),
        up_g,
        mine(vec[5 : 5 + per].reshape(-1)),
        down_g,
        mine(vec[4]),
    )


def solution(mesh):
    placed = (P(None, ("seq", "head"), None),) + (P(),) * 12 + (P(None, ("seq", "head"), None),)
    return jax.shard_map(
        body,
        mesh=mesh,
        in_specs=placed,
        out_specs=(
            P(None, ("seq", "head"), None),
            P(None, ("seq", "head"), None),
            P("seq"),
            P("seq"),
            P("seq", "head"),
            P("seq", "head"),
            P("seq", "head"),
            P("seq", "head"),
            P("seq"),
            P("seq"),
            P("seq", "head"),
            P("seq"),
            P("seq", "head"),
            P("seq"),
        ),
        check_vma=False,
    )
```

```python
import functools

import jax
import jax.numpy as jnp
from jax import lax
from jax.experimental import pallas as pl
from jax.experimental.pallas import tpu as pltpu
from jax.sharding import PartitionSpec as P

MESH = pl.DeviceIdType.MESH
BF = jnp.bfloat16
F32 = jnp.float32
DH = 64
BLOCK = 16
EPSILON = 1e-05
PAIR = 2 * DH
VEC_ROWS = 16


def idiv(value, k):
    return lax.div(value, jnp.int32(k))


def irem(value, k):
    return lax.rem(value, jnp.int32(k))


def bit_of(value, b):
    return irem(idiv(value, 1 << b), 2)


def flip(value, k):
    b = 0
    while k >> b:
        if (k >> b) & 1:
            value = value + (1 - 2 * bit_of(value, b)) * (1 << b)
        b += 1
    return value


def dot(a, b):
    return jnp.dot(a, b, preferred_element_type=F32)


def dot_t(a, b):
    return lax.dot_general(a, b, (((1,), (1,)), ((), ())), preferred_element_type=F32)


def t_dot(a, b):
    return lax.dot_general(a, b, (((0,), (0,)), ((), ())), preferred_element_type=F32)


def two_part_dot(a, b):
    high = b.astype(BF)
    low = (b - high.astype(F32)).astype(BF)
    return dot(a, high) + dot(a, low)


def pair_mean(rows):
    i = lax.broadcasted_iota(jnp.int32, (rows // 2, rows), 0)
    j = lax.broadcasted_iota(jnp.int32, (rows // 2, rows), 1)
    return jnp.where((j >> 1) == i, 0.5, 0.0).astype(BF)


def identity(n):
    i = lax.broadcasted_iota(jnp.int32, (n, n), 0)
    j = lax.broadcasted_iota(jnp.int32, (n, n), 1)
    return jnp.where(i == j, 1.0, 0.0).astype(BF)


def turned(value):
    n = PAIR
    parts = [
        dot_t(identity(n), value[:, i : i + n]).astype(BF) for i in range(0, value.shape[1], n)
    ]
    return parts[0] if len(parts) == 1 else jnp.concatenate(parts, axis=0)


class Plan:
    def __init__(self, seq, head, rows, pos, width, hidden):
        self.seq, self.head, self.rows, self.pos, self.width, self.hidden = seq, head, rows, pos, width, hidden
        self.minor = rows // head
        self.groups = seq // self.minor
        self.tokens = rows * pos
        self.half = self.tokens // 2
        self.pairs = width // PAIR
        self.local = (self.tokens // BLOCK).bit_length() - 1
        self.remote = self.groups.bit_length() - 1
        self.seq_bits = seq.bit_length() - 1
        self.head_bits = head.bit_length() - 1
        self.bits = self.seq_bits + self.head_bits
        self.near = self.half * 2
        self.far = BLOCK * (self.remote - 1)
        cols = width // head
        self.blocks = {
            "down": (hidden // seq, cols),
            "up": (width // seq, hidden // head),
            "out": (width // seq, cols),
            "query": (width // seq, cols),
            "key": (width // seq, cols),
            "value": (width // seq, cols),
        }
        seqs, heads = list(range(self.seq_bits)), list(range(self.seq_bits, self.bits))
        one, two = seqs, seqs[:1] + seqs[:0:-1]

        def cut(name):
            r = self.blocks[name][0]
            m = r // 2 if r % 32 == 0 else r
            return [(name, 0, m)], [(name, m, r)] if m < r else []

        down, up, key = cut("down"), cut("up"), cut("key")
        whole = lambda n: [(n, 0, self.blocks[n][0])]
        self.sums = {
            "down_a": (down[0], one + heads),
            "down_b": (down[1], two + heads),
            "up_a": (up[0], one + heads),
            "up_b": (up[1], two + heads),
            "out": (whole("out"), one[:1] + heads + one[1:]),
            "part_a": (whole("query") + key[0], one + ["head"]),
            "part_b": (key[1] + whole("value"), two + ["head"]),
        }
        self.sums = {n: v for n, v in self.sums.items() if v[0]}

    def sum_shape(self, name):
        parts = self.sums[name][0]
        return (sum(b - a for _, a, b in parts), self.blocks[parts[0][0]][1])

    def got_shapes(self, name):
        left, shapes = self.bits, []
        for b in self.sums[name][1]:
            if b == "head":
                shapes.append((self.head - 1,) + self.sum_shape(name))
            else:
                left -= 1
                shapes.append((2,) * left + self.sum_shape(name))
        return shapes


class Summed:
    def __init__(self, plan, me, name, number, grad, got, send, recv, outs):
        self.plan, self.name, self.number = plan, name, number
        self.s, self.h = me
        self.grad, self.got, self.outs = grad, got, outs
        self.send, self.recv = send, recv
        self.parts, self.order = plan.sums[name]
        self.started, self.stage = [], 0

    def own_bit(self, b):
        n = self.plan.seq_bits
        return bit_of(self.s, b) if b < n else bit_of(self.h, b - n)

    def index(self, fixed, other=None):
        at = []
        for b in reversed(range(self.plan.bits)):
            if b == other:
                at.append(1 - self.own_bit(b))
            elif b in fixed:
                at.append(self.own_bit(b))
            else:
                at.append(slice(None))
        return tuple(at)

    def put(self, name, s, h, block):
        owner = s + h * self.plan.seq
        at = tuple((owner >> b) & 1 for b in reversed(range(self.plan.bits)))
        first = 0
        for part, a, b in self.parts:
            if part == name:
                self.grad[at + (slice(first, first + b - a),)] = block[a:b].astype(BF)
            first += b - a

    def copy(self, source, target, slot, device):
        copy = pltpu.make_async_remote_copy(
            src_ref=source,
            dst_ref=target,
            send_sem=self.send.at[self.number, slot],
            recv_sem=self.recv.at[self.number, slot],
            device_id=device,
            device_id_type=MESH,
        )
        copy.start()
        self.started.append(copy)

    def start(self, stage):
        b = self.order[stage]
        n = self.plan.seq_bits
        if b == "head":
            for k in range(1, self.plan.head):
                peer = flip(self.h, k)
                at = tuple(bit_of(peer, i) for i in reversed(range(self.plan.head_bits)))
                at += self.index(range(n))[self.plan.head_bits :]
                self.copy(self.grad.at[at], self.got[stage].at[k - 1], stage + k - 1, (self.s, peer))
            return
        device = (flip(self.s, 1 << b), self.h) if b < n else (self.s, flip(self.h, 1 << (b - n)))
        source = self.grad.at[self.index(self.order[:stage], b)]
        self.copy(source, self.got[stage], stage, device)

    def finish(self, stage):
        b = self.order[stage]
        if stage + 1 == len(self.order):
            total = self.grad[self.index(range(self.plan.bits))].astype(F32)
            if b == "head":
                for k in range(1, self.plan.head):
                    self.started[stage + k - 1].wait_recv()
                    total = total + self.got[stage][k - 1].astype(F32)
            else:
                self.started[stage].wait_recv()
                total = total + self.got[stage][...].astype(F32)
            first = 0
            for part, a, b in self.parts:
                self.outs[part][a:b, :] = total[first : first + b - a]
                first += b - a
            return
        self.started[stage].wait_recv()
        at = self.index(self.order[: stage + 1])
        combos = [()]
        for a in at:
            if isinstance(a, slice):
                combos = [c + (i,) for c in combos for i in range(2)]
        for combo in combos:
            left = list(combo)
            full = tuple(left.pop(0) if isinstance(a, slice) else a for a in at)
            self.grad[full] = self.grad[full] + self.got[stage][combo]

    def step(self):
        if self.stage:
            self.finish(self.stage - 1)
        if self.stage < len(self.order):
            self.start(self.stage)
        self.stage += 1

    @property
    def done(self):
        return self.stage > len(self.order)

    def drain(self):
        for copy in self.started:
            copy.wait_send()


def layer_kernel(plan, *refs):
    refs = list(refs)

    def take(n):
        taken = refs[:n]
        del refs[:n]
        return taken

    x_in, dy_in, gain_one, shift_one, gain_two, shift_two, up_bias, down_bias = take(8)
    weights_in = take(6)
    lo_out, ig_out = take(2)
    grads_out = dict(zip(plan.blocks, take(6)))
    (vec_out,) = take(1)
    xg, dyg, log, igg = take(4)
    wq, wk, wv, wo, wu, wd = weights = take(6)
    norm_t, n_one, rs_one, n_two, rs_two, norm_two_b, residual, d_residual = take(8)
    qs, kn, vn, kr, vr, kn_t, vn_t, kr_t, vr_t = take(9)
    pn, pr, stats, mask, mixed_t = take(5)
    act_ref, slope_ref, dh_ref = take(3)
    dos, dq_t, dk_ref, dv_ref, far_ref, bar_t = take(6)
    c_send, c_got, d_send, d_got = take(4)
    sums = {}
    for name in plan.sums:
        grad, *got = take(1 + len(plan.sums[name][1]))
        sums[name] = (grad, got)
    vec_bufs, vec_got = take(2)
    send_a, recv_a, send_r, recv_r, send_s, recv_s, here = take(7)
    assert not refs

    seq, head, rows, width, tokens = plan.seq, plan.head, plan.rows, plan.width, plan.tokens
    half, near, far = plan.half, plan.near, plan.far
    s, h = lax.axis_index("seq"), lax.axis_index("head")
    c, g = irem(s, plan.minor), idiv(s, plan.minor)
    j = c * head + h

    def group_peer(k):
        other = flip(j, k)
        return other, (g * plan.minor + idiv(other, head), irem(other, head))

    def row_peer(k):
        other = flip(g, k)
        return other, (other * plan.minor + c, h)

    barrier = pltpu.get_barrier_semaphore()
    peers = [group_peer(k)[1] for k in range(1, rows)] + [row_peer(k)[1] for k in range(1, plan.groups)]
    for device in peers:
        pl.semaphore_signal(barrier, inc=1, device_id=device, device_id_type=MESH)

    loads = [pltpu.make_async_copy(a, b, here.at[i]) for i, (a, b) in enumerate(zip(weights_in, weights))]
    for i in (1, 2, 0, 3, 4, 5):
        loads[i].start()
    own = [
        pltpu.make_async_copy(x_in.at[j], xg.at[j], here.at[6]),
        pltpu.make_async_copy(dy_in.at[j], dyg.at[j], here.at[7]),
    ]
    for copy in own:
        copy.start()

    i_k = lax.broadcasted_iota(jnp.int32, (near, 2 * half), 0)
    i_q = lax.broadcasted_iota(jnp.int32, (near, 2 * half), 1) & (half - 1)
    valid = (i_k < half) & ((i_q >> 5) == (i_k >> 5))
    first = half
    for level in range(1, plan.local - 1):
        count = half >> level
        mine = (i_k >= first) & (i_k < first + count)
        valid = valid | (mine & (((i_q >> (4 + level)) ^ 1) == ((i_k - first) >> 4)))
        first += count
    valid = valid | (i_k >= first)
    mask[...] = jnp.where(valid, 0.0, -1e30).astype(F32)

    pl.semaphore_wait(barrier, len(peers))

    def exchange(number, source, target):
        copies = []
        for k in range(1, rows):
            other, device = group_peer(k)
            copy = pltpu.make_async_remote_copy(
                src_ref=source.at[other],
                dst_ref=target.at[j],
                send_sem=send_a.at[number, k],
                recv_sem=recv_a.at[number, k],
                device_id=device,
                device_id_type=MESH,
            )
            copy.start()
            copies.append(copy)
        return copies

    x_copies = exchange(0, x_in, xg)

    def norm_stats(values):
        center = values - jnp.mean(values, axis=-1, keepdims=True)
        spread = jnp.mean(center * center, axis=-1, keepdims=True)
        scale = lax.rsqrt(spread + EPSILON)
        return center * scale, scale

    def norm_back(d_norm, n, scale, gain):
        weighted = d_norm * gain
        return scale * (
            weighted
            - jnp.mean(weighted, axis=-1, keepdims=True)
            - n * jnp.mean(weighted * n, axis=-1, keepdims=True)
        )

    lane = lax.broadcasted_iota(jnp.int32, (1, PAIR), 1)
    low = lane < DH

    def stack_heads(ref, value):
        for p in range(plan.pairs):
            for a in range(2):
                part = value[a * half : (a + 1) * half, p * PAIR : (p + 1) * PAIR]
                zero = jnp.zeros_like(part)
                ref[p, a, :half, :] = jnp.where(low, part, zero)
                ref[p, a, half:, :] = jnp.where(low, zero, part)

    own[0].wait()
    for copy in x_copies:
        copy.wait_recv()
    dy_copies = exchange(1, dy_in, dyg)
    x = xg[...].reshape(tokens, width).astype(F32)
    n, scale = norm_stats(x)
    n_one[...] = n
    rs_one[...] = scale
    normed = (n * gain_one[...] + shift_one[...]).astype(BF)

    loads[1].wait()
    loads[2].wait()
    level = jnp.concatenate([dot(normed, wk[...]).astype(BF), dot(normed, wv[...]).astype(BF)], axis=1)

    def columns(index, p):
        return slice(index * width + p * PAIR, index * width + (p + 1) * PAIR)

    targets = (kn, vn)
    first = 0
    for l in range(plan.local):
        if l:
            level = dot(pair_mean(level.shape[0]), level).astype(BF)
        count = level.shape[0] // 2
        for index, ref in enumerate(targets):
            for p in range(plan.pairs):
                for a in range(2):
                    b = a if l + 1 < plan.local else 1 - a
                    ref[p, b, first : first + count, :] = level[a * count : (a + 1) * count, columns(index, p)]
        first += count
    level = dot(pair_mean(level.shape[0]), level).astype(BF)
    c_send[0] = level[:, :width]
    c_send[1] = level[:, width:]
    i_a = lax.broadcasted_iota(jnp.int32, (BLOCK, tokens), 0)
    i_b = lax.broadcasted_iota(jnp.int32, (BLOCK, tokens), 1)
    mean_all = jnp.where((i_b >> plan.local) == i_a, 0.5**plan.local, 0.0).astype(BF)
    c_send[2] = dot(mean_all, normed).astype(BF)
    c_copies = []
    for k in range(1, plan.groups):
        other, device = row_peer(k)
        copy = pltpu.make_async_remote_copy(
            src_ref=c_send,
            dst_ref=c_got.at[g],
            send_sem=send_r.at[0, k],
            recv_sem=recv_r.at[0, k],
            device_id=device,
            device_id_type=MESH,
        )
        copy.start()
        c_copies.append(copy)

    loads[0].wait()
    stack_heads(qs, (dot(normed, wq[...]) * (DH**-0.5)).astype(BF))
    norm_t[...] = turned(normed)
    local = near - BLOCK

    def attend_near(p, carry):
        for a in range(2):
            scores = dot_t(kn[p, a, :local, :], qs[p, a]) + mask[:local, :]
            top = jnp.max(scores, axis=0, keepdims=True)
            raised = jnp.exp(scores - top)
            pn[p, a, :local, :] = raised
            stats[p, a, 0:1, :] = top
            stats[p, a, 1:2, :] = jnp.sum(raised, axis=0, keepdims=True)
        return carry

    lax.fori_loop(0, plan.pairs, attend_near, 0)

    for copy in c_copies:
        copy.wait_recv()
    for index in range(3):
        for b in range(plan.remote):
            upper = idiv(g, 1 << b)
            base = (upper + 1 - 2 * irem(upper, 2)) * (1 << b)
            level = c_got[pl.ds(base, 1 << b), index].reshape(BLOCK << b, width)
            for _ in range(b):
                level = dot(pair_mean(level.shape[0]), level).astype(BF)
            if index == 2:
                bar_t[:, b * BLOCK : (b + 1) * BLOCK] = turned(level)
                continue
            for p in range(plan.pairs):
                part = level[:, p * PAIR : (p + 1) * PAIR]
                if b == 0:
                    for a in range(2):
                        targets[index][p, a, local:, :] = part
                else:
                    (kr, vr)[index][p, (b - 1) * BLOCK : b * BLOCK, :] = part

    def attend(p, carry):
        kr_t[p] = turned(kr[p])
        vr_t[p] = turned(vr[p])
        for a in range(2):
            kn_t[p, a] = turned(kn[p, a])
            vn_t[p, a] = turned(vn[p, a])
            q = qs[p, a]
            top_near = stats[p, a, 0:1, :]
            first_far = dot_t(kn[p, a, local:, :], q)
            rest_far = dot_t(kr[p], q)
            top = jnp.maximum(
                top_near,
                jnp.maximum(
                    jnp.max(first_far, axis=0, keepdims=True), jnp.max(rest_far, axis=0, keepdims=True)
                ),
            )
            shrink = jnp.exp(top_near - top)
            first_far = jnp.exp(first_far - top)
            rest_far = jnp.exp(rest_far - top)
            total = (
                stats[p, a, 1:2, :] * shrink
                + jnp.sum(first_far, axis=0, keepdims=True)
                + jnp.sum(rest_far, axis=0, keepdims=True)
            )
            share = 1.0 / total
            pn[p, a, :local, :] = pn[p, a, :local, :] * (shrink * share)
            pn[p, a, local:, :] = first_far * share
            rest_far = rest_far * share
            pr[p, a] = rest_far
            mixed = dot(vn_t[p, a], pn[p, a].astype(BF)) + dot(vr_t[p], rest_far.astype(BF))
            mixed_t[p, :DH, a * half : (a + 1) * half] = mixed[:DH, :half].astype(BF)
            mixed_t[p, DH:, a * half : (a + 1) * half] = mixed[DH:, half:].astype(BF)
        return carry

    lax.fori_loop(0, plan.pairs, attend, 0)

    loads[3].wait()
    res = xg[...].reshape(tokens, width).astype(F32) + t_dot(mixed_t[...].reshape(width, tokens), wo[...])
    residual[...] = res
    n, scale = norm_stats(res)
    n_two[...] = n
    rs_two[...] = scale
    norm_two_b[...] = (n * gain_two[...] + shift_two[...]).astype(BF)

    sums = {
        name: Summed(plan, (s, h), name, i, grad, got, send_s, recv_s, grads_out)
        for i, (name, (grad, got)) in enumerate(sums.items())
    }
    row = lambda a: jnp.sum(a, axis=0, keepdims=True)

    def step(*names):
        for name in names:
            if name in sums:
                sums[name].step()

    def put_all(name, block, first_row, first_col):
        r, w = plan.blocks[name]
        for a in range(0, block.shape[0], r):
            for b in range(0, block.shape[1], w):
                for item in sums.values():
                    item.put(name, (first_row + a) // r, (first_col + b) // w, block[a : a + r, b : b + w])

    loads[4].wait()
    loads[5].wait()
    own[1].wait()
    for copy in dy_copies:
        copy.wait_recv()
    chunk = 512
    dy = dyg[...].reshape(tokens, width)
    for f in range(0, plan.hidden, chunk):
        hid = dot(norm_two_b[...], wu[:, f : f + chunk]) + up_bias[:, f : f + chunk]
        cdf = 0.5 * (1.0 + lax.erf(hid * (0.5**0.5)))
        act = (hid * cdf).astype(BF)
        act_ref[:, f : f + chunk] = act
        slope_ref[:, f : f + chunk] = cdf + hid * (jnp.exp(-0.5 * hid * hid) * 0.3989422804014327)
        put_all("down", t_dot(act, dy), f, 0)
    step("down_a", "down_b")

    hidden_rows = []
    for i, f in enumerate(range(0, plan.hidden, chunk)):
        dh = (dot_t(dy, wd[f : f + chunk, :]) * slope_ref[:, f : f + chunk]).astype(BF)
        dh_ref[:, f : f + chunk] = dh
        hidden_rows.append(row(dh.astype(F32)))
        put_all("up", t_dot(norm_two_b[...], dh), 0, f)
        if i == 2:
            step("down_a", "down_b")
    step("up_a", "up_b")

    d_norm_two = dot_t(dh_ref[...], wu[...])
    n = n_two[...]
    dy_f = dy.astype(F32)
    vec_bufs[0, 2:3, :] = row(d_norm_two * n)
    vec_bufs[0, 3:4, :] = row(d_norm_two)
    vec_bufs[0, 4:5, :] = row(dy_f)
    per = plan.hidden // width
    flat = jnp.concatenate(hidden_rows, axis=1)
    for i in range(per):
        vec_bufs[0, 5 + i : 6 + i, :] = flat[:, i * width : (i + 1) * width]
    d_res = dy_f + norm_back(d_norm_two, n, rs_two[...], gain_two[...])
    d_residual[...] = d_res
    d_mix = d_res.astype(BF)
    step("up_a", "up_b")
    put_all("out", dot(mixed_t[...].reshape(width, tokens), d_mix), 0, 0)
    step("out")
    stack_heads(dos, dot_t(d_mix, wo[...]).astype(BF))

    i_t = lax.broadcasted_iota(jnp.int32, (half, half), 0)
    i_c = lax.broadcasted_iota(jnp.int32, (half, half), 1)
    spread = jnp.zeros((half, half), F32)
    first = 0
    for level in range(1, plan.local):
        spread = spread + jnp.where((i_t >> level) == (i_c - first), 0.5**level, 0.0)
        first += half >> level
    spread = jnp.where(i_c < first, spread, 0.0).astype(BF)

    def attend_back(p, carry):
        dk, dv, dk_far, dv_far = [], [], 0.0, 0.0
        for a in range(2):
            q, do = qs[p, a], dos[p, a]
            prob, prob_far = pn[p, a], pr[p, a]
            d_prob = dot_t(vn[p, a], do)
            d_prob_far = dot_t(vr[p], do)
            inner = row(prob * d_prob) + row(prob_far * d_prob_far)
            d_scores = (prob * (d_prob - inner)).astype(BF)
            d_scores_far = (prob_far * (d_prob_far - inner)).astype(BF)
            dk.append(dot(d_scores, q))
            dv.append(dot(prob.astype(BF), do))
            dk_far = dk_far + dot(d_scores_far, q)
            dv_far = dv_far + dot(prob_far.astype(BF), do)
            dq = (dot(kn_t[p, a], d_scores) + dot(kr_t[p], d_scores_far)) * (DH**-0.5)
            dq_t[p, :DH, a * half : (a + 1) * half] = dq[:DH, :half].astype(BF)
            dq_t[p, DH:, a * half : (a + 1) * half] = dq[DH:, half:].astype(BF)
        other = half + first - BLOCK
        for index, (total, total_far, ref) in enumerate(((dk, dk_far, dk_ref), (dv, dv_far, dv_ref))):
            for a in range(2):
                coarse = jnp.concatenate(
                    [total[a][half:other], total[1 - a][other : other + BLOCK], total[a][local:]], axis=0
                )
                ref[p, a * half : (a + 1) * half, :] = total[a][:half] + two_part_dot(spread, coarse)
            far_ref[index, p, :BLOCK, :] = total[0][local:] + total[1][local:]
            far_ref[index, p, BLOCK:, :] = total_far
        return carry

    lax.fori_loop(0, plan.pairs // 2, attend_back, 0)

    result = residual[...] + dot(act_ref[...], wd[...]) + down_bias[...]
    log[...] = result.astype(BF).reshape(rows, plan.pos, width)
    lo_copies = exchange(2, log, lo_out)
    lo_own = pltpu.make_async_copy(log.at[j], lo_out.at[j], here.at[8])
    lo_own.start()
    step("out")

    lax.fori_loop(plan.pairs // 2, plan.pairs, attend_back, 0)

    i_a = lax.broadcasted_iota(jnp.int32, (BLOCK, BLOCK), 0)
    i_b = lax.broadcasted_iota(jnp.int32, (BLOCK, BLOCK), 1)
    d_copies = []
    for k in range(1, plan.groups):
        other, device = row_peer(k)
        b = k.bit_length() - 1
        offset = irem(other, 1 << b)
        pick = jnp.where(((offset * BLOCK + i_a) >> b) == i_b, 0.5**b, 0.0).astype(BF)
        for index in range(2):
            for p in range(plan.pairs):
                level = far_ref[index, p, BLOCK * b : BLOCK * (b + 1), :].astype(BF)
                d_send[k, index, p] = dot(pick, level).astype(BF)
        copy = pltpu.make_async_remote_copy(
            src_ref=d_send.at[k],
            dst_ref=d_got.at[k],
            send_sem=send_r.at[1, k],
            recv_sem=recv_r.at[1, k],
            device_id=device,
            device_id_type=MESH,
        )
        copy.start()
        d_copies.append(copy)

    d_query_t = dq_t[...].reshape(width, tokens)
    put_all("query", dot_t(norm_t[...], d_query_t), 0, 0)
    for index, (ref, name) in enumerate(((dk_ref, "key"), (dv_ref, "value"))):
        mine = jnp.concatenate([ref[p].astype(BF) for p in range(plan.pairs)], axis=1)
        made = jnp.concatenate([far_ref[index, p].astype(BF) for p in range(plan.pairs)], axis=1)
        put_all(name, dot(norm_t[...], mine) + dot(bar_t[...], made), 0, 0)
        if name == "key":
            step("part_a")
    step("part_b")
    step("down_a", "down_b")
    d_normed = dot_t(turned(d_query_t), wq[...])
    step("part_a", "part_b", "out")

    for copy in d_copies:
        copy.wait_recv()
    i_t = lax.broadcasted_iota(jnp.int32, (tokens, BLOCK), 0)
    i_c = lax.broadcasted_iota(jnp.int32, (tokens, BLOCK), 1)
    last = jnp.where((i_t >> plan.local) == i_c, 0.5**plan.local, 0.0).astype(BF)
    for index, (ref, w) in enumerate(((dk_ref, wk), (dv_ref, wv))):
        pieces = []
        for p in range(plan.pairs):
            coarse = d_got[1, index, p].astype(F32)
            for k in range(2, plan.groups):
                coarse = coarse + d_got[k, index, p].astype(F32)
            pieces.append((ref[p] + two_part_dot(last, coarse)).astype(BF))
        d_normed = d_normed + dot_t(jnp.concatenate(pieces, axis=1), w[...])
    n = n_one[...]
    vec_bufs[0, 0:1, :] = row(d_normed * n)
    vec_bufs[0, 1:2, :] = row(d_normed)
    vec_bufs[0, 5 + per :, :] = jnp.zeros((VEC_ROWS - 5 - per, width), F32)
    d_first = norm_back(d_normed, n, rs_one[...], gain_one[...])
    igg[...] = (d_residual[...] + d_first).astype(BF).reshape(rows, plan.pos, width)

    vec_copies = []

    def vec_start(stage):
        if stage < plan.seq_bits:
            jobs = [(stage, (flip(s, 1 << stage), h))]
        else:
            jobs = [(plan.seq_bits + k - 1, (s, flip(h, k))) for k in range(1, head)]
        for slot, device in jobs:
            copy = pltpu.make_async_remote_copy(
                src_ref=vec_bufs.at[stage],
                dst_ref=vec_got.at[slot],
                send_sem=send_s.at[len(plan.sums), slot],
                recv_sem=recv_s.at[len(plan.sums), slot],
                device_id=device,
                device_id_type=MESH,
            )
            copy.start()
            vec_copies.append(copy)

    def vec_finish(stage):
        vec_copies[stage].wait_recv()
        vec_bufs[stage + 1] = vec_bufs[stage] + vec_got[stage]

    vec_start(0)
    ig_copies = exchange(3, igg, ig_out)
    ig_own = pltpu.make_async_copy(igg.at[j], ig_out.at[j], here.at[9])
    ig_own.start()

    stage = 0
    while stage < plan.seq_bits or not all(item.done for item in sums.values()):
        for name in ("up_a", "up_b", "down_a", "down_b", "part_a", "part_b", "out"):
            if name in sums and not sums[name].done:
                sums[name].step()
        if stage < plan.seq_bits:
            vec_finish(stage)
            vec_start(stage + 1)
        stage += 1
    values = [vec_bufs[plan.seq_bits]]
    for k in range(1, head):
        vec_copies[plan.seq_bits + k - 1].wait_recv()
        values.append(vec_got[plan.seq_bits + k - 1])
    while len(values) > 1:
        values = [values[i] + values[i + 1] for i in range(0, len(values), 2)]
    vec = values[0]

    def own_part(line):
        share = line.shape[1] // seq
        part = line[:, :share]
        for other in range(1, seq):
            part = jnp.where(s == other, line[:, other * share : (other + 1) * share], part)
        return part

    vec_out[...] = jnp.zeros_like(vec_out)
    part = own_part(vec[:8])
    vec_out[:, : part.shape[1]] = part
    part = own_part(jnp.concatenate([vec[5 + i : 6 + i] for i in range(per)], axis=1))
    vec_out[5:6, : part.shape[1]] = part

    for copy in lo_copies + ig_copies:
        copy.wait_recv()
    lo_own.wait()
    ig_own.wait()
    for copy in x_copies + dy_copies + lo_copies + ig_copies + c_copies + d_copies + vec_copies:
        copy.wait_send()
    for item in sums.values():
        item.drain()


def place_kernel(*refs):
    ins, outs, sems = refs[:9], refs[9:-1], refs[-1]
    vec, lines = ins[-1], outs[8:]
    copies = [pltpu.make_async_copy(ins[i], outs[i], sems.at[i]) for i in range(8)]
    for copy in copies:
        copy.start()
    for i, line in enumerate(lines):
        line[...] = vec[i, : line.shape[0]]
    for copy in copies:
        copy.wait()


def body(
    inputs,
    gain_first,
    shift_first,
    query_weight,
    key_weight,
    value_weight,
    out_weight,
    gain_second,
    shift_second,
    up_weight,
    up_bias,
    down_weight,
    down_bias,
    cotangent,
):
    rows, pos, width = inputs.shape
    hidden = up_weight.shape[1]
    plan = Plan(lax.axis_size("seq"), lax.axis_size("head"), rows, pos, width, hidden)
    tokens, pairs, groups, half, near, far = plan.tokens, plan.pairs, plan.groups, plan.half, plan.near, plan.far
    vmem = pl.BlockSpec(memory_space=pltpu.VMEM)
    anywhere = pl.BlockSpec(memory_space=pl.ANY)
    names = list(plan.blocks)

    def buf(*shape, dtype=BF):
        return pltpu.VMEM(shape, dtype)

    scratch = [buf(rows, pos, width)] * 4
    scratch += [buf(width, width)] * 4 + [buf(width, hidden), buf(hidden, width)]
    scratch += [
        buf(width, tokens),
        buf(tokens, width, dtype=F32),
        buf(tokens, 1, dtype=F32),
        buf(tokens, width, dtype=F32),
        buf(tokens, 1, dtype=F32),
        buf(tokens, width),
        buf(tokens, width, dtype=F32),
        buf(tokens, width, dtype=F32),
    ]
    scratch += [
        buf(pairs, 2, tokens, PAIR),
        buf(pairs, 2, near, PAIR),
        buf(pairs, 2, near, PAIR),
        buf(pairs, far, PAIR),
        buf(pairs, far, PAIR),
        buf(pairs, 2, PAIR, near),
        buf(pairs, 2, PAIR, near),
        buf(pairs, PAIR, far),
        buf(pairs, PAIR, far),
    ]
    scratch += [
        buf(pairs, 2, near, tokens, dtype=F32),
        buf(pairs, 2, far, tokens, dtype=F32),
        buf(pairs, 2, 8, tokens, dtype=F32),
        buf(near, tokens, dtype=F32),
        buf(pairs, PAIR, tokens),
    ]
    scratch += [buf(tokens, hidden), buf(tokens, hidden, dtype=F32), buf(tokens, hidden)]
    scratch += [
        buf(pairs, 2, tokens, PAIR),
        buf(pairs, PAIR, tokens),
        buf(pairs, tokens, PAIR, dtype=F32),
        buf(pairs, tokens, PAIR, dtype=F32),
        buf(2, pairs, BLOCK * plan.remote, PAIR, dtype=F32),
        buf(width, BLOCK * plan.remote),
    ]
    scratch += [
        buf(3, BLOCK, width),
        buf(groups, 3, BLOCK, width),
        buf(groups, 2, pairs, BLOCK, PAIR),
        buf(groups, 2, pairs, BLOCK, PAIR),
    ]
    for name in plan.sums:
        scratch += [buf(*(2,) * plan.bits, *plan.sum_shape(name))]
        scratch += [buf(*shape) for shape in plan.got_shapes(name)]
    slots = plan.bits + plan.head
    scratch += [
        buf(plan.seq_bits + 1, VEC_ROWS, width, dtype=F32),
        buf(plan.seq_bits + plan.head - 1, VEC_ROWS, width, dtype=F32),
    ]
    dma = pltpu.SemaphoreType.DMA
    scratch += [dma((4, rows)), dma((4, rows)), dma((2, groups)), dma((2, groups))]
    scratch += [dma((len(plan.sums) + 1, slots)), dma((len(plan.sums) + 1, slots)), dma((10,))]

    line = lambda a: a.reshape(1, -1)
    big = [jax.ShapeDtypeStruct(inputs.shape, BF)] * 2 + [jax.ShapeDtypeStruct(plan.blocks[n], F32) for n in names]
    share = max(width, hidden) // plan.seq
    results = pl.pallas_call(
        functools.partial(layer_kernel, plan),
        out_shape=big + [jax.ShapeDtypeStruct((8, share), F32)],
        in_specs=[anywhere, anywhere] + [vmem] * 6 + [anywhere] * 6,
        out_specs=[anywhere, anywhere] + [vmem] * 7,
        scratch_shapes=scratch,
        compiler_params=pltpu.CompilerParams(
            collective_id=0, has_side_effects=True, vmem_limit_bytes=56 << 20
        ),
        name="layer",
    )(
        inputs,
        cotangent,
        line(gain_first),
        line(shift_first),
        line(gain_second),
        line(shift_second),
        line(up_bias),
        line(down_bias),
        query_weight,
        key_weight,
        value_weight,
        out_weight,
        up_weight,
        down_weight,
    )
    lines = [jax.ShapeDtypeStruct((width // plan.seq,), F32)] * 5 + [jax.ShapeDtypeStruct((hidden // plan.seq,), F32)]
    placed = pl.pallas_call(
        place_kernel,
        out_shape=big + lines,
        in_specs=[anywhere] * 8 + [vmem],
        out_specs=[vmem] * 14,
        scratch_shapes=[dma((8,))],
        name="place",
    )(*results)
    layer_out, input_grad, down_g, up_g, out_g, query_g, key_g, value_g = placed[:8]
    gain_one_g, shift_one_g, gain_two_g, shift_two_g, down_bias_g, up_bias_g = placed[8:]
    return (
        layer_out,
        input_grad,
        gain_one_g,
        shift_one_g,
        query_g,
        key_g,
        value_g,
        out_g,
        gain_two_g,
        shift_two_g,
        up_g,
        up_bias_g,
        down_g,
        down_bias_g,
    )


def solution(mesh):
    placed = (P(None, ("seq", "head"), None),) + (P(),) * 12 + (P(None, ("seq", "head"), None),)
    return jax.shard_map(
        body,
        mesh=mesh,
        in_specs=placed,
        out_specs=(
            P(None, ("seq", "head"), None),
            P(None, ("seq", "head"), None),
            P("seq"),
            P("seq"),
            P("seq", "head"),
            P("seq", "head"),
            P("seq", "head"),
            P("seq", "head"),
            P("seq"),
            P("seq"),
            P("seq", "head"),
            P("seq"),
            P("seq", "head"),
            P("seq"),
        ),
        check_vma=False,
    )
```

```python
import functools

import jax
import jax.numpy as jnp
from jax import lax
from jax.experimental import pallas as pl
from jax.experimental.pallas import tpu as pltpu
from jax.sharding import PartitionSpec as P

MESH = pl.DeviceIdType.MESH
BF = jnp.bfloat16
F32 = jnp.float32
DH = 64
BLOCK = 16
EPSILON = 1e-05
PAIR = 2 * DH
VEC_ROWS = 16
LANES = 128
ORDER = (
    "ffn1a", "dna", "ffn1b", "Abar", "dnb", "dnc", "dna", "ffn2a", "upa", "dnc", "dnb", "ffn2b", "lo", "Alo",
    "upb", "ln2b", "outg", "upa", "dmix", "bar", "upb", "ab0", "ab1", "dnb", "dnc", "outa", "outa", "ab2",
    "ab3", "dna", "dsend", "qkvg", "dnb", "outa", "upb", "dnq", "pa", "pb", "upa", "dnb", "pb", "dnc", "dna",
    "Wd", "ln1b", "vec", "pa", "upb", "dnc", "upa", "Aig", "dna", "vec", "outa", "pb", "outa", "vec", "upb",
    "dnc", "dnb", "upa", "pa", "pb", "vec", "pa", "upa", "vec", "outa", "pa", "pb", "upb",
)
STAGES = {
    "dna": ("straight", "head"),
    "dnb": ("back", "bits"),
    "dnc": ("bits", "straight"),
    "upa": ("straight", "bits"),
    "upb": ("back", "bits"),
    "outa": ("bits", "straight"),
    "pa": ("straight", "head"),
    "pb": ("back", "head"),
}
EIGHTHS = 2


def idiv(value, k):
    return lax.div(value, jnp.int32(k))


def irem(value, k):
    return lax.rem(value, jnp.int32(k))


def bit_of(value, b):
    return irem(idiv(value, 1 << b), 2)


def flip(value, k):
    b = 0
    while k >> b:
        if (k >> b) & 1:
            value = value + (1 - 2 * bit_of(value, b)) * (1 << b)
        b += 1
    return value


def dot(a, b):
    return jnp.dot(a, b, preferred_element_type=F32)


def dot_t(a, b):
    return lax.dot_general(a, b, (((1,), (1,)), ((), ())), preferred_element_type=F32)


def t_dot(a, b):
    return lax.dot_general(a, b, (((0,), (0,)), ((), ())), preferred_element_type=F32)


def two_part_dot(a, b):
    high = b.astype(BF)
    low = (b - high.astype(F32)).astype(BF)
    return dot(a, high) + dot(a, low)


def pair_mean(rows):
    i = lax.broadcasted_iota(jnp.int32, (rows // 2, rows), 0)
    j = lax.broadcasted_iota(jnp.int32, (rows // 2, rows), 1)
    return jnp.where((j >> 1) == i, 0.5, 0.0).astype(BF)


def identity(n):
    i = lax.broadcasted_iota(jnp.int32, (n, n), 0)
    j = lax.broadcasted_iota(jnp.int32, (n, n), 1)
    return jnp.where(i == j, 1.0, 0.0).astype(BF)


def turned(value):
    n = PAIR
    parts = [
        dot_t(identity(n), value[:, i : i + n]).astype(BF) for i in range(0, value.shape[1], n)
    ]
    return parts[0] if len(parts) == 1 else jnp.concatenate(parts, axis=0)


class Plan:
    def __init__(self, seq, head, rows, pos, width, hidden):
        self.seq, self.head, self.rows, self.pos, self.width, self.hidden = seq, head, rows, pos, width, hidden
        self.minor = rows // head
        self.groups = seq // self.minor
        self.tokens = rows * pos
        self.half = self.tokens // 2
        self.pairs = width // PAIR
        self.local = (self.tokens // BLOCK).bit_length() - 1
        self.remote = self.groups.bit_length() - 1
        self.seq_bits = seq.bit_length() - 1
        self.head_bits = head.bit_length() - 1
        self.bits = self.seq_bits + self.head_bits
        self.near = self.half * 2
        self.far = BLOCK * (self.remote - 1)
        cols = width // head
        self.blocks = {
            "down": (hidden // seq, cols),
            "up": (width // seq, hidden // head),
            "out": (width // seq, cols),
            "query": (width // seq, cols),
            "key": (width // seq, cols),
            "value": (width // seq, cols),
        }
        seqs, heads = list(range(self.seq_bits)), list(range(self.seq_bits, self.bits))
        ways = {"core": seqs[:1], "straight": seqs[1:], "back": seqs[:0:-1], "bits": heads, "head": ["head"]}
        stages = {name: [b for way in ("core",) + STAGES[name] for b in ways[way]] for name in STAGES}
        rows_down, rows_up, rows_out = hidden // seq, width // seq, width // seq
        self.fine = rows_down % (2 * LANES) == 0
        half_down = rows_down // 2
        if self.fine:
            self.chunks = [
                [(s * rows_down + i * half_down, half_down) for s in range(seq)] for i in range(2)
            ]
        else:
            self.chunks = [[(0, hidden)], []]

        def tall(name, *cuts):
            return [(name, r, r + n, c, c + LANES) for r, n in cuts for c in range(0, self.blocks[name][1], LANES)]

        if self.fine:
            third = half_down // 8 * EIGHTHS
            step = 2 * half_down
            first = [(c, c + half_down) for c in range(0, hidden // head, step)]
            second = [(c + half_down, c + step) for c in range(0, hidden // head, step)]
            lanes = lambda cs: [("up", 0, rows_up, c, c + LANES) for a, b in cs for c in range(a, b, LANES)]
            self.sums = {
                "dna": (tall("down", (0, half_down - third)), stages["dna"]),
                "dnb": (tall("down", (half_down, half_down - third)), stages["dnb"]),
                "dnc": (
                    tall("down", (half_down - third, third), (2 * half_down - third, third)),
                    stages["dnc"],
                ),
                "upa": (lanes(first), stages["upa"]),
                "upb": (lanes(second), stages["upb"]),
            }
        else:
            self.sums = {
                "dna": (tall("down", (0, rows_down)), stages["dna"]),
                "upb": (tall("up", (0, rows_up)), stages["upb"]),
            }
        self.sums["outa"] = (tall("out", (0, rows_out)), stages["outa"])
        if rows_out % 32 == 0:
            m = rows_out // 2
            self.sums["pa"] = (tall("query", (0, rows_out)) + tall("key", (0, m)), stages["pa"])
            self.sums["pb"] = (tall("key", (m, m)) + tall("value", (0, rows_out)), stages["pb"])
        else:
            self.sums["pa"] = (tall("query", (0, rows_out)) + tall("key", (0, rows_out)), stages["pa"])
            self.sums["pb"] = (tall("value", (0, rows_out)), stages["pb"])

    def sum_shape(self, name):
        return (sum(part[2] - part[1] for part in self.sums[name][0]), LANES)

    def got_shapes(self, name):
        left, shapes = self.bits, []
        for b in self.sums[name][1]:
            if b == "head":
                shapes.append((self.head - 1,) + self.sum_shape(name))
            else:
                left -= 1
                shapes.append((2,) * left + self.sum_shape(name))
        return shapes


class Summed:
    def __init__(self, plan, me, name, number, grad, got, send, recv, outs):
        self.plan, self.name, self.number = plan, name, number
        self.s, self.h = me
        self.grad, self.got, self.outs = grad, got, outs
        self.send, self.recv = send, recv
        self.parts, self.order = plan.sums[name]
        self.started, self.stage = [], 0

    def own_bit(self, b):
        n = self.plan.seq_bits
        return bit_of(self.s, b) if b < n else bit_of(self.h, b - n)

    def index(self, fixed, other=None):
        at = []
        for b in reversed(range(self.plan.bits)):
            if b == other:
                at.append(1 - self.own_bit(b))
            elif b in fixed:
                at.append(self.own_bit(b))
            else:
                at.append(slice(None))
        return tuple(at)

    def put(self, name, s, h, block, row, col):
        owner = s + h * self.plan.seq
        at = tuple((owner >> b) & 1 for b in reversed(range(self.plan.bits)))
        first = 0
        for part, r0, r1, c0, c1 in self.parts:
            if part == name and row <= r0 < row + block.shape[0] and col <= c0 < col + block.shape[1]:
                piece = block[r0 - row : r1 - row, c0 - col : c1 - col]
                self.grad[at + (slice(first, first + r1 - r0),)] = piece.astype(BF)
            first += r1 - r0

    def copy(self, source, target, slot, device):
        copy = pltpu.make_async_remote_copy(
            src_ref=source,
            dst_ref=target,
            send_sem=self.send.at[self.number, slot],
            recv_sem=self.recv.at[self.number, slot],
            device_id=device,
            device_id_type=MESH,
        )
        copy.start()
        self.started.append(copy)

    def start(self, stage):
        b = self.order[stage]
        n = self.plan.seq_bits
        if b == "head":
            for k in range(1, self.plan.head):
                peer = flip(self.h, k)
                at = tuple(bit_of(peer, i) for i in reversed(range(self.plan.head_bits)))
                at += self.index(range(n))[self.plan.head_bits :]
                self.copy(self.grad.at[at], self.got[stage].at[k - 1], stage + k - 1, (self.s, peer))
            return
        device = (flip(self.s, 1 << b), self.h) if b < n else (self.s, flip(self.h, 1 << (b - n)))
        source = self.grad.at[self.index(self.order[:stage], b)]
        self.copy(source, self.got[stage], stage, device)

    def finish(self, stage):
        b = self.order[stage]
        if stage + 1 == len(self.order):
            total = self.grad[self.index(range(self.plan.bits))].astype(F32)
            if b == "head":
                for k in range(1, self.plan.head):
                    self.started[stage + k - 1].wait_recv()
                    total = total + self.got[stage][k - 1].astype(F32)
            else:
                self.started[stage].wait_recv()
                total = total + self.got[stage][...].astype(F32)
            first = 0
            for part, r0, r1, c0, c1 in self.parts:
                self.outs[part][r0:r1, c0:c1] = total[first : first + r1 - r0]
                first += r1 - r0
            return
        self.started[stage].wait_recv()
        at = self.index(self.order[: stage + 1])
        combos = [()]
        for a in at:
            if isinstance(a, slice):
                combos = [c + (i,) for c in combos for i in range(2)]
        for combo in combos:
            left = list(combo)
            full = tuple(left.pop(0) if isinstance(a, slice) else a for a in at)
            self.grad[full] = self.grad[full] + self.got[stage][combo]

    def step(self):
        if self.stage:
            self.finish(self.stage - 1)
        if self.stage < len(self.order):
            self.start(self.stage)
        self.stage += 1

    @property
    def done(self):
        return self.stage > len(self.order)

    def drain(self):
        for copy in self.started:
            copy.wait_send()


def layer_kernel(plan, *refs):
    refs = list(refs)

    def take(n):
        taken = refs[:n]
        del refs[:n]
        return taken

    x_in, dy_in, *lines_in = take(8)
    weights_in = take(6)
    lo_out, ig_out = take(2)
    grads_out = dict(zip(plan.blocks, take(6)))
    lines_out = take(6)
    xg, dyg, log, igg = take(4)
    wq, wk, wv, wo, wu, wd = weights = take(6)
    gain_one, shift_one, gain_two, shift_two, up_bias, down_bias = lines = take(6)
    norm_t, n_one, rs_one, n_two, rs_two, norm_two_b, residual, d_residual = take(8)
    qs, kn, vn, kr, vr, kn_t, vn_t, kr_t, vr_t = take(9)
    pn, pr, stats, mask, mixed_t = take(5)
    act_ref, hid_ref, cdf_ref, dh_ref = take(4)
    dos, dq_t, dk_ref, dv_ref, far_ref, bar_t, d_norm_one = take(7)
    c_send, c_got, c_half, c_half_got, bar_send, bar_got, d_send, d_got = take(8)
    sums = {}
    for name in plan.sums:
        grad, *got = take(1 + len(plan.sums[name][1]))
        sums[name] = (grad, got)
    vec_bufs, vec_got, vec_own, vec_own_got = take(4)
    send_a, recv_a, send_r, recv_r, send_s, recv_s, here = take(7)
    assert not refs

    seq, head, rows, width, tokens = plan.seq, plan.head, plan.rows, plan.width, plan.tokens
    half, near, far = plan.half, plan.near, plan.far
    s, h = lax.axis_index("seq"), lax.axis_index("head")
    c, g = irem(s, plan.minor), idiv(s, plan.minor)
    j = c * head + h

    def group_peer(k):
        other = flip(j, k)
        return other, (g * plan.minor + idiv(other, head), irem(other, head))

    def row_peer(k):
        other = flip(g, k)
        return other, (other * plan.minor + c, h)

    barrier = pltpu.get_barrier_semaphore()
    peers = [group_peer(k)[1] for k in range(1, rows)] + [row_peer(k)[1] for k in range(1, plan.groups)]
    for device in peers:
        pl.semaphore_signal(barrier, inc=1, device_id=device, device_id_type=MESH)

    small = [pltpu.make_async_copy(a, b, here.at[10 + i]) for i, (a, b) in enumerate(zip(lines_in, lines))]
    for copy in small:
        copy.start()
    loads = [pltpu.make_async_copy(a, b, here.at[i]) for i, (a, b) in enumerate(zip(weights_in, weights))]
    for i in (1, 2, 0, 3, 4, 5):
        loads[i].start()
    own = [
        pltpu.make_async_copy(x_in.at[j], xg.at[j], here.at[6]),
        pltpu.make_async_copy(dy_in.at[j], dyg.at[j], here.at[7]),
    ]
    for copy in own:
        copy.start()

    i_k = lax.broadcasted_iota(jnp.int32, (near, 2 * half), 0)
    i_q = lax.broadcasted_iota(jnp.int32, (near, 2 * half), 1) & (half - 1)
    valid = (i_k < half) & ((i_q >> 5) == (i_k >> 5))
    first = half
    for level in range(1, plan.local - 1):
        count = half >> level
        mine = (i_k >= first) & (i_k < first + count)
        valid = valid | (mine & (((i_q >> (4 + level)) ^ 1) == ((i_k - first) >> 4)))
        first += count
    valid = valid | (i_k >= first)
    mask[...] = jnp.where(valid, 0.0, -1e30).astype(F32)

    pl.semaphore_wait(barrier, len(peers))

    def exchange(number, source, target):
        copies = []
        for k in sorted(range(1, rows), key=lambda k: -(k % head)):
            other, device = group_peer(k)
            copy = pltpu.make_async_remote_copy(
                src_ref=source.at[other],
                dst_ref=target.at[j],
                send_sem=send_a.at[number, k],
                recv_sem=recv_a.at[number, k],
                device_id=device,
                device_id_type=MESH,
            )
            copy.start()
            copies.append(copy)
        return copies

    x_copies = exchange(0, x_in, xg)

    def norm_stats(values):
        center = values - jnp.mean(values, axis=-1, keepdims=True)
        spread = jnp.mean(center * center, axis=-1, keepdims=True)
        scale = lax.rsqrt(spread + EPSILON)
        return center * scale, scale

    def norm_back(d_norm, n, scale, gain):
        weighted = d_norm * gain
        return scale * (
            weighted
            - jnp.mean(weighted, axis=-1, keepdims=True)
            - n * jnp.mean(weighted * n, axis=-1, keepdims=True)
        )

    lane = lax.broadcasted_iota(jnp.int32, (1, PAIR), 1)
    low = lane < DH

    def stack_heads(ref, value):
        for p in range(plan.pairs):
            for a in range(2):
                part = value[a * half : (a + 1) * half, p * PAIR : (p + 1) * PAIR]
                zero = jnp.zeros_like(part)
                ref[p, a, :half, :] = jnp.where(low, part, zero)
                ref[p, a, half:, :] = jnp.where(low, zero, part)

    for copy in small:
        copy.wait()
    own[0].wait()
    for copy in x_copies:
        copy.wait_recv()
    dy_copies = exchange(1, dy_in, dyg)
    x = xg[...].reshape(tokens, width).astype(F32)
    n, scale = norm_stats(x)
    n_one[...] = n
    rs_one[...] = scale
    normed = (n * gain_one[...] + shift_one[...]).astype(BF)

    loads[1].wait()
    loads[2].wait()
    level = jnp.concatenate([dot(normed, wk[...]).astype(BF), dot(normed, wv[...]).astype(BF)], axis=1)

    def columns(index, p):
        return slice(index * width + p * PAIR, index * width + (p + 1) * PAIR)

    targets = (kn, vn)
    first = 0
    for l in range(plan.local):
        if l:
            level = dot(pair_mean(level.shape[0]), level).astype(BF)
        count = level.shape[0] // 2
        for index, ref in enumerate(targets):
            for p in range(plan.pairs):
                for a in range(2):
                    b = a if l + 1 < plan.local else 1 - a
                    ref[p, b, first : first + count, :] = level[a * count : (a + 1) * count, columns(index, p)]
        first += count
    level = dot(pair_mean(level.shape[0]), level).astype(BF)
    c_send[0] = level[:, :width]
    c_send[1] = level[:, width:]
    level = dot(pair_mean(level.shape[0]), level).astype(BF)
    c_half[: BLOCK // 2, :] = level[:, :width]
    c_half[BLOCK // 2 :, :] = level[:, width:]
    c_copies = []
    for k in range(1, plan.groups):
        other, device = row_peer(k)
        copy = pltpu.make_async_remote_copy(
            src_ref=c_send if k == 1 else c_half,
            dst_ref=c_got if k == 1 else c_half_got.at[g],
            send_sem=send_r.at[0, k],
            recv_sem=recv_r.at[0, k],
            device_id=device,
            device_id_type=MESH,
        )
        copy.start()
        c_copies.append(copy)

    loads[0].wait()
    stack_heads(qs, (dot(normed, wq[...]) * (DH**-0.5)).astype(BF))
    norm_t[...] = turned(normed)
    local = near - BLOCK

    def attend_near(p, carry):
        for a in range(2):
            scores = dot_t(kn[p, a, :local, :], qs[p, a]) + mask[:local, :]
            top = jnp.max(scores, axis=0, keepdims=True)
            raised = jnp.exp(scores - top)
            pn[p, a, :local, :] = raised
            stats[p, a, 0:1, :] = top
            stats[p, a, 1:2, :] = jnp.sum(raised, axis=0, keepdims=True)
            kn_t[p, a, :, :local] = turned(kn[p, a, :local, :])
            vn_t[p, a, :, :local] = turned(vn[p, a, :local, :])
        return carry

    for p in range(plan.pairs):
        attend_near(p, 0)

    for copy in c_copies:
        copy.wait_recv()

    def sibling(b):
        upper = idiv(g, 1 << b)
        return (upper + 1 - 2 * irem(upper, 2)) * (1 << b)

    for b in range(plan.remote):
        for index in range(2):
            if b == 0:
                level = c_got[index]
            else:
                count = 1 << b
                both_kinds = c_half_got[pl.ds(sibling(b), count)].reshape(BLOCK * count, width)
                i_r = lax.broadcasted_iota(jnp.int32, (BLOCK * count // 2, BLOCK * count), 0)
                i_s = lax.broadcasted_iota(jnp.int32, (BLOCK * count // 2, BLOCK * count), 1)
                own_rows = (i_r >> 3) * BLOCK + index * (BLOCK // 2) + (i_r & 7) == i_s
                level = dot(jnp.where(own_rows, 1.0, 0.0).astype(BF), both_kinds).astype(BF)
                for _ in range(b - 1):
                    level = dot(pair_mean(level.shape[0]), level).astype(BF)
            for p in range(plan.pairs):
                part = level[:, p * PAIR : (p + 1) * PAIR]
                if b == 0:
                    for a in range(2):
                        targets[index][p, a, local:, :] = part
                else:
                    (kr, vr)[index][p, (b - 1) * BLOCK : b * BLOCK, :] = part

    def attend(p, carry):
        kr_t[p] = turned(kr[p])
        vr_t[p] = turned(vr[p])
        for a in range(2):
            kn_t[p, a, :, local:] = turned(kn[p, a, local:, :])
            vn_t[p, a, :, local:] = turned(vn[p, a, local:, :])
            q = qs[p, a]
            top_near = stats[p, a, 0:1, :]
            first_far = dot_t(kn[p, a, local:, :], q)
            rest_far = dot_t(kr[p], q)
            top = jnp.maximum(
                top_near,
                jnp.maximum(
                    jnp.max(first_far, axis=0, keepdims=True), jnp.max(rest_far, axis=0, keepdims=True)
                ),
            )
            shrink = jnp.exp(top_near - top)
            first_far = jnp.exp(first_far - top)
            rest_far = jnp.exp(rest_far - top)
            total = (
                stats[p, a, 1:2, :] * shrink
                + jnp.sum(first_far, axis=0, keepdims=True)
                + jnp.sum(rest_far, axis=0, keepdims=True)
            )
            share = 1.0 / total
            pn[p, a, :local, :] = pn[p, a, :local, :] * (shrink * share)
            pn[p, a, local:, :] = first_far * share
            rest_far = rest_far * share
            pr[p, a] = rest_far
            mixed = dot(vn_t[p, a], pn[p, a].astype(BF)) + dot(vr_t[p], rest_far.astype(BF))
            mixed_t[p, :DH, a * half : (a + 1) * half] = mixed[:DH, :half].astype(BF)
            mixed_t[p, DH:, a * half : (a + 1) * half] = mixed[DH:, half:].astype(BF)
        return carry

    for p in range(plan.pairs):
        attend(p, 0)

    loads[3].wait()
    res = xg[...].reshape(tokens, width).astype(F32) + t_dot(mixed_t[...].reshape(width, tokens), wo[...])
    residual[...] = res
    n, scale = norm_stats(res)
    n_two[...] = n
    rs_two[...] = scale
    norm_two_b[...] = (n * gain_two[...] + shift_two[...]).astype(BF)

    row = lambda a: jnp.sum(a, axis=0, keepdims=True)
    per = plan.hidden // width

    def put_block(name, block, first_row, first_col):
        r, w = plan.blocks[name]
        row_step, col_step = min(r, block.shape[0]), min(w, block.shape[1])
        for a in range(0, block.shape[0], row_step):
            for b in range(0, block.shape[1], col_step):
                s_at, h_at = (first_row + a) // r, (first_col + b) // w
                piece = block[a : a + row_step, b : b + col_step]
                for item in items.values():
                    if item is not vec_sum:
                        item.put(name, s_at, h_at, piece, (first_row + a) % r, (first_col + b) % w)

    class Vectors:
        def __init__(self):
            self.stage, self.started = 0, []

        def copy(self, source, target, slot, device):
            copy = pltpu.make_async_remote_copy(
                src_ref=source,
                dst_ref=target,
                send_sem=send_s.at[len(plan.sums), slot],
                recv_sem=recv_s.at[len(plan.sums), slot],
                device_id=device,
                device_id_type=MESH,
            )
            copy.start()
            self.started.append(copy)

        def step(self):
            n, k = plan.seq_bits, self.stage
            if 0 < k <= n:
                self.started[k - 1].wait_recv()
                vec_bufs[k] = vec_bufs[k - 1] + vec_got[k - 1]
            if k < n:
                self.copy(vec_bufs.at[k], vec_got.at[k], k, (flip(s, 1 << k), h))
            elif k == n:
                vec = vec_bufs[n]
                part = own_part(vec[:8])
                vec_own[:, : part.shape[1]] = part
                part = own_part(jnp.concatenate([vec[5 + i : 6 + i] for i in range(per)], axis=1))
                vec_own[5:6, : part.shape[1]] = part
                for i in range(1, head):
                    self.copy(vec_own, vec_own_got.at[i - 1], n + i - 1, (s, flip(h, i)))
            else:
                values = [vec_own[...]]
                for i in range(1, head):
                    self.started[n + i - 1].wait_recv()
                    values.append(vec_own_got[i - 1])
                while len(values) > 1:
                    values = [values[i] + values[i + 1] for i in range(0, len(values), 2)]
                for i, line in enumerate(lines_out):
                    line[...] = values[0][i, : line.shape[0]]
            self.stage += 1

        @property
        def done(self):
            return self.stage > plan.seq_bits + 1

        def drain(self):
            for copy in self.started:
                copy.wait_send()

    def own_part(line):
        share = line.shape[1] // seq
        part = line[:, :share]
        for other in range(1, seq):
            part = jnp.where(s == other, line[:, other * share : (other + 1) * share], part)
        return part

    vec_sum = Vectors()
    items = {
        name: Summed(plan, (s, h), name, i, grad, got, send_s, recv_s, grads_out)
        for i, (name, (grad, got)) in enumerate(sums.items())
    }
    items["vec"] = vec_sum

    def cotangent():
        return dyg[...].reshape(tokens, width)

    def blocks_of(chunk):
        at, blocks = 0, []
        for start, length in plan.chunks[chunk]:
            for f in range(start, start + length, 512):
                n = min(512, start + length - f)
                if not blocks or blocks[-1][1] + n > 512:
                    blocks.append([[], 0, at])
                blocks[-1][0].append((f, n))
                blocks[-1][1] += n
                at += n
        return [(segments, slice(first, first + n)) for segments, n, first in blocks]

    def columns_of(ref, segments):
        return jnp.concatenate([ref[:, f : f + n] for f, n in segments], axis=1)

    def rows_of(ref, segments):
        return jnp.concatenate([ref[f : f + n, :] for f, n in segments], axis=0)

    def activate(chunk):
        if chunk == 0:
            loads[4].wait()
            loads[5].wait()
            own[1].wait()
            for copy in dy_copies:
                copy.wait_recv()
        for segments, at in blocks_of(chunk):
            hid = dot(norm_two_b[...], columns_of(wu, segments)) + columns_of(up_bias, segments)
            cdf = 0.5 * (1.0 + lax.erf(hid * (0.5**0.5)))
            act = (hid * cdf).astype(BF)
            act_ref[chunk, :, at] = act
            hid_ref[chunk, :, at] = hid
            cdf_ref[chunk, :, at] = cdf
            grad = t_dot(act, cotangent())
            first = 0
            for f, n in segments:
                put_block("down", grad[first : first + n], f, 0)
                first += n

    def deactivate(chunk):
        for segments, at in blocks_of(chunk):
            hid = hid_ref[chunk, :, at]
            slope = cdf_ref[chunk, :, at] + hid * (jnp.exp(-0.5 * hid * hid) * 0.3989422804014327)
            dh = (dot_t(cotangent(), rows_of(wd, segments)) * slope).astype(BF)
            dh_ref[chunk, :, at] = dh
            sums_dh = row(dh.astype(F32))
            grad = t_dot(norm_two_b[...], dh)
            first = 0
            for f, n in segments:
                for o in range(0, n, min(n, width)):
                    line, lane_at = divmod(f + o, width)
                    m = min(n, width)
                    vec_bufs[0, 5 + line : 6 + line, lane_at : lane_at + m] = sums_dh[:, first + o : first + o + m]
                put_block("up", grad[:, first : first + n], 0, f)
                first += n

    def both(ref, weight, product, pick):
        total = None
        for chunk in range(2):
            for segments, at in blocks_of(chunk):
                term = product(ref[chunk, :, at], pick(weight, segments))
                total = term if total is None else total + term
        return total

    def second_norm_back():
        d_norm_two = both(dh_ref, wu, dot_t, columns_of)
        n = n_two[...]
        dy_f = cotangent().astype(F32)
        vec_bufs[0, 2:3, :] = row(d_norm_two * n)
        vec_bufs[0, 3:4, :] = row(d_norm_two)
        vec_bufs[0, 4:5, :] = row(dy_f)
        d_residual[...] = dy_f + norm_back(d_norm_two, n, rs_two[...], gain_two[...])

    def out_grad():
        put_block("out", dot(mixed_t[...].reshape(width, tokens), d_residual[...].astype(BF)), 0, 0)

    def mixed_back():
        stack_heads(dos, dot_t(d_residual[...].astype(BF), wo[...]).astype(BF))

    def layer_output():
        result = residual[...] + both(act_ref, wd, dot, rows_of) + down_bias[...]
        log[...] = result.astype(BF).reshape(rows, plan.pos, width)

    late_copies, own_late = [], []

    def send_layer_output():
        late_copies.extend(exchange(2, log, lo_out))
        own_late.append(pltpu.make_async_copy(log.at[j], lo_out.at[j], here.at[8]))
        own_late[-1].start()

    spread_to = half + sum(half >> level for level in range(1, plan.local))

    def spread_matrix():
        i_t = lax.broadcasted_iota(jnp.int32, (half, half), 0)
        i_c = lax.broadcasted_iota(jnp.int32, (half, half), 1)
        spread = jnp.zeros((half, half), F32)
        first = 0
        for level in range(1, plan.local):
            spread = spread + jnp.where((i_t >> level) == (i_c - first), 0.5**level, 0.0)
            first += half >> level
        return jnp.where(i_c < first, spread, 0.0).astype(BF)

    def attend_back(p):
        spread = spread_matrix()
        dk, dv, dk_far, dv_far = [], [], 0.0, 0.0
        for a in range(2):
            q, do = qs[p, a], dos[p, a]
            prob, prob_far = pn[p, a], pr[p, a]
            d_prob = dot_t(vn[p, a], do)
            d_prob_far = dot_t(vr[p], do)
            inner = row(prob * d_prob) + row(prob_far * d_prob_far)
            d_scores = (prob * (d_prob - inner)).astype(BF)
            d_scores_far = (prob_far * (d_prob_far - inner)).astype(BF)
            dk.append(dot(d_scores, q))
            dv.append(dot(prob.astype(BF), do))
            dk_far = dk_far + dot(d_scores_far, q)
            dv_far = dv_far + dot(prob_far.astype(BF), do)
            dq = (dot(kn_t[p, a], d_scores) + dot(kr_t[p], d_scores_far)) * (DH**-0.5)
            dq_t[p, :DH, a * half : (a + 1) * half] = dq[:DH, :half].astype(BF)
            dq_t[p, DH:, a * half : (a + 1) * half] = dq[DH:, half:].astype(BF)
        other = spread_to - BLOCK
        for index, (total, total_far, ref) in enumerate(((dk, dk_far, dk_ref), (dv, dv_far, dv_ref))):
            for a in range(2):
                coarse = jnp.concatenate(
                    [total[a][half:other], total[1 - a][other : other + BLOCK], total[a][local:]], axis=0
                )
                ref[p, a * half : (a + 1) * half, :] = total[a][:half] + two_part_dot(spread, coarse)
            far_ref[index, p, :BLOCK, :] = total[0][local:] + total[1][local:]
            far_ref[index, p, BLOCK:, :] = total_far

    d_copies = []

    def send_far():
        i_a = lax.broadcasted_iota(jnp.int32, (BLOCK, BLOCK), 0)
        i_b = lax.broadcasted_iota(jnp.int32, (BLOCK, BLOCK), 1)
        for k in range(1, plan.groups):
            other, device = row_peer(k)
            b = k.bit_length() - 1
            offset = irem(other, 1 << b)
            pick = jnp.where(((offset * BLOCK + i_a) >> b) == i_b, 0.5**b, 0.0).astype(BF)
            for index in range(2):
                for p in range(plan.pairs):
                    level = far_ref[index, p, BLOCK * b : BLOCK * (b + 1), :].astype(BF)
                    d_send[k, index, p] = dot(pick, level).astype(BF)
            copy = pltpu.make_async_remote_copy(
                src_ref=d_send.at[k],
                dst_ref=d_got.at[k],
                send_sem=send_r.at[1, k],
                recv_sem=recv_r.at[1, k],
                device_id=device,
                device_id_type=MESH,
            )
            copy.start()
            d_copies.append(copy)

    def part_grads():
        put_block("query", dot_t(norm_t[...], dq_t[...].reshape(width, tokens)), 0, 0)
        for index, (ref, name) in enumerate(((dk_ref, "key"), (dv_ref, "value"))):
            mine = jnp.concatenate([ref[p].astype(BF) for p in range(plan.pairs)], axis=1)
            made = jnp.concatenate([far_ref[index, p].astype(BF) for p in range(plan.pairs)], axis=1)
            put_block(name, dot(norm_t[...], mine) + dot(bar_t[...], made), 0, 0)

    bar_copies = []

    def send_bars():
        i_a = lax.broadcasted_iota(jnp.int32, (BLOCK, tokens), 0)
        i_b = lax.broadcasted_iota(jnp.int32, (BLOCK, tokens), 1)
        mean_all = jnp.where((i_b >> plan.local) == i_a, 0.5**plan.local, 0.0).astype(BF)
        bar_send[...] = dot_t(mean_all, norm_t[...]).astype(BF)
        for k in range(1, plan.groups):
            other, device = row_peer(k)
            copy = pltpu.make_async_remote_copy(
                src_ref=bar_send,
                dst_ref=bar_got.at[g],
                send_sem=send_r.at[2, k],
                recv_sem=recv_r.at[2, k],
                device_id=device,
                device_id_type=MESH,
            )
            copy.start()
            bar_copies.append(copy)

    def take_bars():
        for copy in bar_copies:
            copy.wait_recv()
        for b in range(plan.remote):
            level = bar_got[pl.ds(sibling(b), 1 << b)].reshape(BLOCK << b, width)
            for _ in range(b):
                level = dot(pair_mean(level.shape[0]), level).astype(BF)
            bar_t[:, b * BLOCK : (b + 1) * BLOCK] = turned(level)

    def query_back():
        d_norm_one[...] = dot_t(turned(dq_t[...].reshape(width, tokens)), wq[...])

    def take_far():
        for copy in d_copies:
            copy.wait_recv()

    def first_norm_back():
        i_t = lax.broadcasted_iota(jnp.int32, (tokens, BLOCK), 0)
        i_c = lax.broadcasted_iota(jnp.int32, (tokens, BLOCK), 1)
        last = jnp.where((i_t >> plan.local) == i_c, 0.5**plan.local, 0.0).astype(BF)
        d_normed = d_norm_one[...]
        for index, (ref, w) in enumerate(((dk_ref, wk), (dv_ref, wv))):
            pieces = []
            for p in range(plan.pairs):
                coarse = d_got[1, index, p].astype(F32)
                for k in range(2, plan.groups):
                    coarse = coarse + d_got[k, index, p].astype(F32)
                pieces.append((ref[p] + two_part_dot(last, coarse)).astype(BF))
            d_normed = d_normed + dot_t(jnp.concatenate(pieces, axis=1), w[...])
        n = n_one[...]
        vec_bufs[0, 0:1, :] = row(d_normed * n)
        vec_bufs[0, 1:2, :] = row(d_normed)
        vec_bufs[0, 5 + per :, :] = jnp.zeros((VEC_ROWS - 5 - per, width), F32)
        d_first = norm_back(d_normed, n, rs_one[...], gain_one[...])
        igg[...] = (d_residual[...] + d_first).astype(BF).reshape(rows, plan.pos, width)

    def send_input_grad():
        late_copies.extend(exchange(3, igg, ig_out))
        own_late.append(pltpu.make_async_copy(igg.at[j], ig_out.at[j], here.at[9]))
        own_late[-1].start()

    vec_own[...] = jnp.zeros_like(vec_own)
    work = {
        "ffn1a": lambda: activate(0),
        "ffn1b": lambda: activate(1),
        "ffn2a": lambda: deactivate(0),
        "ffn2b": lambda: deactivate(1),
        "ln2b": second_norm_back,
        "outg": out_grad,
        "lo": layer_output,
        "Alo": send_layer_output,
        "dmix": mixed_back,
        "Abar": send_bars,
        "bar": take_bars,
        "dsend": send_far,
        "qkvg": part_grads,
        "dnq": query_back,
        "Wd": take_far,
        "ln1b": first_norm_back,
        "Aig": send_input_grad,
    }
    first_pairs = {f"ab{i}": range(i, plan.pairs, 4) for i in range(4)}
    for name in ORDER:
        if name in work:
            work[name]()
        elif name in first_pairs:
            for p in first_pairs[name]:
                attend_back(p)
        elif name in items:
            items[name].step()
    while not all(item.done for item in items.values()):
        for item in items.values():
            if not item.done:
                item.step()

    for copy in late_copies:
        copy.wait_recv()
    for copy in own_late:
        copy.wait()
    for copy in x_copies + dy_copies + c_copies + bar_copies + d_copies + late_copies:
        copy.wait_send()
    for item in items.values():
        item.drain()


def place_kernel(*refs):
    count = len(refs) // 2
    ins, outs, sems = refs[:count], refs[count:-1], refs[-1]
    copies = [pltpu.make_async_copy(a, b, sems.at[i]) for i, (a, b) in enumerate(zip(ins, outs))]
    for copy in copies:
        copy.start()
    for copy in copies:
        copy.wait()


def body(
    inputs,
    gain_first,
    shift_first,
    query_weight,
    key_weight,
    value_weight,
    out_weight,
    gain_second,
    shift_second,
    up_weight,
    up_bias,
    down_weight,
    down_bias,
    cotangent,
):
    rows, pos, width = inputs.shape
    hidden = up_weight.shape[1]
    plan = Plan(lax.axis_size("seq"), lax.axis_size("head"), rows, pos, width, hidden)
    tokens, pairs, groups, half, near, far = plan.tokens, plan.pairs, plan.groups, plan.half, plan.near, plan.far
    vmem = pl.BlockSpec(memory_space=pltpu.VMEM)
    anywhere = pl.BlockSpec(memory_space=pl.ANY)
    names = list(plan.blocks)

    def buf(*shape, dtype=BF):
        return pltpu.VMEM(shape, dtype)

    scratch = [buf(rows, pos, width)] * 4
    scratch += [buf(width, width)] * 4 + [buf(width, hidden), buf(hidden, width)]
    scratch += [buf(1, n, dtype=F32) for n in (width, width, width, width, hidden, width)]
    scratch += [
        buf(width, tokens),
        buf(tokens, width, dtype=F32),
        buf(tokens, 1, dtype=F32),
        buf(tokens, width, dtype=F32),
        buf(tokens, 1, dtype=F32),
        buf(tokens, width),
        buf(tokens, width, dtype=F32),
        buf(tokens, width, dtype=F32),
    ]
    scratch += [
        buf(pairs, 2, tokens, PAIR),
        buf(pairs, 2, near, PAIR),
        buf(pairs, 2, near, PAIR),
        buf(pairs, far, PAIR),
        buf(pairs, far, PAIR),
        buf(pairs, 2, PAIR, near),
        buf(pairs, 2, PAIR, near),
        buf(pairs, PAIR, far),
        buf(pairs, PAIR, far),
    ]
    scratch += [
        buf(pairs, 2, near, tokens, dtype=F32),
        buf(pairs, 2, far, tokens, dtype=F32),
        buf(pairs, 2, 8, tokens, dtype=F32),
        buf(near, tokens, dtype=F32),
        buf(pairs, PAIR, tokens),
    ]
    part = sum(n for _, n in plan.chunks[0])
    scratch += [buf(2, tokens, part)] + [buf(2, tokens, part, dtype=F32)] * 2 + [buf(2, tokens, part)]
    scratch += [
        buf(pairs, 2, tokens, PAIR),
        buf(pairs, PAIR, tokens),
        buf(pairs, tokens, PAIR, dtype=F32),
        buf(pairs, tokens, PAIR, dtype=F32),
        buf(2, pairs, BLOCK * plan.remote, PAIR, dtype=F32),
        buf(width, BLOCK * plan.remote),
        buf(tokens, width, dtype=F32),
    ]
    scratch += [
        buf(2, BLOCK, width),
        buf(2, BLOCK, width),
        buf(BLOCK, width),
        buf(groups, BLOCK, width),
        buf(BLOCK, width),
        buf(groups, BLOCK, width),
        buf(groups, 2, pairs, BLOCK, PAIR),
        buf(groups, 2, pairs, BLOCK, PAIR),
    ]
    for name in plan.sums:
        scratch += [buf(*(2,) * plan.bits, *plan.sum_shape(name))]
        scratch += [buf(*shape) for shape in plan.got_shapes(name)]
    slots = plan.bits + plan.head
    share = max(width, hidden) // plan.seq
    scratch += [
        buf(plan.seq_bits + 1, VEC_ROWS, width, dtype=F32),
        buf(plan.seq_bits, VEC_ROWS, width, dtype=F32),
        buf(8, share, dtype=F32),
        buf(plan.head - 1, 8, share, dtype=F32),
    ]
    dma = pltpu.SemaphoreType.DMA
    scratch += [dma((4, rows)), dma((4, rows)), dma((3, groups)), dma((3, groups))]
    scratch += [dma((len(plan.sums) + 1, slots)), dma((len(plan.sums) + 1, slots)), dma((16,))]

    line = lambda a: a.reshape(1, -1)
    big = [jax.ShapeDtypeStruct(inputs.shape, BF)] * 2 + [jax.ShapeDtypeStruct(plan.blocks[n], F32) for n in names]
    lines = [jax.ShapeDtypeStruct((width // plan.seq,), F32)] * 5 + [jax.ShapeDtypeStruct((hidden // plan.seq,), F32)]
    results = pl.pallas_call(
        functools.partial(layer_kernel, plan),
        out_shape=[pltpu.VMEM(o.shape, o.dtype) for o in big + lines],
        in_specs=[anywhere] * 14,
        out_specs=[vmem] * 14,
        scratch_shapes=scratch,
        compiler_params=pltpu.CompilerParams(
            collective_id=0, has_side_effects=True, vmem_limit_bytes=56 << 20
        ),
        name="layer",
    )(
        inputs,
        cotangent,
        line(gain_first),
        line(shift_first),
        line(gain_second),
        line(shift_second),
        line(up_bias),
        line(down_bias),
        query_weight,
        key_weight,
        value_weight,
        out_weight,
        up_weight,
        down_weight,
    )
    placed = pl.pallas_call(
        place_kernel,
        out_shape=big + lines,
        in_specs=[vmem] * 14,
        out_specs=[anywhere] * 14,
        scratch_shapes=[dma((14,))],
        name="place",
    )(*[pltpu.with_memory_space_constraint(r, pltpu.VMEM) for r in results])
    layer_out, input_grad, down_g, up_g, out_g, query_g, key_g, value_g = placed[:8]
    gain_one_g, shift_one_g, gain_two_g, shift_two_g, down_bias_g, up_bias_g = placed[8:]
    return (
        layer_out,
        input_grad,
        gain_one_g,
        shift_one_g,
        query_g,
        key_g,
        value_g,
        out_g,
        gain_two_g,
        shift_two_g,
        up_g,
        up_bias_g,
        down_g,
        down_bias_g,
    )


def solution(mesh):
    placed = (P(None, ("seq", "head"), None),) + (P(),) * 12 + (P(None, ("seq", "head"), None),)
    return jax.shard_map(
        body,
        mesh=mesh,
        in_specs=placed,
        out_specs=(
            P(None, ("seq", "head"), None),
            P(None, ("seq", "head"), None),
            P("seq"),
            P("seq"),
            P("seq", "head"),
            P("seq", "head"),
            P("seq", "head"),
            P("seq", "head"),
            P("seq"),
            P("seq"),
            P("seq", "head"),
            P("seq"),
            P("seq", "head"),
            P("seq"),
        ),
        check_vma=False,
    )
```

```python
import functools

import jax
import jax.numpy as jnp
from jax import lax
from jax.experimental import pallas as pl
from jax.experimental.pallas import tpu as pltpu
from jax.sharding import PartitionSpec as P

MESH = pl.DeviceIdType.MESH
BF = jnp.bfloat16
F32 = jnp.float32
DH = 64
BLOCK = 16
EPSILON = 1e-05
PAIR = 2 * DH
LANES = 128
ORDER = (
    "f10", "f13", "f11", "g10", "g11", "dnc", "f12", "g12", "g13", "dnb", "f21", "dnc", "Abar", "dna", "f20",
    "dnb", "dna", "upa", "f23", "f22", "lo", "upb", "upa", "Alo", "ln2b", "dmix", "outg", "ab3", "upb",
    "outa", "ab0", "outa", "ab2", "ab1", "dnc", "dnb", "bar", "dnq", "qkvg", "dsend", "pb", "pb", "pa", "upa",
    "pa", "outa", "upb", "dnb", "Wd", "ln1b", "vec", "Aig", "dnb", "upa", "vec", "dna", "pb", "upb", "outa",
    "pa", "dnc", "vec", "pb", "dna", "pa", "vec", "upa", "pb", "outa", "dna", "dnb", "dnc", "upb", "pa",
    "dna", "dnc", "pb", "upa", "vec", "outa", "pa",
)
STAGES = {
    "dna": ("straight", "bits"),
    "dnb": ("back", "bits"),
    "dnc": ("bits", "straight"),
    "upa": ("straight", "bits"),
    "upb": ("back", "head"),
    "outa": ("bits", "back"),
    "pa": ("back", "bits"),
    "pb": ("straight", "bits"),
}
EIGHTHS = 6


def idiv(value, k):
    return lax.div(value, jnp.int32(k))


def irem(value, k):
    return lax.rem(value, jnp.int32(k))


def bit_of(value, b):
    return irem(idiv(value, 1 << b), 2)


def flip(value, k):
    b = 0
    while k >> b:
        if (k >> b) & 1:
            value = value + (1 - 2 * bit_of(value, b)) * (1 << b)
        b += 1
    return value


def dot(a, b):
    return jnp.dot(a, b, preferred_element_type=F32)


def dot_t(a, b):
    return lax.dot_general(a, b, (((1,), (1,)), ((), ())), preferred_element_type=F32)


def t_dot(a, b):
    return lax.dot_general(a, b, (((0,), (0,)), ((), ())), preferred_element_type=F32)


def two_part_dot(a, b):
    high = b.astype(BF)
    low = (b - high.astype(F32)).astype(BF)
    return dot(a, high) + dot(a, low)


def pair_mean(rows):
    i = lax.broadcasted_iota(jnp.int32, (rows // 2, rows), 0)
    j = lax.broadcasted_iota(jnp.int32, (rows // 2, rows), 1)
    return jnp.where((j >> 1) == i, 0.5, 0.0).astype(BF)


def identity(n):
    i = lax.broadcasted_iota(jnp.int32, (n, n), 0)
    j = lax.broadcasted_iota(jnp.int32, (n, n), 1)
    return jnp.where(i == j, 1.0, 0.0).astype(BF)


def turned(value):
    n = PAIR
    parts = [
        dot_t(identity(n), value[:, i : i + n]).astype(BF) for i in range(0, value.shape[1], n)
    ]
    return parts[0] if len(parts) == 1 else jnp.concatenate(parts, axis=0)


class Plan:
    def __init__(self, seq, head, rows, pos, width, hidden):
        self.seq, self.head, self.rows, self.pos, self.width, self.hidden = seq, head, rows, pos, width, hidden
        self.minor = rows // head
        self.groups = seq // self.minor
        self.tokens = rows * pos
        self.half = self.tokens // 2
        self.pairs = width // PAIR
        self.local = (self.tokens // BLOCK).bit_length() - 1
        self.remote = self.groups.bit_length() - 1
        self.seq_bits = seq.bit_length() - 1
        self.head_bits = head.bit_length() - 1
        self.bits = self.seq_bits + self.head_bits
        self.near = self.half + sum(self.half >> level for level in range(1, self.local))
        self.lines = 5 + hidden // width
        self.far = BLOCK * self.remote
        cols = width // head
        self.blocks = {
            "down": (hidden // seq, cols),
            "up": (width // seq, hidden // head),
            "out": (width // seq, cols),
            "query": (width // seq, cols),
            "key": (width // seq, cols),
            "value": (width // seq, cols),
        }
        seqs, heads = list(range(self.seq_bits)), list(range(self.seq_bits, self.bits))
        ways = {"core": seqs[:1], "straight": seqs[1:], "back": seqs[:0:-1], "bits": heads, "head": ["head"]}
        stages = {name: [b for way in ("core",) + STAGES[name] for b in ways[way]] for name in STAGES}
        rows_down, rows_up, rows_out = hidden // seq, width // seq, width // seq
        self.fine = rows_down % (2 * LANES) == 0
        half_down = rows_down // 2
        if self.fine:
            self.chunks = [
                [(s * rows_down + i * half_down, half_down) for s in range(seq)] for i in range(2)
            ]
        else:
            self.chunks = [[(0, hidden)], []]

        def tall(name, *cuts):
            return [(name, r, r + n, c, c + LANES) for r, n in cuts for c in range(0, self.blocks[name][1], LANES)]

        if self.fine:
            third = half_down // 8 * EIGHTHS
            step = 2 * half_down
            first = [(c, c + half_down) for c in range(0, hidden // head, step)]
            second = [(c + half_down, c + step) for c in range(0, hidden // head, step)]
            lanes = lambda cs: [("up", 0, rows_up, c, c + LANES) for a, b in cs for c in range(a, b, LANES)]
            self.sums = {
                "dna": (tall("down", (0, half_down - third)), stages["dna"]),
                "dnb": (tall("down", (half_down, half_down)), stages["dnb"]),
                "dnc": (tall("down", (half_down - third, third)), stages["dnc"]),
                "upa": (lanes(first), stages["upa"]),
                "upb": (lanes(second), stages["upb"]),
            }
        else:
            self.sums = {
                "dna": (tall("down", (0, rows_down)), stages["dna"]),
                "upb": (tall("up", (0, rows_up)), stages["upb"]),
            }
        self.sums["outa"] = (tall("out", (0, rows_out)), stages["outa"])
        if rows_out % 32 == 0:
            m = rows_out // 2
            self.sums["pa"] = (tall("query", (0, rows_out)) + tall("key", (0, m)), stages["pa"])
            self.sums["pb"] = (tall("key", (m, m)) + tall("value", (0, rows_out)), stages["pb"])
        else:
            self.sums["pa"] = (tall("query", (0, rows_out)) + tall("key", (0, rows_out)), stages["pa"])
            self.sums["pb"] = (tall("value", (0, rows_out)), stages["pb"])

    def sum_shape(self, name):
        return (sum(part[2] - part[1] for part in self.sums[name][0]), LANES)

    def got_shapes(self, name):
        left, shapes = self.bits, []
        for b in self.sums[name][1]:
            if b == "head":
                shapes.append((self.head - 1,) + self.sum_shape(name))
            else:
                left -= 1
                shapes.append((2,) * left + self.sum_shape(name))
        return shapes


class Summed:
    def __init__(self, plan, me, name, number, grad, got, send, recv, outs):
        self.plan, self.name, self.number = plan, name, number
        self.s, self.h = me
        self.grad, self.got, self.outs = grad, got, outs
        self.send, self.recv = send, recv
        self.parts, self.order = plan.sums[name]
        self.started, self.stage = [], 0

    def own_bit(self, b):
        n = self.plan.seq_bits
        return bit_of(self.s, b) if b < n else bit_of(self.h, b - n)

    def index(self, fixed, other=None):
        at = []
        for b in reversed(range(self.plan.bits)):
            if b == other:
                at.append(1 - self.own_bit(b))
            elif b in fixed:
                at.append(self.own_bit(b))
            else:
                at.append(slice(None))
        return tuple(at)

    def put(self, name, s, h, block, row, col):
        owner = s + h * self.plan.seq
        at = tuple((owner >> b) & 1 for b in reversed(range(self.plan.bits)))
        first = 0
        for part, r0, r1, c0, c1 in self.parts:
            if part == name and row <= r0 < row + block.shape[0] and col <= c0 < col + block.shape[1]:
                piece = block[r0 - row : r1 - row, c0 - col : c1 - col]
                self.grad[at + (slice(first, first + r1 - r0),)] = piece.astype(BF)
            first += r1 - r0

    def copy(self, source, target, slot, device):
        copy = pltpu.make_async_remote_copy(
            src_ref=source,
            dst_ref=target,
            send_sem=self.send.at[self.number, slot],
            recv_sem=self.recv.at[self.number, slot],
            device_id=device,
            device_id_type=MESH,
        )
        copy.start()
        self.started.append(copy)

    def start(self, stage):
        b = self.order[stage]
        n = self.plan.seq_bits
        if b == "head":
            for k in range(1, self.plan.head):
                peer = flip(self.h, k)
                at = tuple(bit_of(peer, i) for i in reversed(range(self.plan.head_bits)))
                at += self.index(range(n))[self.plan.head_bits :]
                self.copy(self.grad.at[at], self.got[stage].at[k - 1], stage + k - 1, (self.s, peer))
            return
        device = (flip(self.s, 1 << b), self.h) if b < n else (self.s, flip(self.h, 1 << (b - n)))
        source = self.grad.at[self.index(self.order[:stage], b)]
        self.copy(source, self.got[stage], stage, device)

    def finish(self, stage):
        b = self.order[stage]
        if stage + 1 == len(self.order):
            total = self.grad[self.index(range(self.plan.bits))].astype(F32)
            if b == "head":
                for k in range(1, self.plan.head):
                    self.started[stage + k - 1].wait_recv()
                    total = total + self.got[stage][k - 1].astype(F32)
            else:
                self.started[stage].wait_recv()
                total = total + self.got[stage][...].astype(F32)
            first = 0
            for part, r0, r1, c0, c1 in self.parts:
                self.outs[part][r0:r1, c0:c1] = total[first : first + r1 - r0]
                first += r1 - r0
            return
        self.started[stage].wait_recv()
        at = self.index(self.order[: stage + 1])
        combos = [()]
        for a in at:
            if isinstance(a, slice):
                combos = [c + (i,) for c in combos for i in range(2)]
        for combo in combos:
            left = list(combo)
            full = tuple(left.pop(0) if isinstance(a, slice) else a for a in at)
            self.grad[full] = self.grad[full] + self.got[stage][combo]

    def step(self):
        if self.stage:
            self.finish(self.stage - 1)
        if self.stage < len(self.order):
            self.start(self.stage)
        self.stage += 1

    @property
    def done(self):
        return self.stage > len(self.order)

    def drain(self):
        for copy in self.started:
            copy.wait_send()


def layer_kernel(plan, *refs):
    refs = list(refs)

    def take(n):
        taken = refs[:n]
        del refs[:n]
        return taken

    x_in, dy_in, *lines_in = take(8)
    weights_in = take(6)
    lo_out, ig_out = take(2)
    grads_out = dict(zip(plan.blocks, take(6)))
    lines_out = take(6)
    xg, dyg, log, igg = take(4)
    wq, wk, wv, wo, wu, wd = weights = take(6)
    gain_one, shift_one, gain_two, shift_two, up_bias, down_bias = lines = take(6)
    norm_t, n_one, rs_one, n_two, rs_two, norm_two_b, residual, d_residual = take(8)
    qs, kn, vn, kf, vf, near_values = take(6)
    pn, pf, stats, mask, mixed_t = take(5)
    act_ref, hid_ref, cdf_ref, dh_ref = take(4)
    dos, dq_t, dk_ref, dv_ref, far_ref, bar_t, d_norm_one = take(7)
    c_send, c_got, c_half, c_half_got, bar_send, bar_got, d_send, d_got, d_half, d_half_got, far_parts = take(11)
    sums = {}
    for name in plan.sums:
        grad, *got = take(1 + len(plan.sums[name][1]))
        sums[name] = (grad, got)
    vec_bufs, vec_got, vec_own, vec_own_got = take(4)
    send_a, recv_a, send_r, recv_r, send_s, recv_s, here = take(7)
    assert not refs

    seq, head, rows, width, tokens = plan.seq, plan.head, plan.rows, plan.width, plan.tokens
    half, near, far = plan.half, plan.near, plan.far
    s, h = lax.axis_index("seq"), lax.axis_index("head")
    c, g = irem(s, plan.minor), idiv(s, plan.minor)
    j = c * head + h

    def group_peer(k):
        other = flip(j, k)
        return other, (g * plan.minor + idiv(other, head), irem(other, head))

    def row_peer(k):
        other = flip(g, k)
        return other, (other * plan.minor + c, h)

    barrier = pltpu.get_barrier_semaphore()
    peers = [group_peer(k)[1] for k in range(1, rows)] + [row_peer(k)[1] for k in range(1, plan.groups)]
    for device in peers:
        pl.semaphore_signal(barrier, inc=1, device_id=device, device_id_type=MESH)

    small = [pltpu.make_async_copy(a, b, here.at[10 + i]) for i, (a, b) in enumerate(zip(lines_in, lines))]
    for copy in small:
        copy.start()
    loads = [pltpu.make_async_copy(a, b, here.at[i]) for i, (a, b) in enumerate(zip(weights_in, weights))]
    for i in (1, 2, 0, 3, 4, 5):
        loads[i].start()
    own = [
        pltpu.make_async_copy(x_in.at[j], xg.at[j], here.at[6]),
        pltpu.make_async_copy(dy_in.at[j], dyg.at[j], here.at[7]),
    ]
    for copy in own:
        copy.start()

    i_k = lax.broadcasted_iota(jnp.int32, (near, 2 * half), 0)
    i_q = lax.broadcasted_iota(jnp.int32, (near, 2 * half), 1) & (half - 1)
    valid = (i_k < half) & ((i_q >> 5) == (i_k >> 5))
    first = half
    for level in range(1, plan.local - 1):
        count = half >> level
        mine = (i_k >= first) & (i_k < first + count)
        valid = valid | (mine & (((i_q >> (4 + level)) ^ 1) == ((i_k - first) >> 4)))
        first += count
    valid = valid | (i_k >= first)
    mask[...] = jnp.where(valid, 0.0, -1e30).astype(F32)

    pl.semaphore_wait(barrier, len(peers))

    def exchange(number, source, target):
        copies = []
        for k in sorted(range(1, rows), key=lambda k: -(k % head)):
            other, device = group_peer(k)
            copy = pltpu.make_async_remote_copy(
                src_ref=source.at[other],
                dst_ref=target.at[j],
                send_sem=send_a.at[number, k],
                recv_sem=recv_a.at[number, k],
                device_id=device,
                device_id_type=MESH,
            )
            copy.start()
            copies.append(copy)
        return copies

    x_copies = exchange(0, x_in, xg)

    def norm_stats(values):
        center = values - jnp.mean(values, axis=-1, keepdims=True)
        spread = jnp.mean(center * center, axis=-1, keepdims=True)
        scale = lax.rsqrt(spread + EPSILON)
        return center * scale, scale

    def norm_back(d_norm, n, scale, gain):
        weighted = d_norm * gain
        return scale * (
            weighted
            - jnp.mean(weighted, axis=-1, keepdims=True)
            - n * jnp.mean(weighted * n, axis=-1, keepdims=True)
        )

    lane = lax.broadcasted_iota(jnp.int32, (1, PAIR), 1)
    low = lane < DH

    def stack_heads(ref, value):
        for p in range(plan.pairs):
            for a in range(2):
                part = value[a * half : (a + 1) * half, p * PAIR : (p + 1) * PAIR]
                zero = jnp.zeros_like(part)
                ref[p, a, :half, :] = jnp.where(low, part, zero)
                ref[p, a, half:, :] = jnp.where(low, zero, part)

    for copy in small:
        copy.wait()
    own[0].wait()
    near_first = x_copies[::-1]
    for copy in near_first[:-2]:
        copy.wait_recv()
    dy_copies = exchange(1, dy_in, dyg)
    for copy in near_first[-2:]:
        copy.wait_recv()
    x = xg[...].reshape(tokens, width).astype(F32)
    n, scale = norm_stats(x)
    n_one[...] = n
    rs_one[...] = scale
    normed = (n * gain_one[...] + shift_one[...]).astype(BF)

    loads[1].wait()
    loads[2].wait()
    level = jnp.concatenate([dot(normed, wk[...]).astype(BF), dot(normed, wv[...]).astype(BF)], axis=1)

    def columns(index, p):
        return slice(index * width + p * PAIR, index * width + (p + 1) * PAIR)

    targets = (kn, vn)
    first = 0
    for l in range(plan.local):
        if l:
            level = dot(pair_mean(level.shape[0]), level).astype(BF)
        count = level.shape[0] // 2
        for index, ref in enumerate(targets):
            for p in range(plan.pairs):
                for a in range(2):
                    b = a if l + 1 < plan.local else 1 - a
                    ref[p, b, first : first + count, :] = level[a * count : (a + 1) * count, columns(index, p)]
        first += count
    level = dot(pair_mean(level.shape[0]), level).astype(BF)
    c_send[0] = level[:, :width]
    c_send[1] = level[:, width:]
    level = dot(pair_mean(level.shape[0]), level).astype(BF)
    c_half[: BLOCK // 2, :] = level[:, :width]
    c_half[BLOCK // 2 :, :] = level[:, width:]
    c_copies = []
    for k in range(1, plan.groups):
        other, device = row_peer(k)
        copy = pltpu.make_async_remote_copy(
            src_ref=c_send if k == 1 else c_half,
            dst_ref=c_got if k == 1 else c_half_got.at[g],
            send_sem=send_r.at[0, k],
            recv_sem=recv_r.at[0, k],
            device_id=device,
            device_id_type=MESH,
        )
        copy.start()
        c_copies.append(copy)

    loads[0].wait()
    stack_heads(qs, (dot(normed, wq[...]) * (DH**-0.5)).astype(BF))
    norm_t[...] = turned(normed)

    def attend_near(p):
        for a in range(2):
            at = slice((2 * p + a) * tokens, (2 * p + a + 1) * tokens)
            scores = dot_t(kn[p, a], qs[p, a]) + mask[...]
            top = jnp.max(scores, axis=0, keepdims=True)
            raised = jnp.exp(scores - top)
            pn[p, a] = raised
            stats[0:1, at] = top
            stats[1:2, at] = jnp.sum(raised, axis=0, keepdims=True)
            near_values[p, a] = dot(turned(vn[p, a]), raised.astype(BF))

    for p in range(plan.pairs):
        attend_near(p)

    for copy in c_copies:
        copy.wait_recv()

    def sibling(b):
        upper = idiv(g, 1 << b)
        return (upper + 1 - 2 * irem(upper, 2)) * (1 << b)

    for b in range(plan.remote):
        for index in range(2):
            if b == 0:
                level = c_got[index]
            else:
                count = 1 << b
                both_kinds = c_half_got[pl.ds(sibling(b), count)].reshape(BLOCK * count, width)
                i_r = lax.broadcasted_iota(jnp.int32, (BLOCK * count // 2, BLOCK * count), 0)
                i_s = lax.broadcasted_iota(jnp.int32, (BLOCK * count // 2, BLOCK * count), 1)
                own_rows = (i_r >> 3) * BLOCK + index * (BLOCK // 2) + (i_r & 7) == i_s
                level = dot(jnp.where(own_rows, 1.0, 0.0).astype(BF), both_kinds).astype(BF)
                for _ in range(b - 1):
                    level = dot(pair_mean(level.shape[0]), level).astype(BF)
            for p in range(plan.pairs):
                part = level[:, p * PAIR : (p + 1) * PAIR]
                (kf, vf)[index][p, b * BLOCK : (b + 1) * BLOCK, :] = part

    halves = [(p, a) for p in range(plan.pairs) for a in range(2)]
    scores = jnp.concatenate([dot_t(kf[p], qs[p, a]) for p, a in halves], axis=1)
    top_near = stats[0:1, :]
    top = jnp.maximum(top_near, jnp.max(scores, axis=0, keepdims=True))
    shrink = jnp.exp(top_near - top)
    raised = jnp.exp(scores - top)
    share = 1.0 / (stats[1:2, :] * shrink + jnp.sum(raised, axis=0, keepdims=True))
    near_share = shrink * share
    stats[2:3, :] = near_share
    prob = raised * share
    pf[...] = prob
    prob = prob.astype(BF)
    for i, (p, a) in enumerate(halves):
        at = slice(i * tokens, (i + 1) * tokens)
        mixed = near_values[p, a] * near_share[:, at] + t_dot(vf[p], prob[:, at])
        mixed_t[p, :DH, a * half : (a + 1) * half] = mixed[:DH, :half].astype(BF)
        mixed_t[p, DH:, a * half : (a + 1) * half] = mixed[DH:, half:].astype(BF)

    loads[3].wait()
    res = xg[...].reshape(tokens, width).astype(F32) + t_dot(mixed_t[...].reshape(width, tokens), wo[...])
    residual[...] = res
    n, scale = norm_stats(res)
    n_two[...] = n
    rs_two[...] = scale
    norm_two_b[...] = (n * gain_two[...] + shift_two[...]).astype(BF)

    row = lambda a: jnp.sum(a, axis=0, keepdims=True)
    per = plan.hidden // width

    def put_block(name, block, first_row, first_col):
        r, w = plan.blocks[name]
        row_step, col_step = min(r, block.shape[0]), min(w, block.shape[1])
        for a in range(0, block.shape[0], row_step):
            for b in range(0, block.shape[1], col_step):
                s_at, h_at = (first_row + a) // r, (first_col + b) // w
                piece = block[a : a + row_step, b : b + col_step]
                for item in items.values():
                    if item is not vec_sum:
                        item.put(name, s_at, h_at, piece, (first_row + a) % r, (first_col + b) % w)

    class Vectors:
        def __init__(self):
            self.stage, self.started = 0, []

        def copy(self, source, target, slot, device):
            copy = pltpu.make_async_remote_copy(
                src_ref=source,
                dst_ref=target,
                send_sem=send_s.at[len(plan.sums), slot],
                recv_sem=recv_s.at[len(plan.sums), slot],
                device_id=device,
                device_id_type=MESH,
            )
            copy.start()
            self.started.append(copy)

        def step(self):
            n, k = plan.seq_bits, self.stage
            if 0 < k <= n:
                self.started[k - 1].wait_recv()
                vec_bufs[k] = vec_bufs[k - 1] + vec_got[k - 1]
            if k < n:
                self.copy(vec_bufs.at[k], vec_got.at[k], k, (flip(s, 1 << k), h))
            elif k == n:
                vec = vec_bufs[n]
                part = own_part(vec[:8])
                vec_own[:, : part.shape[1]] = part
                part = own_part(jnp.concatenate([vec[5 + i : 6 + i] for i in range(per)], axis=1))
                vec_own[5:6, : part.shape[1]] = part
                for i in range(1, head):
                    self.copy(vec_own, vec_own_got.at[i - 1], n + i - 1, (s, flip(h, i)))
            else:
                values = [vec_own[...]]
                for i in range(1, head):
                    self.started[n + i - 1].wait_recv()
                    values.append(vec_own_got[i - 1])
                while len(values) > 1:
                    values = [values[i] + values[i + 1] for i in range(0, len(values), 2)]
                for i, line in enumerate(lines_out):
                    line[...] = values[0][i, : line.shape[0]]
            self.stage += 1

        @property
        def done(self):
            return self.stage > plan.seq_bits + 1

        def drain(self):
            for copy in self.started:
                copy.wait_send()

    def own_part(line):
        share = line.shape[1] // seq
        part = line[:, :share]
        for other in range(1, seq):
            part = jnp.where(s == other, line[:, other * share : (other + 1) * share], part)
        return part

    vec_sum = Vectors()
    items = {
        name: Summed(plan, (s, h), name, i, grad, got, send_s, recv_s, grads_out)
        for i, (name, (grad, got)) in enumerate(sums.items())
    }
    items["vec"] = vec_sum

    def cotangent():
        return dyg[...].reshape(tokens, width)

    def blocks_of(chunk):
        at, blocks = 0, []
        for start, length in plan.chunks[chunk]:
            for f in range(start, start + length, 512):
                n = min(512, start + length - f)
                if not blocks or blocks[-1][1] + n > 512:
                    blocks.append([[], 0, at])
                blocks[-1][0].append((f, n))
                blocks[-1][1] += n
                at += n
        return [(segments, slice(first, first + n)) for segments, n, first in blocks]

    def columns_of(ref, segments):
        return jnp.concatenate([ref[:, f : f + n] for f, n in segments], axis=1)

    def rows_of(ref, segments):
        return jnp.concatenate([ref[f : f + n, :] for f, n in segments], axis=0)

    flat = [(chunk, *block) for chunk in range(2) for block in blocks_of(chunk)]
    quarters = [flat[i : i + 1] for i in range(4)] if plan.fine else [flat, [], [], []]

    def activate(quarter):
        if quarter == 0:
            loads[4].wait()
        for chunk, segments, at in quarters[quarter]:
            hid = dot(norm_two_b[...], columns_of(wu, segments)) + columns_of(up_bias, segments)
            cdf = 0.5 * (1.0 + lax.erf(hid * (0.5**0.5)))
            act = (hid * cdf).astype(BF)
            act_ref[chunk, :, at] = act
            hid_ref[chunk, :, at] = hid
            cdf_ref[chunk, :, at] = cdf

    def down_grad(quarter):
        if quarter == 0:
            loads[5].wait()
            own[1].wait()
            for copy in dy_copies:
                copy.wait_recv()
        for chunk, segments, at in quarters[quarter]:
            grad = t_dot(act_ref[chunk, :, at], cotangent())
            first = 0
            for f, n in segments:
                put_block("down", grad[first : first + n], f, 0)
                first += n

    def deactivate(quarter):
        for chunk, segments, at in quarters[quarter]:
            hid = hid_ref[chunk, :, at]
            slope = cdf_ref[chunk, :, at] + hid * (jnp.exp(-0.5 * hid * hid) * 0.3989422804014327)
            dh = (dot_t(cotangent(), rows_of(wd, segments)) * slope).astype(BF)
            dh_ref[chunk, :, at] = dh
            sums_dh = row(dh.astype(F32))
            grad = t_dot(norm_two_b[...], dh)
            first = 0
            for f, n in segments:
                for o in range(0, n, min(n, width)):
                    line, lane_at = divmod(f + o, width)
                    m = min(n, width)
                    vec_bufs[0, 5 + line : 6 + line, lane_at : lane_at + m] = sums_dh[:, first + o : first + o + m]
                put_block("up", grad[:, first : first + n], 0, f)
                first += n

    def both(ref, weight, product, pick):
        total = None
        for chunk in range(2):
            for segments, at in blocks_of(chunk):
                term = product(ref[chunk, :, at], pick(weight, segments))
                total = term if total is None else total + term
        return total

    def second_norm_back():
        d_norm_two = both(dh_ref, wu, dot_t, columns_of)
        n = n_two[...]
        dy_f = cotangent().astype(F32)
        vec_bufs[0, 2:3, :] = row(d_norm_two * n)
        vec_bufs[0, 3:4, :] = row(d_norm_two)
        vec_bufs[0, 4:5, :] = row(dy_f)
        d_residual[...] = dy_f + norm_back(d_norm_two, n, rs_two[...], gain_two[...])

    def out_grad():
        put_block("out", dot(mixed_t[...].reshape(width, tokens), d_residual[...].astype(BF)), 0, 0)

    def mixed_back():
        stack_heads(dos, dot_t(d_residual[...].astype(BF), wo[...]).astype(BF))

    def layer_output():
        result = residual[...] + both(act_ref, wd, dot, rows_of) + down_bias[...]
        log[...] = result.astype(BF).reshape(rows, plan.pos, width)

    late_copies, own_late = [], []

    def send_layer_output():
        late_copies.extend(exchange(2, log, lo_out))
        own_late.append(pltpu.make_async_copy(log.at[j], lo_out.at[j], here.at[8]))
        own_late[-1].start()

    def spread_matrix():
        i_t = lax.broadcasted_iota(jnp.int32, (half, near - half), 0)
        i_c = lax.broadcasted_iota(jnp.int32, (half, near - half), 1)
        spread = jnp.zeros((half, near - half), F32)
        first = 0
        for level in range(1, plan.local):
            spread = spread + jnp.where((i_t >> level) == (i_c - first), 0.5**level, 0.0)
            first += half >> level
        return spread.astype(BF)

    def attend_back(p):
        spread = spread_matrix()
        dk, dv, dk_far, dv_far = [], [], 0.0, 0.0
        k_far, v_far = kf[p], vf[p]
        for a in range(2):
            at = slice((2 * p + a) * tokens, (2 * p + a + 1) * tokens)
            q, do = qs[p, a], dos[p, a]
            prob, prob_far = pn[p, a] * stats[2:3, at], pf[:, at]
            d_prob = dot_t(vn[p, a], do)
            d_prob_far = dot_t(v_far, do)
            inner = row(prob * d_prob) + row(prob_far * d_prob_far)
            d_scores = (prob * (d_prob - inner)).astype(BF)
            d_scores_far = (prob_far * (d_prob_far - inner)).astype(BF)
            dk.append(dot(d_scores, q))
            dv.append(dot(prob.astype(BF), do))
            dk_far = dk_far + dot(d_scores_far, q)
            dv_far = dv_far + dot(prob_far.astype(BF), do)
            dq = (t_dot(kn[p, a], d_scores) + t_dot(k_far, d_scores_far)) * (DH**-0.5)
            dq_t[p, :DH, a * half : (a + 1) * half] = dq[:DH, :half].astype(BF)
            dq_t[p, DH:, a * half : (a + 1) * half] = dq[DH:, half:].astype(BF)
        other = near - BLOCK
        for index, (total, total_far, ref) in enumerate(((dk, dk_far, dk_ref), (dv, dv_far, dv_ref))):
            for a in range(2):
                coarse = jnp.concatenate([total[a][half:other], total[1 - a][other:]], axis=0)
                ref[p, a * half : (a + 1) * half, :] = total[a][:half] + two_part_dot(spread, coarse)
            far_ref[index, p] = total_far

    d_copies = []

    def send_far():
        i_a = lax.broadcasted_iota(jnp.int32, (BLOCK, BLOCK), 0)
        i_b = lax.broadcasted_iota(jnp.int32, (BLOCK, BLOCK), 1)
        for k in range(1, plan.groups):
            other, device = row_peer(k)
            b = k.bit_length() - 1
            offset = irem(other, 1 << b)
            for index in range(2):
                for p in range(plan.pairs):
                    level = far_ref[index, p, BLOCK * b : BLOCK * (b + 1), :].astype(BF)
                    if b == 0:
                        d_send[index, p] = level
                        continue
                    rows_at = (offset * (BLOCK // 2) + (i_a & 7)) >> (b - 1)
                    pick = jnp.where((rows_at == i_b) & ((i_a >> 3) == index), 0.5**b, 0.0).astype(BF)
                    part = dot(pick, level)
                    if index == 0:
                        far_parts[p] = part
                    else:
                        d_half[k, p] = (far_parts[p] + part).astype(BF)
            copy = pltpu.make_async_remote_copy(
                src_ref=d_send if k == 1 else d_half.at[k],
                dst_ref=d_got if k == 1 else d_half_got.at[k],
                send_sem=send_r.at[1, k],
                recv_sem=recv_r.at[1, k],
                device_id=device,
                device_id_type=MESH,
            )
            copy.start()
            d_copies.append(copy)

    def part_grads():
        put_block("query", dot_t(norm_t[...], dq_t[...].reshape(width, tokens)), 0, 0)
        for index, (ref, name) in enumerate(((dk_ref, "key"), (dv_ref, "value"))):
            mine = jnp.concatenate([ref[p].astype(BF) for p in range(plan.pairs)], axis=1)
            made = jnp.concatenate([far_ref[index, p].astype(BF) for p in range(plan.pairs)], axis=1)
            put_block(name, dot(norm_t[...], mine) + dot(bar_t[...], made), 0, 0)

    bar_copies = []

    def send_bars():
        i_a = lax.broadcasted_iota(jnp.int32, (BLOCK, tokens), 0)
        i_b = lax.broadcasted_iota(jnp.int32, (BLOCK, tokens), 1)
        mean_all = jnp.where((i_b >> plan.local) == i_a, 0.5**plan.local, 0.0).astype(BF)
        bar_send[...] = dot_t(mean_all, norm_t[...]).astype(BF)
        for k in range(1, plan.groups):
            other, device = row_peer(k)
            copy = pltpu.make_async_remote_copy(
                src_ref=bar_send,
                dst_ref=bar_got.at[g],
                send_sem=send_r.at[2, k],
                recv_sem=recv_r.at[2, k],
                device_id=device,
                device_id_type=MESH,
            )
            copy.start()
            bar_copies.append(copy)

    def take_bars():
        for copy in bar_copies:
            copy.wait_recv()
        for b in range(plan.remote):
            level = bar_got[pl.ds(sibling(b), 1 << b)].reshape(BLOCK << b, width)
            for _ in range(b):
                level = dot(pair_mean(level.shape[0]), level).astype(BF)
            bar_t[:, b * BLOCK : (b + 1) * BLOCK] = turned(level)

    def query_back():
        d_norm_one[...] = dot_t(turned(dq_t[...].reshape(width, tokens)), wq[...])

    def take_far():
        for copy in d_copies:
            copy.wait_recv()

    def first_norm_back():
        i_t = lax.broadcasted_iota(jnp.int32, (tokens, BLOCK), 0)
        i_c = lax.broadcasted_iota(jnp.int32, (tokens, BLOCK), 1)
        last = jnp.where((i_t >> plan.local) == i_c, 0.5**plan.local, 0.0).astype(BF)
        half_of = [
            jnp.where((i_t >> (plan.local + 1)) == i_c - (BLOCK // 2) * i, 0.5**plan.local, 0.0).astype(BF)
            for i in range(2)
        ]
        d_normed = d_norm_one[...]
        for index, (ref, w) in enumerate(((dk_ref, wk), (dv_ref, wv))):
            pieces = []
            for p in range(plan.pairs):
                total = ref[p] + dot(last, d_got[index, p])
                if plan.groups > 2:
                    coarse = d_half_got[2, p].astype(F32)
                    for k in range(3, plan.groups):
                        coarse = coarse + d_half_got[k, p].astype(F32)
                    total = total + two_part_dot(half_of[index], coarse)
                pieces.append(total.astype(BF))
            d_normed = d_normed + dot_t(jnp.concatenate(pieces, axis=1), w[...])
        n = n_one[...]
        vec_bufs[0, 0:1, :] = row(d_normed * n)
        vec_bufs[0, 1:2, :] = row(d_normed)
        d_first = norm_back(d_normed, n, rs_one[...], gain_one[...])
        igg[...] = (d_residual[...] + d_first).astype(BF).reshape(rows, plan.pos, width)

    def send_input_grad():
        late_copies.extend(exchange(3, igg, ig_out))
        own_late.append(pltpu.make_async_copy(igg.at[j], ig_out.at[j], here.at[9]))
        own_late[-1].start()

    vec_own[...] = jnp.zeros_like(vec_own)
    work = {
        **{f"f1{i}": functools.partial(activate, i) for i in range(4)},
        **{f"g1{i}": functools.partial(down_grad, i) for i in range(4)},
        **{f"f2{i}": functools.partial(deactivate, i) for i in range(4)},
        "ln2b": second_norm_back,
        "outg": out_grad,
        "lo": layer_output,
        "Alo": send_layer_output,
        "dmix": mixed_back,
        "Abar": send_bars,
        "bar": take_bars,
        "dsend": send_far,
        "qkvg": part_grads,
        "dnq": query_back,
        "Wd": take_far,
        "ln1b": first_norm_back,
        "Aig": send_input_grad,
    }
    first_pairs = {f"ab{i}": range(i, plan.pairs, 4) for i in range(4)}
    for name in ORDER:
        if name in work:
            work[name]()
        elif name in first_pairs:
            for p in first_pairs[name]:
                attend_back(p)
        elif name in items:
            items[name].step()
    while not all(item.done for item in items.values()):
        for item in items.values():
            if not item.done:
                item.step()

    for copy in late_copies:
        copy.wait_recv()
    for copy in own_late:
        copy.wait()
    for copy in x_copies + dy_copies + c_copies + bar_copies + d_copies + late_copies:
        copy.wait_send()
    for item in items.values():
        item.drain()


def place_kernel(*refs):
    count = len(refs) // 2
    ins, outs, sems = refs[:count], refs[count:-1], refs[-1]
    copies = [pltpu.make_async_copy(a, b, sems.at[i]) for i, (a, b) in enumerate(zip(ins, outs))]
    for copy in copies:
        copy.start()
    for copy in copies:
        copy.wait()


def body(
    inputs,
    gain_first,
    shift_first,
    query_weight,
    key_weight,
    value_weight,
    out_weight,
    gain_second,
    shift_second,
    up_weight,
    up_bias,
    down_weight,
    down_bias,
    cotangent,
):
    rows, pos, width = inputs.shape
    hidden = up_weight.shape[1]
    plan = Plan(lax.axis_size("seq"), lax.axis_size("head"), rows, pos, width, hidden)
    tokens, pairs, groups, half, near, far = plan.tokens, plan.pairs, plan.groups, plan.half, plan.near, plan.far
    vmem = pl.BlockSpec(memory_space=pltpu.VMEM)
    anywhere = pl.BlockSpec(memory_space=pl.ANY)
    names = list(plan.blocks)

    def buf(*shape, dtype=BF):
        return pltpu.VMEM(shape, dtype)

    scratch = [buf(rows, pos, width)] * 4
    scratch += [buf(width, width)] * 4 + [buf(width, hidden), buf(hidden, width)]
    scratch += [buf(1, n, dtype=F32) for n in (width, width, width, width, hidden, width)]
    scratch += [
        buf(width, tokens),
        buf(tokens, width, dtype=F32),
        buf(tokens, 1, dtype=F32),
        buf(tokens, width, dtype=F32),
        buf(tokens, 1, dtype=F32),
        buf(tokens, width),
        buf(tokens, width, dtype=F32),
        buf(tokens, width, dtype=F32),
    ]
    scratch += [
        buf(pairs, 2, tokens, PAIR),
        buf(pairs, 2, near, PAIR),
        buf(pairs, 2, near, PAIR),
        buf(pairs, far, PAIR),
        buf(pairs, far, PAIR),
        buf(pairs, 2, PAIR, tokens, dtype=F32),
    ]
    scratch += [
        buf(pairs, 2, near, tokens, dtype=F32),
        buf(far, 2 * pairs * tokens, dtype=F32),
        buf(8, 2 * pairs * tokens, dtype=F32),
        buf(near, tokens, dtype=F32),
        buf(pairs, PAIR, tokens),
    ]
    part = sum(n for _, n in plan.chunks[0])
    scratch += [buf(2, tokens, part)] + [buf(2, tokens, part, dtype=F32)] * 2 + [buf(2, tokens, part)]
    scratch += [
        buf(pairs, 2, tokens, PAIR),
        buf(pairs, PAIR, tokens),
        buf(pairs, tokens, PAIR, dtype=F32),
        buf(pairs, tokens, PAIR, dtype=F32),
        buf(2, pairs, BLOCK * plan.remote, PAIR, dtype=F32),
        buf(width, BLOCK * plan.remote),
        buf(tokens, width, dtype=F32),
    ]
    scratch += [
        buf(2, BLOCK, width),
        buf(2, BLOCK, width),
        buf(BLOCK, width),
        buf(groups, BLOCK, width),
        buf(BLOCK, width),
        buf(groups, BLOCK, width),
        buf(2, pairs, BLOCK, PAIR),
        buf(2, pairs, BLOCK, PAIR),
        buf(groups, pairs, BLOCK, PAIR),
        buf(groups, pairs, BLOCK, PAIR),
        buf(pairs, BLOCK, PAIR, dtype=F32),
    ]
    for name in plan.sums:
        scratch += [buf(*(2,) * plan.bits, *plan.sum_shape(name))]
        scratch += [buf(*shape) for shape in plan.got_shapes(name)]
    slots = plan.bits + plan.head
    share = max(width, hidden) // plan.seq
    scratch += [
        buf(plan.seq_bits + 1, plan.lines, width, dtype=F32),
        buf(plan.seq_bits, plan.lines, width, dtype=F32),
        buf(8, share, dtype=F32),
        buf(plan.head - 1, 8, share, dtype=F32),
    ]
    dma = pltpu.SemaphoreType.DMA
    scratch += [dma((4, rows)), dma((4, rows)), dma((3, groups)), dma((3, groups))]
    scratch += [dma((len(plan.sums) + 1, slots)), dma((len(plan.sums) + 1, slots)), dma((16,))]

    line = lambda a: a.reshape(1, -1)
    big = [jax.ShapeDtypeStruct(inputs.shape, BF)] * 2 + [jax.ShapeDtypeStruct(plan.blocks[n], F32) for n in names]
    lines = [jax.ShapeDtypeStruct((width // plan.seq,), F32)] * 5 + [jax.ShapeDtypeStruct((hidden // plan.seq,), F32)]
    results = pl.pallas_call(
        functools.partial(layer_kernel, plan),
        out_shape=[pltpu.VMEM(o.shape, o.dtype) for o in big + lines],
        in_specs=[anywhere] * 14,
        out_specs=[vmem] * 14,
        scratch_shapes=scratch,
        compiler_params=pltpu.CompilerParams(
            collective_id=0, has_side_effects=True, vmem_limit_bytes=56 << 20
        ),
        name="layer",
    )(
        inputs,
        cotangent,
        line(gain_first),
        line(shift_first),
        line(gain_second),
        line(shift_second),
        line(up_bias),
        line(down_bias),
        query_weight,
        key_weight,
        value_weight,
        out_weight,
        up_weight,
        down_weight,
    )
    placed = pl.pallas_call(
        place_kernel,
        out_shape=big + lines,
        in_specs=[vmem] * 14,
        out_specs=[anywhere] * 14,
        scratch_shapes=[dma((14,))],
        name="place",
    )(*[pltpu.with_memory_space_constraint(r, pltpu.VMEM) for r in results])
    layer_out, input_grad, down_g, up_g, out_g, query_g, key_g, value_g = placed[:8]
    gain_one_g, shift_one_g, gain_two_g, shift_two_g, down_bias_g, up_bias_g = placed[8:]
    return (
        layer_out,
        input_grad,
        gain_one_g,
        shift_one_g,
        query_g,
        key_g,
        value_g,
        out_g,
        gain_two_g,
        shift_two_g,
        up_g,
        up_bias_g,
        down_g,
        down_bias_g,
    )


def solution(mesh):
    placed = (P(None, ("seq", "head"), None),) + (P(),) * 12 + (P(None, ("seq", "head"), None),)
    return jax.shard_map(
        body,
        mesh=mesh,
        in_specs=placed,
        out_specs=(
            P(None, ("seq", "head"), None),
            P(None, ("seq", "head"), None),
            P("seq"),
            P("seq"),
            P("seq", "head"),
            P("seq", "head"),
            P("seq", "head"),
            P("seq", "head"),
            P("seq"),
            P("seq"),
            P("seq", "head"),
            P("seq"),
            P("seq", "head"),
            P("seq"),
        ),
        check_vma=False,
    )
```

```python
import functools

import jax
import jax.numpy as jnp
from jax import lax
from jax.experimental import pallas as pl
from jax.experimental.pallas import tpu as pltpu
from jax.sharding import PartitionSpec as P

MESH = pl.DeviceIdType.MESH
BF = jnp.bfloat16
F32 = jnp.float32
DH = 64
BLOCK = 16
EPSILON = 1e-05
PAIR = 2 * DH
LANES = 128
ORDER = (
    "f10", "f13", "f11", "g10", "g11", "dnc", "f12", "g12", "g13", "dnb", "f21", "dnc", "Abar", "dna", "f20",
    "dnb", "upa", "f23", "dna", "f22", "lo", "upb", "upa", "Alo", "ln2b", "dmix", "ab3", "outg", "upb",
    "outa", "ab0", "outa", "ab2", "ab1", "dnc", "dnb", "bar", "dnq", "qkvg", "dsend", "pb", "pb", "pa", "upa",
    "pa", "outa", "upb", "dnb", "Wd", "ln1b", "Aig", "vec", "dnb", "upa", "vec", "dna", "pb", "upb", "outa",
    "pa", "vec", "pb", "dnc", "dna", "pa", "vec", "upa", "pb", "dna", "dnb", "dnc", "upb", "outa", "pa",
    "dna", "dnc", "pb", "upa", "vec", "outa", "pa",
)
STAGES = {
    "dna": ("straight", "bits"),
    "dnb": ("back", "bits"),
    "dnc": ("bits", "straight"),
    "upa": ("straight", "bits"),
    "upb": ("back", "head"),
    "outa": ("bits", "back"),
    "pa": ("back", "bits"),
    "pb": ("straight", "bits"),
}
EIGHTHS = 6


def idiv(value, k):
    return lax.div(value, jnp.int32(k))


def irem(value, k):
    return lax.rem(value, jnp.int32(k))


def bit_of(value, b):
    return irem(idiv(value, 1 << b), 2)


def flip(value, k):
    b = 0
    while k >> b:
        if (k >> b) & 1:
            value = value + (1 - 2 * bit_of(value, b)) * (1 << b)
        b += 1
    return value


def dot(a, b):
    return jnp.dot(a, b, preferred_element_type=F32)


def dot_t(a, b):
    return lax.dot_general(a, b, (((1,), (1,)), ((), ())), preferred_element_type=F32)


def t_dot(a, b):
    return lax.dot_general(a, b, (((0,), (0,)), ((), ())), preferred_element_type=F32)


def two_part_dot(a, b):
    high = b.astype(BF)
    low = (b - high.astype(F32)).astype(BF)
    return dot(a, high) + dot(a, low)


def pair_mean(rows):
    i = lax.broadcasted_iota(jnp.int32, (rows // 2, rows), 0)
    j = lax.broadcasted_iota(jnp.int32, (rows // 2, rows), 1)
    return jnp.where((j >> 1) == i, 0.5, 0.0).astype(BF)


def identity(n):
    i = lax.broadcasted_iota(jnp.int32, (n, n), 0)
    j = lax.broadcasted_iota(jnp.int32, (n, n), 1)
    return jnp.where(i == j, 1.0, 0.0).astype(BF)


def turned(value):
    n = PAIR
    parts = [
        dot_t(identity(n), value[:, i : i + n]).astype(BF) for i in range(0, value.shape[1], n)
    ]
    return parts[0] if len(parts) == 1 else jnp.concatenate(parts, axis=0)


class Plan:
    def __init__(self, seq, head, rows, pos, width, hidden):
        self.seq, self.head, self.rows, self.pos, self.width, self.hidden = seq, head, rows, pos, width, hidden
        self.minor = rows // head
        self.groups = seq // self.minor
        self.tokens = rows * pos
        self.half = self.tokens // 2
        self.pairs = width // PAIR
        self.local = (self.tokens // BLOCK).bit_length() - 1
        self.remote = self.groups.bit_length() - 1
        self.seq_bits = seq.bit_length() - 1
        self.head_bits = head.bit_length() - 1
        self.bits = self.seq_bits + self.head_bits
        self.near = self.half + sum(self.half >> level for level in range(1, self.local))
        self.lines = 5 + hidden // width
        self.far = BLOCK * self.remote
        cols = width // head
        self.blocks = {
            "down": (hidden // seq, cols),
            "up": (width // seq, hidden // head),
            "out": (width // seq, cols),
            "query": (width // seq, cols),
            "key": (width // seq, cols),
            "value": (width // seq, cols),
        }
        seqs, heads = list(range(self.seq_bits)), list(range(self.seq_bits, self.bits))
        ways = {"core": seqs[:1], "straight": seqs[1:], "back": seqs[:0:-1], "bits": heads, "head": ["head"]}
        ways["quad"] = ["quad"] if len(seqs) == 3 else seqs[1:]
        stages = {name: [b for way in ("core",) + STAGES[name] for b in ways[way]] for name in STAGES}
        rows_down, rows_up, rows_out = hidden // seq, width // seq, width // seq
        self.fine = rows_down % (2 * LANES) == 0
        half_down = rows_down // 2
        if self.fine:
            self.chunks = [
                [(s * rows_down + i * half_down, half_down) for s in range(seq)] for i in range(2)
            ]
        else:
            self.chunks = [[(0, hidden)], []]

        def tall(name, *cuts):
            return [(name, r, r + n, c, c + LANES) for r, n in cuts for c in range(0, self.blocks[name][1], LANES)]

        if self.fine:
            third = half_down // 8 * EIGHTHS
            step = 2 * half_down
            first = [(c, c + half_down) for c in range(0, hidden // head, step)]
            second = [(c + half_down, c + step) for c in range(0, hidden // head, step)]
            lanes = lambda cs: [("up", 0, rows_up, c, c + LANES) for a, b in cs for c in range(a, b, LANES)]
            self.sums = {
                "dna": (tall("down", (0, half_down - third)), stages["dna"]),
                "dnb": (tall("down", (half_down, half_down)), stages["dnb"]),
                "dnc": (tall("down", (half_down - third, third)), stages["dnc"]),
                "upa": (lanes(first), stages["upa"]),
                "upb": (lanes(second), stages["upb"]),
            }
        else:
            self.sums = {
                "dna": (tall("down", (0, rows_down)), stages["dna"]),
                "upb": (tall("up", (0, rows_up)), stages["upb"]),
            }
        self.sums["outa"] = (tall("out", (0, rows_out)), stages["outa"])
        if rows_out % 32 == 0:
            m = rows_out // 2
            self.sums["pa"] = (tall("query", (0, rows_out)) + tall("key", (0, m)), stages["pa"])
            self.sums["pb"] = (tall("key", (m, m)) + tall("value", (0, rows_out)), stages["pb"])
        else:
            self.sums["pa"] = (tall("query", (0, rows_out)) + tall("key", (0, rows_out)), stages["pa"])
            self.sums["pb"] = (tall("value", (0, rows_out)), stages["pb"])

    def sum_shape(self, name):
        return (sum(part[2] - part[1] for part in self.sums[name][0]), LANES)

    def bits_of(self, stage):
        if stage == "head":
            return list(range(self.seq_bits, self.bits))
        return list(range(1, self.seq_bits)) if stage == "quad" else [stage]

    def got_shapes(self, name):
        left, shapes = self.bits, []
        for stage in self.sums[name][1]:
            settled = len(self.bits_of(stage))
            left -= settled
            many = (2**settled - 1,) if isinstance(stage, str) else ()
            shapes.append(many + (2,) * left + self.sum_shape(name))
        return shapes


class Summed:
    def __init__(self, plan, me, name, number, grad, got, send, recv, outs):
        self.plan, self.name, self.number = plan, name, number
        self.s, self.h = me
        self.grad, self.got, self.outs = grad, got, outs
        self.send, self.recv = send, recv
        self.parts, self.order = plan.sums[name]
        self.started, self.stage = [], 0

    def own_bit(self, b):
        n = self.plan.seq_bits
        return bit_of(self.s, b) if b < n else bit_of(self.h, b - n)

    def index(self, fixed, others={}):
        at = []
        for b in reversed(range(self.plan.bits)):
            if b in others:
                at.append(others[b])
            elif b in fixed:
                at.append(self.own_bit(b))
            else:
                at.append(slice(None))
        return tuple(at)

    def put(self, name, s, h, block, row, col):
        owner = s + h * self.plan.seq
        at = tuple((owner >> b) & 1 for b in reversed(range(self.plan.bits)))
        first = 0
        for part, r0, r1, c0, c1 in self.parts:
            if part == name and row <= r0 < row + block.shape[0] and col <= c0 < col + block.shape[1]:
                piece = block[r0 - row : r1 - row, c0 - col : c1 - col]
                self.grad[at + (slice(first, first + r1 - r0),)] = piece.astype(BF)
            first += r1 - r0

    def copy(self, source, target, slot, device):
        copy = pltpu.make_async_remote_copy(
            src_ref=source,
            dst_ref=target,
            send_sem=self.send.at[self.number, slot],
            recv_sem=self.recv.at[self.number, slot],
            device_id=device,
            device_id_type=MESH,
        )
        copy.start()
        self.started.append(copy)
        return copy

    def settled(self, stage):
        return [b for way in self.order[:stage] for b in self.plan.bits_of(way)]

    def start(self, stage):
        way = self.order[stage]
        n, first = self.plan.seq_bits, len(self.started)
        self.arriving = []
        if isinstance(way, str):
            bits = self.plan.bits_of(way)
            base = 1 << bits[0] if way == "quad" else 1
            for k in range(1, 2 ** len(bits)):
                device = (flip(self.s, k * base), self.h) if way == "quad" else (self.s, flip(self.h, k))
                others = {b: bit_of(device[0], b) if b < n else bit_of(device[1], b - n) for b in bits}
                source = self.grad.at[self.index(self.settled(stage), others)]
                self.arriving.append(self.copy(source, self.got[stage].at[k - 1], first + k - 1, device))
            return
        b = way
        device = (flip(self.s, 1 << b), self.h) if b < n else (self.s, flip(self.h, 1 << (b - n)))
        source = self.grad.at[self.index(self.settled(stage), {b: 1 - self.own_bit(b)})]
        self.arriving.append(self.copy(source, self.got[stage], first, device))

    def finish(self, stage):
        arriving = self.arriving
        for copy in arriving:
            copy.wait_recv()
        got = self.got[stage]
        pieces = [got.at[k] for k in range(len(arriving))] if len(arriving) > 1 else [got]
        at = self.index(self.settled(stage + 1))
        if stage + 1 == len(self.order):
            total = self.grad[at].astype(F32)
            for piece in pieces:
                total = total + piece[...].astype(F32)
            first = 0
            for part, r0, r1, c0, c1 in self.parts:
                self.outs[part][r0:r1, c0:c1] = total[first : first + r1 - r0]
                first += r1 - r0
            return
        combos = [()]
        for a in at:
            if isinstance(a, slice):
                combos = [c + (i,) for c in combos for i in range(2)]
        for combo in combos:
            left = list(combo)
            full = tuple(left.pop(0) if isinstance(a, slice) else a for a in at)
            if len(pieces) == 1:
                self.grad[full] = self.grad[full] + pieces[0][combo]
                continue
            total = self.grad[full].astype(F32)
            for piece in pieces:
                total = total + piece[combo].astype(F32)
            self.grad[full] = total.astype(BF)

    def step(self):
        if self.stage:
            self.finish(self.stage - 1)
        if self.stage < len(self.order):
            self.start(self.stage)
        self.stage += 1

    @property
    def done(self):
        return self.stage > len(self.order)

    def drain(self):
        for copy in self.started:
            copy.wait_send()


def layer_kernel(plan, *refs):
    refs = list(refs)

    def take(n):
        taken = refs[:n]
        del refs[:n]
        return taken

    x_in, dy_in, *lines_in = take(8)
    weights_in = take(6)
    lo_out, ig_out = take(2)
    grads_out = dict(zip(plan.blocks, take(6)))
    lines_out = take(6)
    xg, dyg, log, igg = take(4)
    wq, wk, wv, wo, wu, wd = weights = take(6)
    gain_one, shift_one, gain_two, shift_two, up_bias, down_bias = lines = take(6)
    norm_t, norm_b, n_one, rs_one, n_two, rs_two, norm_two_b, residual, d_residual = take(9)
    qs, kn, vn, kf, vf, near_values = take(6)
    pn, pf, stats, mask, mixed_t = take(5)
    act_ref, hid_ref, cdf_ref, dh_ref = take(4)
    dos, dq_t, dk_ref, dv_ref, far_ref, bar_t, d_norm_one = take(7)
    c_send, c_got, c_half, c_half_got, bar_send, bar_got, d_send, d_got, d_half, d_half_got, far_parts = take(11)
    sums = {}
    for name in plan.sums:
        grad, *got = take(1 + len(plan.sums[name][1]))
        sums[name] = (grad, got)
    vec_bufs, vec_got, vec_own, vec_own_got = take(4)
    send_a, recv_a, send_r, recv_r, send_s, recv_s, here = take(7)
    assert not refs

    seq, head, rows, width, tokens = plan.seq, plan.head, plan.rows, plan.width, plan.tokens
    half, near, far = plan.half, plan.near, plan.far
    s, h = lax.axis_index("seq"), lax.axis_index("head")
    c, g = irem(s, plan.minor), idiv(s, plan.minor)
    j = c * head + h

    def group_peer(k):
        other = flip(j, k)
        return other, (g * plan.minor + idiv(other, head), irem(other, head))

    def row_peer(k):
        other = flip(g, k)
        return other, (other * plan.minor + c, h)

    barrier = pltpu.get_barrier_semaphore()
    peers = [group_peer(k)[1] for k in range(1, rows)] + [row_peer(k)[1] for k in range(1, plan.groups)]
    for device in peers:
        pl.semaphore_signal(barrier, inc=1, device_id=device, device_id_type=MESH)

    small = [pltpu.make_async_copy(a, b, here.at[10 + i]) for i, (a, b) in enumerate(zip(lines_in, lines))]
    for copy in small:
        copy.start()
    loads = [pltpu.make_async_copy(a, b, here.at[i]) for i, (a, b) in enumerate(zip(weights_in, weights))]
    for i in (1, 2, 0, 3, 4, 5):
        loads[i].start()
    own = [
        pltpu.make_async_copy(x_in.at[j], xg.at[j], here.at[6]),
        pltpu.make_async_copy(dy_in.at[j], dyg.at[j], here.at[7]),
    ]
    for copy in own:
        copy.start()

    i_k = lax.broadcasted_iota(jnp.int32, (near, 2 * half), 0)
    i_q = lax.broadcasted_iota(jnp.int32, (near, 2 * half), 1) & (half - 1)
    valid = (i_k < half) & ((i_q >> 5) == (i_k >> 5))
    first = half
    for level in range(1, plan.local - 1):
        count = half >> level
        mine = (i_k >= first) & (i_k < first + count)
        valid = valid | (mine & (((i_q >> (4 + level)) ^ 1) == ((i_k - first) >> 4)))
        first += count
    valid = valid | (i_k >= first)
    mask[...] = jnp.where(valid, 0.0, -1e30).astype(F32)

    pl.semaphore_wait(barrier, len(peers))

    def exchange(number, source, target):
        copies = []
        for k in sorted(range(1, rows), key=lambda k: -(k % head)):
            other, device = group_peer(k)
            copy = pltpu.make_async_remote_copy(
                src_ref=source.at[other],
                dst_ref=target.at[j],
                send_sem=send_a.at[number, k],
                recv_sem=recv_a.at[number, k],
                device_id=device,
                device_id_type=MESH,
            )
            copy.start()
            copies.append(copy)
        return copies

    x_copies = exchange(0, x_in, xg)

    def norm_stats(values):
        center = values - jnp.mean(values, axis=-1, keepdims=True)
        spread = jnp.mean(center * center, axis=-1, keepdims=True)
        scale = lax.rsqrt(spread + EPSILON)
        return center * scale, scale

    def norm_back(d_norm, n, scale, gain):
        weighted = d_norm * gain
        return scale * (
            weighted
            - jnp.mean(weighted, axis=-1, keepdims=True)
            - n * jnp.mean(weighted * n, axis=-1, keepdims=True)
        )

    lane = lax.broadcasted_iota(jnp.int32, (1, PAIR), 1)
    low = lane < DH

    def stack_heads(ref, value):
        for p in range(plan.pairs):
            for a in range(2):
                part = value[a * half : (a + 1) * half, p * PAIR : (p + 1) * PAIR]
                zero = jnp.zeros_like(part)
                ref[p, a, :half, :] = jnp.where(low, part, zero)
                ref[p, a, half:, :] = jnp.where(low, zero, part)

    for copy in small:
        copy.wait()
    own[0].wait()
    near_first = x_copies[::-1]
    for copy in near_first[:-2]:
        copy.wait_recv()
    dy_copies = exchange(1, dy_in, dyg)
    for copy in near_first[-2:]:
        copy.wait_recv()
    x = xg[...].reshape(tokens, width).astype(F32)
    n, scale = norm_stats(x)
    n_one[...] = n
    rs_one[...] = scale
    normed = (n * gain_one[...] + shift_one[...]).astype(BF)

    loads[1].wait()
    loads[2].wait()
    level = jnp.concatenate([dot(normed, wk[...]).astype(BF), dot(normed, wv[...]).astype(BF)], axis=1)

    def columns(index, p):
        return slice(index * width + p * PAIR, index * width + (p + 1) * PAIR)

    targets = (kn, vn)
    first = 0
    for l in range(plan.local):
        if l:
            level = dot(pair_mean(level.shape[0]), level).astype(BF)
        count = level.shape[0] // 2
        for index, ref in enumerate(targets):
            for p in range(plan.pairs):
                for a in range(2):
                    b = a if l + 1 < plan.local else 1 - a
                    ref[p, b, first : first + count, :] = level[a * count : (a + 1) * count, columns(index, p)]
        first += count
    level = dot(pair_mean(level.shape[0]), level).astype(BF)
    c_send[0] = level[:, :width]
    c_send[1] = level[:, width:]
    level = dot(pair_mean(level.shape[0]), level).astype(BF)
    c_half[: BLOCK // 2, :] = level[:, :width]
    c_half[BLOCK // 2 :, :] = level[:, width:]
    c_copies = []
    for k in range(1, plan.groups):
        other, device = row_peer(k)
        copy = pltpu.make_async_remote_copy(
            src_ref=c_send if k == 1 else c_half,
            dst_ref=c_got if k == 1 else c_half_got.at[g],
            send_sem=send_r.at[0, k],
            recv_sem=recv_r.at[0, k],
            device_id=device,
            device_id_type=MESH,
        )
        copy.start()
        c_copies.append(copy)

    loads[0].wait()
    stack_heads(qs, (dot(normed, wq[...]) * (DH**-0.5)).astype(BF))
    norm_b[...] = normed

    def attend_near(p):
        scores = jnp.concatenate([dot_t(kn[p, a], qs[p, a]) + mask[...] for a in range(2)], axis=1)
        top = jnp.max(scores, axis=0, keepdims=True)
        raised = jnp.exp(scores - top)
        at = slice(2 * p * tokens, (2 * p + 2) * tokens)
        stats[0:1, at] = top
        stats[1:2, at] = jnp.sum(raised, axis=0, keepdims=True)
        for a in range(2):
            part = raised[:, a * tokens : (a + 1) * tokens]
            pn[p, a] = part
            near_values[p, a] = t_dot(vn[p, a], part.astype(BF))

    for p in range(plan.pairs):
        attend_near(p)

    for copy in c_copies:
        copy.wait_recv()

    def sibling(b):
        upper = idiv(g, 1 << b)
        return (upper + 1 - 2 * irem(upper, 2)) * (1 << b)

    for b in range(plan.remote):
        for index in range(2):
            if b == 0:
                level = c_got[index]
            else:
                count = 1 << b
                both_kinds = c_half_got[pl.ds(sibling(b), count)].reshape(BLOCK * count, width)
                i_r = lax.broadcasted_iota(jnp.int32, (BLOCK * count // 2, BLOCK * count), 0)
                i_s = lax.broadcasted_iota(jnp.int32, (BLOCK * count // 2, BLOCK * count), 1)
                own_rows = (i_r >> 3) * BLOCK + index * (BLOCK // 2) + (i_r & 7) == i_s
                level = dot(jnp.where(own_rows, 1.0, 0.0).astype(BF), both_kinds).astype(BF)
                for _ in range(b - 1):
                    level = dot(pair_mean(level.shape[0]), level).astype(BF)
            for p in range(plan.pairs):
                part = level[:, p * PAIR : (p + 1) * PAIR]
                (kf, vf)[index][p, b * BLOCK : (b + 1) * BLOCK, :] = part

    halves = [(p, a) for p in range(plan.pairs) for a in range(2)]
    scores = jnp.concatenate([dot_t(kf[p], qs[p, a]) for p, a in halves], axis=1)
    top_near = stats[0:1, :]
    top = jnp.maximum(top_near, jnp.max(scores, axis=0, keepdims=True))
    shrink = jnp.exp(top_near - top)
    raised = jnp.exp(scores - top)
    share = 1.0 / (stats[1:2, :] * shrink + jnp.sum(raised, axis=0, keepdims=True))
    near_share = shrink * share
    stats[2:3, :] = near_share
    prob = raised * share
    pf[...] = prob
    prob = prob.astype(BF)
    for i, (p, a) in enumerate(halves):
        at = slice(i * tokens, (i + 1) * tokens)
        mixed = near_values[p, a] * near_share[:, at] + t_dot(vf[p], prob[:, at])
        mixed_t[p, :DH, a * half : (a + 1) * half] = mixed[:DH, :half].astype(BF)
        mixed_t[p, DH:, a * half : (a + 1) * half] = mixed[DH:, half:].astype(BF)

    loads[3].wait()
    res = xg[...].reshape(tokens, width).astype(F32) + t_dot(mixed_t[...].reshape(width, tokens), wo[...])
    residual[...] = res
    n, scale = norm_stats(res)
    n_two[...] = n
    rs_two[...] = scale
    norm_two_b[...] = (n * gain_two[...] + shift_two[...]).astype(BF)

    row = lambda a: jnp.sum(a, axis=0, keepdims=True)
    per = plan.hidden // width

    def put_block(name, block, first_row, first_col):
        r, w = plan.blocks[name]
        row_step, col_step = min(r, block.shape[0]), min(w, block.shape[1])
        for a in range(0, block.shape[0], row_step):
            for b in range(0, block.shape[1], col_step):
                s_at, h_at = (first_row + a) // r, (first_col + b) // w
                piece = block[a : a + row_step, b : b + col_step]
                for item in items.values():
                    if item is not vec_sum:
                        item.put(name, s_at, h_at, piece, (first_row + a) % r, (first_col + b) % w)

    class Vectors:
        def __init__(self):
            self.stage, self.started = 0, []

        def copy(self, source, target, slot, device):
            copy = pltpu.make_async_remote_copy(
                src_ref=source,
                dst_ref=target,
                send_sem=send_s.at[len(plan.sums), slot],
                recv_sem=recv_s.at[len(plan.sums), slot],
                device_id=device,
                device_id_type=MESH,
            )
            copy.start()
            self.started.append(copy)

        def step(self):
            n, k = plan.seq_bits, self.stage
            if 0 < k <= n:
                self.started[k - 1].wait_recv()
                vec_bufs[k] = vec_bufs[k - 1] + vec_got[k - 1]
            if k < n:
                self.copy(vec_bufs.at[k], vec_got.at[k], k, (flip(s, 1 << k), h))
            elif k == n:
                vec = vec_bufs[n]
                part = own_part(vec[:8])
                vec_own[:, : part.shape[1]] = part
                part = own_part(jnp.concatenate([vec[5 + i : 6 + i] for i in range(per)], axis=1))
                vec_own[5:6, : part.shape[1]] = part
                for i in range(1, head):
                    self.copy(vec_own, vec_own_got.at[i - 1], n + i - 1, (s, flip(h, i)))
            else:
                values = [vec_own[...]]
                for i in range(1, head):
                    self.started[n + i - 1].wait_recv()
                    values.append(vec_own_got[i - 1])
                while len(values) > 1:
                    values = [values[i] + values[i + 1] for i in range(0, len(values), 2)]
                for i, line in enumerate(lines_out):
                    line[...] = values[0][i, : line.shape[0]]
            self.stage += 1

        @property
        def done(self):
            return self.stage > plan.seq_bits + 1

        def drain(self):
            for copy in self.started:
                copy.wait_send()

    def own_part(line):
        share = line.shape[1] // seq
        part = line[:, :share]
        for other in range(1, seq):
            part = jnp.where(s == other, line[:, other * share : (other + 1) * share], part)
        return part

    vec_sum = Vectors()
    items = {
        name: Summed(plan, (s, h), name, i, grad, got, send_s, recv_s, grads_out)
        for i, (name, (grad, got)) in enumerate(sums.items())
    }
    items["vec"] = vec_sum

    def cotangent():
        return dyg[...].reshape(tokens, width)

    def blocks_of(chunk):
        at, blocks = 0, []
        for start, length in plan.chunks[chunk]:
            for f in range(start, start + length, 512):
                n = min(512, start + length - f)
                if not blocks or blocks[-1][1] + n > 512:
                    blocks.append([[], 0, at])
                blocks[-1][0].append((f, n))
                blocks[-1][1] += n
                at += n
        return [(segments, slice(first, first + n)) for segments, n, first in blocks]

    def columns_of(ref, segments):
        return jnp.concatenate([ref[:, f : f + n] for f, n in segments], axis=1)

    def rows_of(ref, segments):
        return jnp.concatenate([ref[f : f + n, :] for f, n in segments], axis=0)

    flat = [(chunk, *block) for chunk in range(2) for block in blocks_of(chunk)]
    quarters = [flat[i : i + 1] for i in range(4)] if plan.fine else [flat, [], [], []]

    def activate(quarter):
        if quarter == 0:
            loads[4].wait()
        for chunk, segments, at in quarters[quarter]:
            hid = dot(norm_two_b[...], columns_of(wu, segments)) + columns_of(up_bias, segments)
            cdf = 0.5 * (1.0 + lax.erf(hid * (0.5**0.5)))
            act = (hid * cdf).astype(BF)
            act_ref[chunk, :, at] = act
            hid_ref[chunk, :, at] = hid
            cdf_ref[chunk, :, at] = cdf

    def down_grad(quarter):
        if quarter == 0:
            loads[5].wait()
            own[1].wait()
            for copy in dy_copies:
                copy.wait_recv()
        for chunk, segments, at in quarters[quarter]:
            grad = t_dot(act_ref[chunk, :, at], cotangent())
            first = 0
            for f, n in segments:
                put_block("down", grad[first : first + n], f, 0)
                first += n

    def deactivate(quarter):
        for chunk, segments, at in quarters[quarter]:
            hid = hid_ref[chunk, :, at]
            slope = cdf_ref[chunk, :, at] + hid * (jnp.exp(-0.5 * hid * hid) * 0.3989422804014327)
            dh = (dot_t(cotangent(), rows_of(wd, segments)) * slope).astype(BF)
            dh_ref[chunk, :, at] = dh
            sums_dh = row(dh.astype(F32))
            grad = t_dot(norm_two_b[...], dh)
            first = 0
            for f, n in segments:
                for o in range(0, n, min(n, width)):
                    line, lane_at = divmod(f + o, width)
                    m = min(n, width)
                    vec_bufs[0, 5 + line : 6 + line, lane_at : lane_at + m] = sums_dh[:, first + o : first + o + m]
                put_block("up", grad[:, first : first + n], 0, f)
                first += n

    def both(ref, weight, product, pick):
        total = None
        for chunk in range(2):
            for segments, at in blocks_of(chunk):
                term = product(ref[chunk, :, at], pick(weight, segments))
                total = term if total is None else total + term
        return total

    def second_norm_back():
        d_norm_two = both(dh_ref, wu, dot_t, columns_of)
        n = n_two[...]
        dy_f = cotangent().astype(F32)
        vec_bufs[0, 2:3, :] = row(d_norm_two * n)
        vec_bufs[0, 3:4, :] = row(d_norm_two)
        vec_bufs[0, 4:5, :] = row(dy_f)
        d_residual[...] = dy_f + norm_back(d_norm_two, n, rs_two[...], gain_two[...])

    def out_grad():
        put_block("out", dot(mixed_t[...].reshape(width, tokens), d_residual[...].astype(BF)), 0, 0)

    def mixed_back():
        stack_heads(dos, dot_t(d_residual[...].astype(BF), wo[...]).astype(BF))

    def layer_output():
        result = residual[...] + both(act_ref, wd, dot, rows_of) + down_bias[...]
        log[...] = result.astype(BF).reshape(rows, plan.pos, width)

    late_copies, own_late = [], []

    def send_layer_output():
        late_copies.extend(exchange(2, log, lo_out))
        own_late.append(pltpu.make_async_copy(log.at[j], lo_out.at[j], here.at[8]))
        own_late[-1].start()

    def spread_matrix():
        i_t = lax.broadcasted_iota(jnp.int32, (half, near - half), 0)
        i_c = lax.broadcasted_iota(jnp.int32, (half, near - half), 1)
        spread = jnp.zeros((half, near - half), F32)
        first = 0
        for level in range(1, plan.local):
            spread = spread + jnp.where((i_t >> level) == (i_c - first), 0.5**level, 0.0)
            first += half >> level
        return spread.astype(BF)

    def attend_back(p):
        spread = spread_matrix()
        dk, dv, dk_far, dv_far = [], [], 0.0, 0.0
        k_far, v_far = kf[p], vf[p]
        for a in range(2):
            at = slice((2 * p + a) * tokens, (2 * p + a + 1) * tokens)
            q, do = qs[p, a], dos[p, a]
            prob, prob_far = pn[p, a] * stats[2:3, at], pf[:, at]
            d_prob = dot_t(vn[p, a], do)
            d_prob_far = dot_t(v_far, do)
            inner = row(prob * d_prob) + row(prob_far * d_prob_far)
            d_scores = (prob * (d_prob - inner)).astype(BF)
            d_scores_far = (prob_far * (d_prob_far - inner)).astype(BF)
            dk.append(dot(d_scores, q))
            dv.append(dot(prob.astype(BF), do))
            dk_far = dk_far + dot(d_scores_far, q)
            dv_far = dv_far + dot(prob_far.astype(BF), do)
            dq = (t_dot(kn[p, a], d_scores) + t_dot(k_far, d_scores_far)) * (DH**-0.5)
            dq_t[p, :DH, a * half : (a + 1) * half] = dq[:DH, :half].astype(BF)
            dq_t[p, DH:, a * half : (a + 1) * half] = dq[DH:, half:].astype(BF)
        other = near - BLOCK
        for index, (total, total_far, ref) in enumerate(((dk, dk_far, dk_ref), (dv, dv_far, dv_ref))):
            for a in range(2):
                coarse = jnp.concatenate([total[a][half:other], total[1 - a][other:]], axis=0)
                ref[p, a * half : (a + 1) * half, :] = total[a][:half] + two_part_dot(spread, coarse)
            far_ref[index, p] = total_far

    d_copies = []

    def send_far():
        i_a = lax.broadcasted_iota(jnp.int32, (BLOCK, BLOCK), 0)
        i_b = lax.broadcasted_iota(jnp.int32, (BLOCK, BLOCK), 1)
        for k in range(1, plan.groups):
            other, device = row_peer(k)
            b = k.bit_length() - 1
            offset = irem(other, 1 << b)
            for index in range(2):
                for p in range(plan.pairs):
                    level = far_ref[index, p, BLOCK * b : BLOCK * (b + 1), :].astype(BF)
                    if b == 0:
                        d_send[index, p] = level
                        continue
                    rows_at = (offset * (BLOCK // 2) + (i_a & 7)) >> (b - 1)
                    pick = jnp.where((rows_at == i_b) & ((i_a >> 3) == index), 0.5**b, 0.0).astype(BF)
                    part = dot(pick, level)
                    if index == 0:
                        far_parts[p] = part
                    else:
                        d_half[k, p] = (far_parts[p] + part).astype(BF)
            copy = pltpu.make_async_remote_copy(
                src_ref=d_send if k == 1 else d_half.at[k],
                dst_ref=d_got if k == 1 else d_half_got.at[k],
                send_sem=send_r.at[1, k],
                recv_sem=recv_r.at[1, k],
                device_id=device,
                device_id_type=MESH,
            )
            copy.start()
            d_copies.append(copy)

    def part_grads():
        put_block("query", dot_t(norm_t[...], dq_t[...].reshape(width, tokens)), 0, 0)
        for index, (ref, name) in enumerate(((dk_ref, "key"), (dv_ref, "value"))):
            mine = jnp.concatenate([ref[p].astype(BF) for p in range(plan.pairs)], axis=1)
            made = jnp.concatenate([far_ref[index, p].astype(BF) for p in range(plan.pairs)], axis=1)
            put_block(name, dot(norm_t[...], mine) + dot(bar_t[...], made), 0, 0)

    bar_copies = []

    def send_bars():
        i_a = lax.broadcasted_iota(jnp.int32, (BLOCK, tokens), 0)
        i_b = lax.broadcasted_iota(jnp.int32, (BLOCK, tokens), 1)
        mean_all = jnp.where((i_b >> plan.local) == i_a, 0.5**plan.local, 0.0).astype(BF)
        bar_send[...] = dot(mean_all, norm_b[...]).astype(BF)
        for k in range(1, plan.groups):
            other, device = row_peer(k)
            copy = pltpu.make_async_remote_copy(
                src_ref=bar_send,
                dst_ref=bar_got.at[g],
                send_sem=send_r.at[2, k],
                recv_sem=recv_r.at[2, k],
                device_id=device,
                device_id_type=MESH,
            )
            copy.start()
            bar_copies.append(copy)

    def take_bars():
        norm_t[...] = turned(norm_b[...])
        for copy in bar_copies:
            copy.wait_recv()
        for b in range(plan.remote):
            level = bar_got[pl.ds(sibling(b), 1 << b)].reshape(BLOCK << b, width)
            for _ in range(b):
                level = dot(pair_mean(level.shape[0]), level).astype(BF)
            bar_t[:, b * BLOCK : (b + 1) * BLOCK] = turned(level)

    def query_back():
        d_norm_one[...] = dot_t(turned(dq_t[...].reshape(width, tokens)), wq[...])

    def take_far():
        for copy in d_copies:
            copy.wait_recv()

    def first_norm_back():
        i_t = lax.broadcasted_iota(jnp.int32, (tokens, BLOCK), 0)
        i_c = lax.broadcasted_iota(jnp.int32, (tokens, BLOCK), 1)
        last = jnp.where((i_t >> plan.local) == i_c, 0.5**plan.local, 0.0).astype(BF)
        half_of = [
            jnp.where((i_t >> (plan.local + 1)) == i_c - (BLOCK // 2) * i, 0.5**plan.local, 0.0).astype(BF)
            for i in range(2)
        ]
        d_normed = d_norm_one[...]
        for index, (ref, w) in enumerate(((dk_ref, wk), (dv_ref, wv))):
            pieces = []
            for p in range(plan.pairs):
                total = ref[p] + dot(last, d_got[index, p])
                if plan.groups > 2:
                    coarse = d_half_got[2, p].astype(F32)
                    for k in range(3, plan.groups):
                        coarse = coarse + d_half_got[k, p].astype(F32)
                    total = total + two_part_dot(half_of[index], coarse)
                pieces.append(total.astype(BF))
            d_normed = d_normed + dot_t(jnp.concatenate(pieces, axis=1), w[...])
        n = n_one[...]
        vec_bufs[0, 0:1, :] = row(d_normed * n)
        vec_bufs[0, 1:2, :] = row(d_normed)
        d_first = norm_back(d_normed, n, rs_one[...], gain_one[...])
        igg[...] = (d_residual[...] + d_first).astype(BF).reshape(rows, plan.pos, width)

    def send_input_grad():
        late_copies.extend(exchange(3, igg, ig_out))
        own_late.append(pltpu.make_async_copy(igg.at[j], ig_out.at[j], here.at[9]))
        own_late[-1].start()

    vec_own[...] = jnp.zeros_like(vec_own)
    work = {
        **{f"f1{i}": functools.partial(activate, i) for i in range(4)},
        **{f"g1{i}": functools.partial(down_grad, i) for i in range(4)},
        **{f"f2{i}": functools.partial(deactivate, i) for i in range(4)},
        "ln2b": second_norm_back,
        "outg": out_grad,
        "lo": layer_output,
        "Alo": send_layer_output,
        "dmix": mixed_back,
        "Abar": send_bars,
        "bar": take_bars,
        "dsend": send_far,
        "qkvg": part_grads,
        "dnq": query_back,
        "Wd": take_far,
        "ln1b": first_norm_back,
        "Aig": send_input_grad,
    }
    first_pairs = {f"ab{i}": range(i, plan.pairs, 4) for i in range(4)}
    for name in ORDER:
        if name in work:
            work[name]()
        elif name in first_pairs:
            for p in first_pairs[name]:
                attend_back(p)
        elif name in items:
            items[name].step()
    while not all(item.done for item in items.values()):
        for item in items.values():
            if not item.done:
                item.step()

    for copy in late_copies:
        copy.wait_recv()
    for copy in own_late:
        copy.wait()
    for copy in x_copies + dy_copies + c_copies + bar_copies + d_copies + late_copies:
        copy.wait_send()
    for item in items.values():
        item.drain()


def place_kernel(*refs):
    count = len(refs) // 2
    ins, outs, sems = refs[:count], refs[count:-1], refs[-1]
    copies = [pltpu.make_async_copy(a, b, sems.at[i]) for i, (a, b) in enumerate(zip(ins, outs))]
    for copy in copies:
        copy.start()
    for copy in copies:
        copy.wait()


def body(
    inputs,
    gain_first,
    shift_first,
    query_weight,
    key_weight,
    value_weight,
    out_weight,
    gain_second,
    shift_second,
    up_weight,
    up_bias,
    down_weight,
    down_bias,
    cotangent,
):
    rows, pos, width = inputs.shape
    hidden = up_weight.shape[1]
    plan = Plan(lax.axis_size("seq"), lax.axis_size("head"), rows, pos, width, hidden)
    tokens, pairs, groups, half, near, far = plan.tokens, plan.pairs, plan.groups, plan.half, plan.near, plan.far
    vmem = pl.BlockSpec(memory_space=pltpu.VMEM)
    anywhere = pl.BlockSpec(memory_space=pl.ANY)
    names = list(plan.blocks)

    def buf(*shape, dtype=BF):
        return pltpu.VMEM(shape, dtype)

    scratch = [buf(rows, pos, width)] * 4
    scratch += [buf(width, width)] * 4 + [buf(width, hidden), buf(hidden, width)]
    scratch += [buf(1, n, dtype=F32) for n in (width, width, width, width, hidden, width)]
    scratch += [
        buf(width, tokens),
        buf(tokens, width),
        buf(tokens, width, dtype=F32),
        buf(tokens, 1, dtype=F32),
        buf(tokens, width, dtype=F32),
        buf(tokens, 1, dtype=F32),
        buf(tokens, width),
        buf(tokens, width, dtype=F32),
        buf(tokens, width, dtype=F32),
    ]
    scratch += [
        buf(pairs, 2, tokens, PAIR),
        buf(pairs, 2, near, PAIR),
        buf(pairs, 2, near, PAIR),
        buf(pairs, far, PAIR),
        buf(pairs, far, PAIR),
        buf(pairs, 2, PAIR, tokens, dtype=F32),
    ]
    scratch += [
        buf(pairs, 2, near, tokens, dtype=F32),
        buf(far, 2 * pairs * tokens, dtype=F32),
        buf(8, 2 * pairs * tokens, dtype=F32),
        buf(near, tokens, dtype=F32),
        buf(pairs, PAIR, tokens),
    ]
    part = sum(n for _, n in plan.chunks[0])
    scratch += [buf(2, tokens, part)] + [buf(2, tokens, part, dtype=F32)] * 2 + [buf(2, tokens, part)]
    scratch += [
        buf(pairs, 2, tokens, PAIR),
        buf(pairs, PAIR, tokens),
        buf(pairs, tokens, PAIR, dtype=F32),
        buf(pairs, tokens, PAIR, dtype=F32),
        buf(2, pairs, BLOCK * plan.remote, PAIR, dtype=F32),
        buf(width, BLOCK * plan.remote),
        buf(tokens, width, dtype=F32),
    ]
    scratch += [
        buf(2, BLOCK, width),
        buf(2, BLOCK, width),
        buf(BLOCK, width),
        buf(groups, BLOCK, width),
        buf(BLOCK, width),
        buf(groups, BLOCK, width),
        buf(2, pairs, BLOCK, PAIR),
        buf(2, pairs, BLOCK, PAIR),
        buf(groups, pairs, BLOCK, PAIR),
        buf(groups, pairs, BLOCK, PAIR),
        buf(pairs, BLOCK, PAIR, dtype=F32),
    ]
    for name in plan.sums:
        scratch += [buf(*(2,) * plan.bits, *plan.sum_shape(name))]
        scratch += [buf(*shape) for shape in plan.got_shapes(name)]
    slots = plan.bits + plan.head
    share = max(width, hidden) // plan.seq
    scratch += [
        buf(plan.seq_bits + 1, plan.lines, width, dtype=F32),
        buf(plan.seq_bits, plan.lines, width, dtype=F32),
        buf(8, share, dtype=F32),
        buf(plan.head - 1, 8, share, dtype=F32),
    ]
    dma = pltpu.SemaphoreType.DMA
    scratch += [dma((4, rows)), dma((4, rows)), dma((3, groups)), dma((3, groups))]
    scratch += [dma((len(plan.sums) + 1, slots)), dma((len(plan.sums) + 1, slots)), dma((16,))]

    line = lambda a: a.reshape(1, -1)
    big = [jax.ShapeDtypeStruct(inputs.shape, BF)] * 2 + [jax.ShapeDtypeStruct(plan.blocks[n], F32) for n in names]
    lines = [jax.ShapeDtypeStruct((width // plan.seq,), F32)] * 5 + [jax.ShapeDtypeStruct((hidden // plan.seq,), F32)]
    results = pl.pallas_call(
        functools.partial(layer_kernel, plan),
        out_shape=[pltpu.VMEM(o.shape, o.dtype) for o in big + lines],
        in_specs=[anywhere] * 14,
        out_specs=[vmem] * 14,
        scratch_shapes=scratch,
        compiler_params=pltpu.CompilerParams(
            collective_id=0, has_side_effects=True, vmem_limit_bytes=56 << 20
        ),
        name="layer",
    )(
        inputs,
        cotangent,
        line(gain_first),
        line(shift_first),
        line(gain_second),
        line(shift_second),
        line(up_bias),
        line(down_bias),
        query_weight,
        key_weight,
        value_weight,
        out_weight,
        up_weight,
        down_weight,
    )
    placed = pl.pallas_call(
        place_kernel,
        out_shape=big + lines,
        in_specs=[vmem] * 14,
        out_specs=[anywhere] * 14,
        scratch_shapes=[dma((14,))],
        name="place",
    )(*[pltpu.with_memory_space_constraint(r, pltpu.VMEM) for r in results])
    layer_out, input_grad, down_g, up_g, out_g, query_g, key_g, value_g = placed[:8]
    gain_one_g, shift_one_g, gain_two_g, shift_two_g, down_bias_g, up_bias_g = placed[8:]
    return (
        layer_out,
        input_grad,
        gain_one_g,
        shift_one_g,
        query_g,
        key_g,
        value_g,
        out_g,
        gain_two_g,
        shift_two_g,
        up_g,
        up_bias_g,
        down_g,
        down_bias_g,
    )


def solution(mesh):
    placed = (P(None, ("seq", "head"), None),) + (P(),) * 12 + (P(None, ("seq", "head"), None),)
    return jax.shard_map(
        body,
        mesh=mesh,
        in_specs=placed,
        out_specs=(
            P(None, ("seq", "head"), None),
            P(None, ("seq", "head"), None),
            P("seq"),
            P("seq"),
            P("seq", "head"),
            P("seq", "head"),
            P("seq", "head"),
            P("seq", "head"),
            P("seq"),
            P("seq"),
            P("seq", "head"),
            P("seq"),
            P("seq", "head"),
            P("seq"),
        ),
        check_vma=False,
    )
```

```python
import functools

import jax
import jax.numpy as jnp
from jax import lax
from jax.experimental import pallas as pl
from jax.experimental.pallas import tpu as pltpu
from jax.sharding import PartitionSpec as P

MESH = pl.DeviceIdType.MESH
BF = jnp.bfloat16
F32 = jnp.float32
DH = 64
BLOCK = 16
EPSILON = 1e-05
PAIR = 2 * DH
LANES = 128
ORDER = (
    "f10", "f13", "f11", "g10", "g11", "dnc", "f12", "g12", "g13", "dnb", "f21", "dnc", "Abar", "dna", "f20",
    "dnb", "upa", "f23", "dna", "f22", "lo", "upb", "upa", "Alo", "ln2b", "dmix", "ab3", "outg", "upb",
    "outa", "ab0", "outa", "ab2", "ab1", "dnc", "dnb", "bar", "dnq", "qkvg", "dsend", "pb", "pb", "pa", "upa",
    "pa", "outa", "upb", "dnb", "Wd", "ln1b", "Aig", "vec", "dnb", "upa", "vec", "dna", "pb", "upb", "outa",
    "pa", "vec", "pb", "dnc", "dna", "pa", "vec", "upa", "pb", "dna", "dnb", "dnc", "upb", "outa", "pa",
    "dna", "dnc", "pb", "upa", "vec", "outa", "pa",
)
STAGES = {
    "dna": ("straight", "bits"),
    "dnb": ("back", "bits"),
    "dnc": ("bits", "straight"),
    "upa": ("straight", "bits"),
    "upb": ("back", "head"),
    "outa": ("bits", "back"),
    "pa": ("back", "bits"),
    "pb": ("straight", "bits"),
}
EIGHTHS = 6


def idiv(value, k):
    return lax.div(value, jnp.int32(k))


def irem(value, k):
    return lax.rem(value, jnp.int32(k))


def bit_of(value, b):
    return irem(idiv(value, 1 << b), 2)


def flip(value, k):
    b = 0
    while k >> b:
        if (k >> b) & 1:
            value = value + (1 - 2 * bit_of(value, b)) * (1 << b)
        b += 1
    return value


def dot(a, b):
    return jnp.dot(a, b, preferred_element_type=F32)


def dot_t(a, b):
    return lax.dot_general(a, b, (((1,), (1,)), ((), ())), preferred_element_type=F32)


def t_dot(a, b):
    return lax.dot_general(a, b, (((0,), (0,)), ((), ())), preferred_element_type=F32)


def two_part_dot(a, b):
    high = b.astype(BF)
    low = (b - high.astype(F32)).astype(BF)
    return dot(a, high) + dot(a, low)


def pair_mean(rows):
    i = lax.broadcasted_iota(jnp.int32, (rows // 2, rows), 0)
    j = lax.broadcasted_iota(jnp.int32, (rows // 2, rows), 1)
    return jnp.where((j >> 1) == i, 0.5, 0.0).astype(BF)


def identity(n):
    i = lax.broadcasted_iota(jnp.int32, (n, n), 0)
    j = lax.broadcasted_iota(jnp.int32, (n, n), 1)
    return jnp.where(i == j, 1.0, 0.0).astype(BF)


def turned(value):
    n = PAIR
    parts = [
        dot_t(identity(n), value[:, i : i + n]).astype(BF) for i in range(0, value.shape[1], n)
    ]
    return parts[0] if len(parts) == 1 else jnp.concatenate(parts, axis=0)


class Plan:
    def __init__(self, seq, head, rows, pos, width, hidden):
        self.seq, self.head, self.rows, self.pos, self.width, self.hidden = seq, head, rows, pos, width, hidden
        self.minor = rows // head
        self.groups = seq // self.minor
        self.tokens = rows * pos
        self.half = self.tokens // 2
        self.pairs = width // PAIR
        self.local = (self.tokens // BLOCK).bit_length() - 1
        self.remote = self.groups.bit_length() - 1
        self.seq_bits = seq.bit_length() - 1
        self.head_bits = head.bit_length() - 1
        self.bits = self.seq_bits + self.head_bits
        self.near = self.half + sum(self.half >> level for level in range(1, self.local))
        self.lines = 5 + hidden // width
        self.far = BLOCK * self.remote
        cols = width // head
        self.blocks = {
            "down": (hidden // seq, cols),
            "up": (width // seq, hidden // head),
            "out": (width // seq, cols),
            "query": (width // seq, cols),
            "key": (width // seq, cols),
            "value": (width // seq, cols),
        }
        seqs, heads = list(range(self.seq_bits)), list(range(self.seq_bits, self.bits))
        ways = {"core": seqs[:1], "straight": seqs[1:], "back": seqs[:0:-1], "bits": heads, "head": ["head"]}
        ways["quad"] = ["quad"] if len(seqs) == 3 else seqs[1:]
        stages = {name: [b for way in ("core",) + STAGES[name] for b in ways[way]] for name in STAGES}
        rows_down, rows_up, rows_out = hidden // seq, width // seq, width // seq
        self.fine = rows_down % (2 * LANES) == 0
        half_down = rows_down // 2
        if self.fine:
            self.chunks = [
                [(s * rows_down + i * half_down, half_down) for s in range(seq)] for i in range(2)
            ]
        else:
            self.chunks = [[(0, hidden)], []]

        def tall(name, *cuts):
            return [(name, r, r + n, c, c + LANES) for r, n in cuts for c in range(0, self.blocks[name][1], LANES)]

        if self.fine:
            third = half_down // 8 * EIGHTHS
            step = 2 * half_down
            first = [(c, c + half_down) for c in range(0, hidden // head, step)]
            second = [(c + half_down, c + step) for c in range(0, hidden // head, step)]
            lanes = lambda cs: [("up", 0, rows_up, c, c + LANES) for a, b in cs for c in range(a, b, LANES)]
            self.sums = {
                "dna": (tall("down", (0, half_down - third)), stages["dna"]),
                "dnb": (tall("down", (half_down, half_down)), stages["dnb"]),
                "dnc": (tall("down", (half_down - third, third)), stages["dnc"]),
                "upa": (lanes(first), stages["upa"]),
                "upb": (lanes(second), stages["upb"]),
            }
        else:
            self.sums = {
                "dna": (tall("down", (0, rows_down)), stages["dna"]),
                "upb": (tall("up", (0, rows_up)), stages["upb"]),
            }
        self.sums["outa"] = (tall("out", (0, rows_out)), stages["outa"])
        if rows_out % 32 == 0:
            m = rows_out // 2
            self.sums["pa"] = (tall("query", (0, rows_out)) + tall("key", (0, m)), stages["pa"])
            self.sums["pb"] = (tall("key", (m, m)) + tall("value", (0, rows_out)), stages["pb"])
        else:
            self.sums["pa"] = (tall("query", (0, rows_out)) + tall("key", (0, rows_out)), stages["pa"])
            self.sums["pb"] = (tall("value", (0, rows_out)), stages["pb"])

    def sum_shape(self, name):
        return (sum(part[2] - part[1] for part in self.sums[name][0]), LANES)

    def bits_of(self, stage):
        if stage == "head":
            return list(range(self.seq_bits, self.bits))
        return list(range(1, self.seq_bits)) if stage == "quad" else [stage]

    def got_shapes(self, name):
        left, shapes = self.bits, []
        for stage in self.sums[name][1]:
            settled = len(self.bits_of(stage))
            left -= settled
            many = (2**settled - 1,) if isinstance(stage, str) else ()
            shapes.append(many + (2,) * left + self.sum_shape(name))
        return shapes


class Summed:
    def __init__(self, plan, me, name, number, grad, got, send, recv, outs):
        self.plan, self.name, self.number = plan, name, number
        self.s, self.h = me
        self.grad, self.got, self.outs = grad, got, outs
        self.send, self.recv = send, recv
        self.parts, self.order = plan.sums[name]
        self.started, self.stage = [], 0

    def own_bit(self, b):
        n = self.plan.seq_bits
        return bit_of(self.s, b) if b < n else bit_of(self.h, b - n)

    def index(self, fixed, others={}):
        at = []
        for b in reversed(range(self.plan.bits)):
            if b in others:
                at.append(others[b])
            elif b in fixed:
                at.append(self.own_bit(b))
            else:
                at.append(slice(None))
        return tuple(at)

    def put(self, name, s, h, block, row, col):
        owner = s + h * self.plan.seq
        at = tuple((owner >> b) & 1 for b in reversed(range(self.plan.bits)))
        first = 0
        for part, r0, r1, c0, c1 in self.parts:
            if part == name and row <= r0 < row + block.shape[0] and col <= c0 < col + block.shape[1]:
                piece = block[r0 - row : r1 - row, c0 - col : c1 - col]
                self.grad[at + (slice(first, first + r1 - r0),)] = piece.astype(BF)
            first += r1 - r0

    def copy(self, source, target, slot, device):
        copy = pltpu.make_async_remote_copy(
            src_ref=source,
            dst_ref=target,
            send_sem=self.send.at[self.number, slot],
            recv_sem=self.recv.at[self.number, slot],
            device_id=device,
            device_id_type=MESH,
        )
        copy.start()
        self.started.append(copy)
        return copy

    def settled(self, stage):
        return [b for way in self.order[:stage] for b in self.plan.bits_of(way)]

    def start(self, stage):
        way = self.order[stage]
        n, first = self.plan.seq_bits, len(self.started)
        self.arriving = []
        if isinstance(way, str):
            bits = self.plan.bits_of(way)
            base = 1 << bits[0] if way == "quad" else 1
            for k in range(1, 2 ** len(bits)):
                device = (flip(self.s, k * base), self.h) if way == "quad" else (self.s, flip(self.h, k))
                others = {b: bit_of(device[0], b) if b < n else bit_of(device[1], b - n) for b in bits}
                source = self.grad.at[self.index(self.settled(stage), others)]
                self.arriving.append(self.copy(source, self.got[stage].at[k - 1], first + k - 1, device))
            return
        b = way
        device = (flip(self.s, 1 << b), self.h) if b < n else (self.s, flip(self.h, 1 << (b - n)))
        source = self.grad.at[self.index(self.settled(stage), {b: 1 - self.own_bit(b)})]
        self.arriving.append(self.copy(source, self.got[stage], first, device))

    def finish(self, stage):
        arriving = self.arriving
        for copy in arriving:
            copy.wait_recv()
        got = self.got[stage]
        pieces = [got.at[k] for k in range(len(arriving))] if len(arriving) > 1 else [got]
        at = self.index(self.settled(stage + 1))
        if stage + 1 == len(self.order):
            total = self.grad[at].astype(F32)
            for piece in pieces:
                total = total + piece[...].astype(F32)
            first = 0
            for part, r0, r1, c0, c1 in self.parts:
                self.outs[part][r0:r1, c0:c1] = total[first : first + r1 - r0]
                first += r1 - r0
            return
        combos = [()]
        for a in at:
            if isinstance(a, slice):
                combos = [c + (i,) for c in combos for i in range(2)]
        for combo in combos:
            left = list(combo)
            full = tuple(left.pop(0) if isinstance(a, slice) else a for a in at)
            if len(pieces) == 1:
                self.grad[full] = self.grad[full] + pieces[0][combo]
                continue
            total = self.grad[full].astype(F32)
            for piece in pieces:
                total = total + piece[combo].astype(F32)
            self.grad[full] = total.astype(BF)

    def step(self):
        if self.stage:
            self.finish(self.stage - 1)
        if self.stage < len(self.order):
            self.start(self.stage)
        self.stage += 1

    @property
    def done(self):
        return self.stage > len(self.order)

    def drain(self):
        for copy in self.started:
            copy.wait_send()


def layer_kernel(plan, *refs):
    refs = list(refs)

    def take(n):
        taken = refs[:n]
        del refs[:n]
        return taken

    x_in, dy_in, *lines_in = take(8)
    weights_in = take(6)
    lo_out, ig_out = take(2)
    grads_out = dict(zip(plan.blocks, take(6)))
    lines_out = take(6)
    xg, dyg, log, igg = take(4)
    wq, wk, wv, wo, wu, wd = weights = take(6)
    gain_one, shift_one, gain_two, shift_two, up_bias, down_bias = lines = take(6)
    norm_t, norm_b, n_one, rs_one, n_two, rs_two, norm_two_b, residual, d_residual = take(9)
    qs, kn, vn, kf, vf, near_values = take(6)
    pn, pf, stats, mask, mixed_t = take(5)
    act_ref, hid_ref, cdf_ref, dh_ref = take(4)
    dos, dq_t, dk_ref, dv_ref, far_ref, bar_t, d_norm_one = take(7)
    c_send, c_got, c_half, c_half_got, bar_send, bar_got, d_send, d_got, d_half, d_half_got, far_parts = take(11)
    sums = {}
    for name in plan.sums:
        grad, *got = take(1 + len(plan.sums[name][1]))
        sums[name] = (grad, got)
    vec_bufs, vec_got, vec_own, vec_own_got = take(4)
    send_a, recv_a, send_r, recv_r, send_s, recv_s, here = take(7)
    assert not refs

    seq, head, rows, width, tokens = plan.seq, plan.head, plan.rows, plan.width, plan.tokens
    half, near, far = plan.half, plan.near, plan.far
    s, h = lax.axis_index("seq"), lax.axis_index("head")
    c, g = irem(s, plan.minor), idiv(s, plan.minor)
    j = c * head + h

    def group_peer(k):
        other = flip(j, k)
        return other, (g * plan.minor + idiv(other, head), irem(other, head))

    def row_peer(k):
        other = flip(g, k)
        return other, (other * plan.minor + c, h)

    barrier = pltpu.get_barrier_semaphore()
    peers = [group_peer(k)[1] for k in range(1, rows)] + [row_peer(k)[1] for k in range(1, plan.groups)]
    for device in peers:
        pl.semaphore_signal(barrier, inc=1, device_id=device, device_id_type=MESH)

    small = [pltpu.make_async_copy(a, b, here.at[10 + i]) for i, (a, b) in enumerate(zip(lines_in, lines))]
    for copy in small:
        copy.start()
    loads = [pltpu.make_async_copy(a, b, here.at[i]) for i, (a, b) in enumerate(zip(weights_in, weights))]
    for i in (1, 2, 0, 3, 4, 5):
        loads[i].start()
    own = [
        pltpu.make_async_copy(x_in.at[j], xg.at[j], here.at[6]),
        pltpu.make_async_copy(dy_in.at[j], dyg.at[j], here.at[7]),
    ]
    for copy in own:
        copy.start()

    i_k = lax.broadcasted_iota(jnp.int32, (near, 2 * half), 0)
    i_q = lax.broadcasted_iota(jnp.int32, (near, 2 * half), 1) & (half - 1)
    valid = (i_k < half) & ((i_q >> 5) == (i_k >> 5))
    first = half
    for level in range(1, plan.local - 1):
        count = half >> level
        mine = (i_k >= first) & (i_k < first + count)
        valid = valid | (mine & (((i_q >> (4 + level)) ^ 1) == ((i_k - first) >> 4)))
        first += count
    valid = valid | (i_k >= first)
    mask[...] = jnp.where(valid, 0.0, -1e30).astype(F32)

    pl.semaphore_wait(barrier, len(peers))

    def exchange(number, source, target):
        copies = []
        for k in sorted(range(1, rows), key=lambda k: -(k % head)):
            other, device = group_peer(k)
            copy = pltpu.make_async_remote_copy(
                src_ref=source.at[other],
                dst_ref=target.at[j],
                send_sem=send_a.at[number, k],
                recv_sem=recv_a.at[number, k],
                device_id=device,
                device_id_type=MESH,
            )
            copy.start()
            copies.append(copy)
        return copies

    x_copies = exchange(0, x_in, xg)

    def norm_stats(values):
        center = values - jnp.mean(values, axis=-1, keepdims=True)
        spread = jnp.mean(center * center, axis=-1, keepdims=True)
        scale = lax.rsqrt(spread + EPSILON)
        return center * scale, scale

    def norm_back(d_norm, n, scale, gain):
        weighted = d_norm * gain
        return scale * (
            weighted
            - jnp.mean(weighted, axis=-1, keepdims=True)
            - n * jnp.mean(weighted * n, axis=-1, keepdims=True)
        )

    lane = lax.broadcasted_iota(jnp.int32, (1, PAIR), 1)
    low = lane < DH

    def stack_heads(ref, value):
        for p in range(plan.pairs):
            for a in range(2):
                part = value[a * half : (a + 1) * half, p * PAIR : (p + 1) * PAIR]
                zero = jnp.zeros_like(part)
                ref[p, a, :half, :] = jnp.where(low, part, zero)
                ref[p, a, half:, :] = jnp.where(low, zero, part)

    for copy in small:
        copy.wait()
    own[0].wait()
    near_first = x_copies[::-1]
    for copy in near_first[:-2]:
        copy.wait_recv()
    dy_copies = exchange(1, dy_in, dyg)
    for copy in near_first[-2:]:
        copy.wait_recv()
    x = xg[...].reshape(tokens, width).astype(F32)
    n, scale = norm_stats(x)
    n_one[...] = n
    rs_one[...] = scale
    normed = (n * gain_one[...] + shift_one[...]).astype(BF)

    loads[1].wait()
    loads[2].wait()
    level = jnp.concatenate([dot(normed, wk[...]).astype(BF), dot(normed, wv[...]).astype(BF)], axis=1)

    def columns(index, p):
        return slice(index * width + p * PAIR, index * width + (p + 1) * PAIR)

    targets = (kn, vn)
    first = 0
    for l in range(plan.local):
        if l:
            level = dot(pair_mean(level.shape[0]), level).astype(BF)
        count = level.shape[0] // 2
        for index, ref in enumerate(targets):
            for p in range(plan.pairs):
                for a in range(2):
                    b = a if l + 1 < plan.local else 1 - a
                    ref[p, b, first : first + count, :] = level[a * count : (a + 1) * count, columns(index, p)]
        first += count
    level = dot(pair_mean(level.shape[0]), level).astype(BF)
    c_send[0] = level[:, :width]
    c_send[1] = level[:, width:]
    level = dot(pair_mean(level.shape[0]), level).astype(BF)
    c_half[: BLOCK // 2, :] = level[:, :width]
    c_half[BLOCK // 2 :, :] = level[:, width:]
    c_copies = []
    for k in reversed(range(1, plan.groups)):
        other, device = row_peer(k)
        copy = pltpu.make_async_remote_copy(
            src_ref=c_send if k == 1 else c_half,
            dst_ref=c_got if k == 1 else c_half_got.at[g],
            send_sem=send_r.at[0, k],
            recv_sem=recv_r.at[0, k],
            device_id=device,
            device_id_type=MESH,
        )
        copy.start()
        c_copies.append(copy)

    loads[0].wait()
    stack_heads(qs, (dot(normed, wq[...]) * (DH**-0.5)).astype(BF))
    norm_b[...] = normed

    def attend_near(p):
        scores = jnp.concatenate([dot_t(kn[p, a], qs[p, a]) + mask[...] for a in range(2)], axis=1)
        top = jnp.max(scores, axis=0, keepdims=True)
        raised = jnp.exp(scores - top)
        at = slice(2 * p * tokens, (2 * p + 2) * tokens)
        stats[0:1, at] = top
        stats[1:2, at] = jnp.sum(raised, axis=0, keepdims=True)
        for a in range(2):
            part = raised[:, a * tokens : (a + 1) * tokens]
            pn[p, a] = part
            near_values[p, a] = t_dot(vn[p, a], part.astype(BF))

    for p in range(plan.pairs):
        attend_near(p)

    for copy in c_copies:
        copy.wait_recv()

    def sibling(b):
        upper = idiv(g, 1 << b)
        return (upper + 1 - 2 * irem(upper, 2)) * (1 << b)

    for b in range(plan.remote):
        for index in range(2):
            if b == 0:
                level = c_got[index]
            else:
                count = 1 << b
                both_kinds = c_half_got[pl.ds(sibling(b), count)].reshape(BLOCK * count, width)
                i_r = lax.broadcasted_iota(jnp.int32, (BLOCK * count // 2, BLOCK * count), 0)
                i_s = lax.broadcasted_iota(jnp.int32, (BLOCK * count // 2, BLOCK * count), 1)
                own_rows = (i_r >> 3) * BLOCK + index * (BLOCK // 2) + (i_r & 7) == i_s
                level = dot(jnp.where(own_rows, 1.0, 0.0).astype(BF), both_kinds).astype(BF)
                for _ in range(b - 1):
                    level = dot(pair_mean(level.shape[0]), level).astype(BF)
            for p in range(plan.pairs):
                part = level[:, p * PAIR : (p + 1) * PAIR]
                (kf, vf)[index][p, b * BLOCK : (b + 1) * BLOCK, :] = part

    halves = [(p, a) for p in range(plan.pairs) for a in range(2)]
    scores = jnp.concatenate([dot_t(kf[p], qs[p, a]) for p, a in halves], axis=1)
    top_near = stats[0:1, :]
    top = jnp.maximum(top_near, jnp.max(scores, axis=0, keepdims=True))
    shrink = jnp.exp(top_near - top)
    raised = jnp.exp(scores - top)
    share = 1.0 / (stats[1:2, :] * shrink + jnp.sum(raised, axis=0, keepdims=True))
    near_share = shrink * share
    stats[2:3, :] = near_share
    prob = raised * share
    pf[...] = prob
    prob = prob.astype(BF)
    for i, (p, a) in enumerate(halves):
        at = slice(i * tokens, (i + 1) * tokens)
        mixed = near_values[p, a] * near_share[:, at] + t_dot(vf[p], prob[:, at])
        mixed_t[p, :DH, a * half : (a + 1) * half] = mixed[:DH, :half].astype(BF)
        mixed_t[p, DH:, a * half : (a + 1) * half] = mixed[DH:, half:].astype(BF)

    loads[3].wait()
    res = xg[...].reshape(tokens, width).astype(F32) + t_dot(mixed_t[...].reshape(width, tokens), wo[...])
    residual[...] = res
    n, scale = norm_stats(res)
    n_two[...] = n
    rs_two[...] = scale
    norm_two_b[...] = (n * gain_two[...] + shift_two[...]).astype(BF)

    row = lambda a: jnp.sum(a, axis=0, keepdims=True)
    per = plan.hidden // width

    def put_block(name, block, first_row, first_col):
        r, w = plan.blocks[name]
        row_step, col_step = min(r, block.shape[0]), min(w, block.shape[1])
        for a in range(0, block.shape[0], row_step):
            for b in range(0, block.shape[1], col_step):
                s_at, h_at = (first_row + a) // r, (first_col + b) // w
                piece = block[a : a + row_step, b : b + col_step]
                for item in items.values():
                    if item is not vec_sum:
                        item.put(name, s_at, h_at, piece, (first_row + a) % r, (first_col + b) % w)

    class Vectors:
        def __init__(self):
            self.stage, self.started = 0, []

        def copy(self, source, target, slot, device):
            copy = pltpu.make_async_remote_copy(
                src_ref=source,
                dst_ref=target,
                send_sem=send_s.at[len(plan.sums), slot],
                recv_sem=recv_s.at[len(plan.sums), slot],
                device_id=device,
                device_id_type=MESH,
            )
            copy.start()
            self.started.append(copy)

        def step(self):
            n, k = plan.seq_bits, self.stage
            if 0 < k <= n:
                self.started[k - 1].wait_recv()
                vec_bufs[k] = vec_bufs[k - 1] + vec_got[k - 1]
            if k < n:
                self.copy(vec_bufs.at[k], vec_got.at[k], k, (flip(s, 1 << k), h))
            elif k == n:
                vec = vec_bufs[n]
                part = own_part(vec[:8])
                vec_own[:, : part.shape[1]] = part
                part = own_part(jnp.concatenate([vec[5 + i : 6 + i] for i in range(per)], axis=1))
                vec_own[5:6, : part.shape[1]] = part
                for i in range(1, head):
                    self.copy(vec_own, vec_own_got.at[i - 1], n + i - 1, (s, flip(h, i)))
            else:
                values = [vec_own[...]]
                for i in range(1, head):
                    self.started[n + i - 1].wait_recv()
                    values.append(vec_own_got[i - 1])
                while len(values) > 1:
                    values = [values[i] + values[i + 1] for i in range(0, len(values), 2)]
                for i, line in enumerate(lines_out):
                    line[...] = values[0][i, : line.shape[0]]
            self.stage += 1

        @property
        def done(self):
            return self.stage > plan.seq_bits + 1

        def drain(self):
            for copy in self.started:
                copy.wait_send()

    def own_part(line):
        share = line.shape[1] // seq
        part = line[:, :share]
        for other in range(1, seq):
            part = jnp.where(s == other, line[:, other * share : (other + 1) * share], part)
        return part

    vec_sum = Vectors()
    items = {
        name: Summed(plan, (s, h), name, i, grad, got, send_s, recv_s, grads_out)
        for i, (name, (grad, got)) in enumerate(sums.items())
    }
    items["vec"] = vec_sum

    def cotangent():
        return dyg[...].reshape(tokens, width)

    def blocks_of(chunk):
        at, blocks = 0, []
        for start, length in plan.chunks[chunk]:
            for f in range(start, start + length, 512):
                n = min(512, start + length - f)
                if not blocks or blocks[-1][1] + n > 512:
                    blocks.append([[], 0, at])
                blocks[-1][0].append((f, n))
                blocks[-1][1] += n
                at += n
        return [(segments, slice(first, first + n)) for segments, n, first in blocks]

    def columns_of(ref, segments):
        return jnp.concatenate([ref[:, f : f + n] for f, n in segments], axis=1)

    def rows_of(ref, segments):
        return jnp.concatenate([ref[f : f + n, :] for f, n in segments], axis=0)

    flat = [(chunk, *block) for chunk in range(2) for block in blocks_of(chunk)]
    quarters = [flat[i : i + 1] for i in range(4)] if plan.fine else [flat, [], [], []]

    def activate(quarter):
        if quarter == 0:
            loads[4].wait()
        for chunk, segments, at in quarters[quarter]:
            hid = dot(norm_two_b[...], columns_of(wu, segments)) + columns_of(up_bias, segments)
            cdf = 0.5 * (1.0 + lax.erf(hid * (0.5**0.5)))
            act = (hid * cdf).astype(BF)
            act_ref[chunk, :, at] = act
            hid_ref[chunk, :, at] = hid
            cdf_ref[chunk, :, at] = cdf

    def down_grad(quarter):
        if quarter == 0:
            loads[5].wait()
            own[1].wait()
            for copy in dy_copies:
                copy.wait_recv()
        for chunk, segments, at in quarters[quarter]:
            grad = t_dot(act_ref[chunk, :, at], cotangent())
            first = 0
            for f, n in segments:
                put_block("down", grad[first : first + n], f, 0)
                first += n

    def deactivate(quarter):
        for chunk, segments, at in quarters[quarter]:
            hid = hid_ref[chunk, :, at]
            slope = cdf_ref[chunk, :, at] + hid * (jnp.exp(-0.5 * hid * hid) * 0.3989422804014327)
            dh = (dot_t(cotangent(), rows_of(wd, segments)) * slope).astype(BF)
            dh_ref[chunk, :, at] = dh
            sums_dh = row(dh.astype(F32))
            grad = t_dot(norm_two_b[...], dh)
            first = 0
            for f, n in segments:
                for o in range(0, n, min(n, width)):
                    line, lane_at = divmod(f + o, width)
                    m = min(n, width)
                    vec_bufs[0, 5 + line : 6 + line, lane_at : lane_at + m] = sums_dh[:, first + o : first + o + m]
                put_block("up", grad[:, first : first + n], 0, f)
                first += n

    def both(ref, weight, product, pick):
        total = None
        for chunk in range(2):
            for segments, at in blocks_of(chunk):
                term = product(ref[chunk, :, at], pick(weight, segments))
                total = term if total is None else total + term
        return total

    def second_norm_back():
        d_norm_two = both(dh_ref, wu, dot_t, columns_of)
        n = n_two[...]
        dy_f = cotangent().astype(F32)
        vec_bufs[0, 2:3, :] = row(d_norm_two * n)
        vec_bufs[0, 3:4, :] = row(d_norm_two)
        vec_bufs[0, 4:5, :] = row(dy_f)
        d_residual[...] = dy_f + norm_back(d_norm_two, n, rs_two[...], gain_two[...])

    def out_grad():
        put_block("out", dot(mixed_t[...].reshape(width, tokens), d_residual[...].astype(BF)), 0, 0)

    def mixed_back():
        stack_heads(dos, dot_t(d_residual[...].astype(BF), wo[...]).astype(BF))

    def layer_output():
        result = residual[...] + both(act_ref, wd, dot, rows_of) + down_bias[...]
        log[...] = result.astype(BF).reshape(rows, plan.pos, width)

    late_copies, own_late = [], []

    def send_layer_output():
        late_copies.extend(exchange(2, log, lo_out))
        own_late.append(pltpu.make_async_copy(log.at[j], lo_out.at[j], here.at[8]))
        own_late[-1].start()

    def spread_matrix():
        i_t = lax.broadcasted_iota(jnp.int32, (half, near - half), 0)
        i_c = lax.broadcasted_iota(jnp.int32, (half, near - half), 1)
        spread = jnp.zeros((half, near - half), F32)
        first = 0
        for level in range(1, plan.local):
            spread = spread + jnp.where((i_t >> level) == (i_c - first), 0.5**level, 0.0)
            first += half >> level
        return spread.astype(BF)

    def attend_back(p):
        spread = spread_matrix()
        dk, dv, dk_far, dv_far = [], [], 0.0, 0.0
        k_far, v_far = kf[p], vf[p]
        for a in range(2):
            at = slice((2 * p + a) * tokens, (2 * p + a + 1) * tokens)
            q, do = qs[p, a], dos[p, a]
            prob, prob_far = pn[p, a] * stats[2:3, at], pf[:, at]
            d_prob = dot_t(vn[p, a], do)
            d_prob_far = dot_t(v_far, do)
            inner = row(prob * d_prob) + row(prob_far * d_prob_far)
            d_scores = (prob * (d_prob - inner)).astype(BF)
            d_scores_far = (prob_far * (d_prob_far - inner)).astype(BF)
            dk.append(dot(d_scores, q))
            dv.append(dot(prob.astype(BF), do))
            dk_far = dk_far + dot(d_scores_far, q)
            dv_far = dv_far + dot(prob_far.astype(BF), do)
            dq = (t_dot(kn[p, a], d_scores) + t_dot(k_far, d_scores_far)) * (DH**-0.5)
            dq_t[p, :DH, a * half : (a + 1) * half] = dq[:DH, :half].astype(BF)
            dq_t[p, DH:, a * half : (a + 1) * half] = dq[DH:, half:].astype(BF)
        other = near - BLOCK
        for index, (total, total_far, ref) in enumerate(((dk, dk_far, dk_ref), (dv, dv_far, dv_ref))):
            for a in range(2):
                coarse = jnp.concatenate([total[a][half:other], total[1 - a][other:]], axis=0)
                ref[p, a * half : (a + 1) * half, :] = total[a][:half] + two_part_dot(spread, coarse)
            far_ref[index, p] = total_far

    d_copies = []

    def send_far():
        i_a = lax.broadcasted_iota(jnp.int32, (BLOCK, BLOCK), 0)
        i_b = lax.broadcasted_iota(jnp.int32, (BLOCK, BLOCK), 1)
        for k in range(1, plan.groups):
            other, device = row_peer(k)
            b = k.bit_length() - 1
            offset = irem(other, 1 << b)
            for index in range(2):
                for p in range(plan.pairs):
                    level = far_ref[index, p, BLOCK * b : BLOCK * (b + 1), :].astype(BF)
                    if b == 0:
                        d_send[index, p] = level
                        continue
                    rows_at = (offset * (BLOCK // 2) + (i_a & 7)) >> (b - 1)
                    pick = jnp.where((rows_at == i_b) & ((i_a >> 3) == index), 0.5**b, 0.0).astype(BF)
                    part = dot(pick, level)
                    if index == 0:
                        far_parts[p] = part
                    else:
                        d_half[k, p] = (far_parts[p] + part).astype(BF)
            copy = pltpu.make_async_remote_copy(
                src_ref=d_send if k == 1 else d_half.at[k],
                dst_ref=d_got if k == 1 else d_half_got.at[k],
                send_sem=send_r.at[1, k],
                recv_sem=recv_r.at[1, k],
                device_id=device,
                device_id_type=MESH,
            )
            copy.start()
            d_copies.append(copy)

    def part_grads():
        put_block("query", dot_t(norm_t[...], dq_t[...].reshape(width, tokens)), 0, 0)
        for index, (ref, name) in enumerate(((dk_ref, "key"), (dv_ref, "value"))):
            mine = jnp.concatenate([ref[p].astype(BF) for p in range(plan.pairs)], axis=1)
            made = jnp.concatenate([far_ref[index, p].astype(BF) for p in range(plan.pairs)], axis=1)
            put_block(name, dot(norm_t[...], mine) + dot(bar_t[...], made), 0, 0)

    bar_copies = []

    def send_bars():
        i_a = lax.broadcasted_iota(jnp.int32, (BLOCK, tokens), 0)
        i_b = lax.broadcasted_iota(jnp.int32, (BLOCK, tokens), 1)
        mean_all = jnp.where((i_b >> plan.local) == i_a, 0.5**plan.local, 0.0).astype(BF)
        bar_send[...] = dot(mean_all, norm_b[...]).astype(BF)
        for k in range(1, plan.groups):
            other, device = row_peer(k)
            copy = pltpu.make_async_remote_copy(
                src_ref=bar_send,
                dst_ref=bar_got.at[g],
                send_sem=send_r.at[2, k],
                recv_sem=recv_r.at[2, k],
                device_id=device,
                device_id_type=MESH,
            )
            copy.start()
            bar_copies.append(copy)

    def take_bars():
        norm_t[...] = turned(norm_b[...])
        for copy in bar_copies:
            copy.wait_recv()
        for b in range(plan.remote):
            level = bar_got[pl.ds(sibling(b), 1 << b)].reshape(BLOCK << b, width)
            for _ in range(b):
                level = dot(pair_mean(level.shape[0]), level).astype(BF)
            bar_t[:, b * BLOCK : (b + 1) * BLOCK] = turned(level)

    def query_back():
        d_norm_one[...] = dot_t(turned(dq_t[...].reshape(width, tokens)), wq[...])

    def take_far():
        for copy in d_copies:
            copy.wait_recv()

    def first_norm_back():
        i_t = lax.broadcasted_iota(jnp.int32, (tokens, BLOCK), 0)
        i_c = lax.broadcasted_iota(jnp.int32, (tokens, BLOCK), 1)
        last = jnp.where((i_t >> plan.local) == i_c, 0.5**plan.local, 0.0).astype(BF)
        half_of = [
            jnp.where((i_t >> (plan.local + 1)) == i_c - (BLOCK // 2) * i, 0.5**plan.local, 0.0).astype(BF)
            for i in range(2)
        ]
        d_normed = d_norm_one[...]
        for index, (ref, w) in enumerate(((dk_ref, wk), (dv_ref, wv))):
            pieces = []
            for p in range(plan.pairs):
                total = ref[p] + dot(last, d_got[index, p])
                if plan.groups > 2:
                    coarse = d_half_got[2, p].astype(F32)
                    for k in range(3, plan.groups):
                        coarse = coarse + d_half_got[k, p].astype(F32)
                    total = total + two_part_dot(half_of[index], coarse)
                pieces.append(total.astype(BF))
            d_normed = d_normed + dot_t(jnp.concatenate(pieces, axis=1), w[...])
        n = n_one[...]
        vec_bufs[0, 0:1, :] = row(d_normed * n)
        vec_bufs[0, 1:2, :] = row(d_normed)
        d_first = norm_back(d_normed, n, rs_one[...], gain_one[...])
        igg[...] = (d_residual[...] + d_first).astype(BF).reshape(rows, plan.pos, width)

    def send_input_grad():
        late_copies.extend(exchange(3, igg, ig_out))
        own_late.append(pltpu.make_async_copy(igg.at[j], ig_out.at[j], here.at[9]))
        own_late[-1].start()

    vec_own[...] = jnp.zeros_like(vec_own)
    work = {
        **{f"f1{i}": functools.partial(activate, i) for i in range(4)},
        **{f"g1{i}": functools.partial(down_grad, i) for i in range(4)},
        **{f"f2{i}": functools.partial(deactivate, i) for i in range(4)},
        "ln2b": second_norm_back,
        "outg": out_grad,
        "lo": layer_output,
        "Alo": send_layer_output,
        "dmix": mixed_back,
        "Abar": send_bars,
        "bar": take_bars,
        "dsend": send_far,
        "qkvg": part_grads,
        "dnq": query_back,
        "Wd": take_far,
        "ln1b": first_norm_back,
        "Aig": send_input_grad,
    }
    first_pairs = {f"ab{i}": range(i, plan.pairs, 4) for i in range(4)}
    for name in ORDER:
        if name in work:
            work[name]()
        elif name in first_pairs:
            for p in first_pairs[name]:
                attend_back(p)
        elif name in items:
            items[name].step()
    while not all(item.done for item in items.values()):
        for item in items.values():
            if not item.done:
                item.step()

    for copy in late_copies:
        copy.wait_recv()
    for copy in own_late:
        copy.wait()
    for copy in x_copies + dy_copies + c_copies + bar_copies + d_copies + late_copies:
        copy.wait_send()
    for item in items.values():
        item.drain()


def place_kernel(*refs):
    count = len(refs) // 2
    ins, outs, sems = refs[:count], refs[count:-1], refs[-1]
    copies = [pltpu.make_async_copy(a, b, sems.at[i]) for i, (a, b) in enumerate(zip(ins, outs))]
    for copy in copies:
        copy.start()
    for copy in copies:
        copy.wait()


def body(
    inputs,
    gain_first,
    shift_first,
    query_weight,
    key_weight,
    value_weight,
    out_weight,
    gain_second,
    shift_second,
    up_weight,
    up_bias,
    down_weight,
    down_bias,
    cotangent,
):
    rows, pos, width = inputs.shape
    hidden = up_weight.shape[1]
    plan = Plan(lax.axis_size("seq"), lax.axis_size("head"), rows, pos, width, hidden)
    tokens, pairs, groups, half, near, far = plan.tokens, plan.pairs, plan.groups, plan.half, plan.near, plan.far
    vmem = pl.BlockSpec(memory_space=pltpu.VMEM)
    anywhere = pl.BlockSpec(memory_space=pl.ANY)
    names = list(plan.blocks)

    def buf(*shape, dtype=BF):
        return pltpu.VMEM(shape, dtype)

    scratch = [buf(rows, pos, width)] * 4
    scratch += [buf(width, width)] * 4 + [buf(width, hidden), buf(hidden, width)]
    scratch += [buf(1, n, dtype=F32) for n in (width, width, width, width, hidden, width)]
    scratch += [
        buf(width, tokens),
        buf(tokens, width),
        buf(tokens, width, dtype=F32),
        buf(tokens, 1, dtype=F32),
        buf(tokens, width, dtype=F32),
        buf(tokens, 1, dtype=F32),
        buf(tokens, width),
        buf(tokens, width, dtype=F32),
        buf(tokens, width, dtype=F32),
    ]
    scratch += [
        buf(pairs, 2, tokens, PAIR),
        buf(pairs, 2, near, PAIR),
        buf(pairs, 2, near, PAIR),
        buf(pairs, far, PAIR),
        buf(pairs, far, PAIR),
        buf(pairs, 2, PAIR, tokens, dtype=F32),
    ]
    scratch += [
        buf(pairs, 2, near, tokens, dtype=F32),
        buf(far, 2 * pairs * tokens, dtype=F32),
        buf(8, 2 * pairs * tokens, dtype=F32),
        buf(near, tokens, dtype=F32),
        buf(pairs, PAIR, tokens),
    ]
    part = sum(n for _, n in plan.chunks[0])
    scratch += [buf(2, tokens, part)] + [buf(2, tokens, part, dtype=F32)] * 2 + [buf(2, tokens, part)]
    scratch += [
        buf(pairs, 2, tokens, PAIR),
        buf(pairs, PAIR, tokens),
        buf(pairs, tokens, PAIR, dtype=F32),
        buf(pairs, tokens, PAIR, dtype=F32),
        buf(2, pairs, BLOCK * plan.remote, PAIR, dtype=F32),
        buf(width, BLOCK * plan.remote),
        buf(tokens, width, dtype=F32),
    ]
    scratch += [
        buf(2, BLOCK, width),
        buf(2, BLOCK, width),
        buf(BLOCK, width),
        buf(groups, BLOCK, width),
        buf(BLOCK, width),
        buf(groups, BLOCK, width),
        buf(2, pairs, BLOCK, PAIR),
        buf(2, pairs, BLOCK, PAIR),
        buf(groups, pairs, BLOCK, PAIR),
        buf(groups, pairs, BLOCK, PAIR),
        buf(pairs, BLOCK, PAIR, dtype=F32),
    ]
    for name in plan.sums:
        scratch += [buf(*(2,) * plan.bits, *plan.sum_shape(name))]
        scratch += [buf(*shape) for shape in plan.got_shapes(name)]
    slots = plan.bits + plan.head
    share = max(width, hidden) // plan.seq
    scratch += [
        buf(plan.seq_bits + 1, plan.lines, width, dtype=F32),
        buf(plan.seq_bits, plan.lines, width, dtype=F32),
        buf(8, share, dtype=F32),
        buf(plan.head - 1, 8, share, dtype=F32),
    ]
    dma = pltpu.SemaphoreType.DMA
    scratch += [dma((4, rows)), dma((4, rows)), dma((3, groups)), dma((3, groups))]
    scratch += [dma((len(plan.sums) + 1, slots)), dma((len(plan.sums) + 1, slots)), dma((16,))]

    line = lambda a: a.reshape(1, -1)
    big = [jax.ShapeDtypeStruct(inputs.shape, BF)] * 2 + [jax.ShapeDtypeStruct(plan.blocks[n], F32) for n in names]
    lines = [jax.ShapeDtypeStruct((width // plan.seq,), F32)] * 5 + [jax.ShapeDtypeStruct((hidden // plan.seq,), F32)]
    results = pl.pallas_call(
        functools.partial(layer_kernel, plan),
        out_shape=[pltpu.VMEM(o.shape, o.dtype) for o in big + lines],
        in_specs=[anywhere] * 14,
        out_specs=[vmem] * 14,
        scratch_shapes=scratch,
        compiler_params=pltpu.CompilerParams(
            collective_id=0, has_side_effects=True, vmem_limit_bytes=56 << 20
        ),
        name="layer",
    )(
        inputs,
        cotangent,
        line(gain_first),
        line(shift_first),
        line(gain_second),
        line(shift_second),
        line(up_bias),
        line(down_bias),
        query_weight,
        key_weight,
        value_weight,
        out_weight,
        up_weight,
        down_weight,
    )
    placed = pl.pallas_call(
        place_kernel,
        out_shape=big + lines,
        in_specs=[vmem] * 14,
        out_specs=[anywhere] * 14,
        scratch_shapes=[dma((14,))],
        name="place",
    )(*[pltpu.with_memory_space_constraint(r, pltpu.VMEM) for r in results])
    layer_out, input_grad, down_g, up_g, out_g, query_g, key_g, value_g = placed[:8]
    gain_one_g, shift_one_g, gain_two_g, shift_two_g, down_bias_g, up_bias_g = placed[8:]
    return (
        layer_out,
        input_grad,
        gain_one_g,
        shift_one_g,
        query_g,
        key_g,
        value_g,
        out_g,
        gain_two_g,
        shift_two_g,
        up_g,
        up_bias_g,
        down_g,
        down_bias_g,
    )


def solution(mesh):
    placed = (P(None, ("seq", "head"), None),) + (P(),) * 12 + (P(None, ("seq", "head"), None),)
    return jax.shard_map(
        body,
        mesh=mesh,
        in_specs=placed,
        out_specs=(
            P(None, ("seq", "head"), None),
            P(None, ("seq", "head"), None),
            P("seq"),
            P("seq"),
            P("seq", "head"),
            P("seq", "head"),
            P("seq", "head"),
            P("seq", "head"),
            P("seq"),
            P("seq"),
            P("seq", "head"),
            P("seq"),
            P("seq", "head"),
            P("seq"),
        ),
        check_vma=False,
    )
```
